32 devices in a mesh: sec: 4 (over x, core), swath: 8 (over z, y).
Axes of the slice: x: 2, y: 2, z: 4, core: 2. Of those that a mesh axis runs over, the one named last changes fastest.
Arguments:
- radar_l: bfloat16 [6, 1536, 1024], P(None, 'sec', 'swath'), may hold values from -6 to 6
- radar_s: bfloat16 [6, 1024, 1024], P(None, 'sec', 'swath'), may hold values from -6 to 6
- weights_l: bfloat16 [12288, 128, 128], P(('sec', 'swath')), may hold values from -0.5 to 0.5
- weights_s: bfloat16 [8192, 128, 128], P(('sec', 'swath')), may hold values from -0.5 to 0.5
- owner_l: int32 [12288, 1], P(('sec', 'swath')), may hold values from 0 to 31; in each aligned block of 384 rows (0 to 383, 384 to 767, ...) at most 24 rows name the same one
- owner_s: int32 [8192, 1], P(('sec', 'swath')), may hold values from 0 to 31; in each aligned block of 256 rows (0 to 255, 256 to 511, ...) at most 16 rows name the same one
- slot_l: int32 [12288], P(('sec', 'swath')), may hold values from 0 to 255
- slot_s: int32 [8192], P(('sec', 'swath')), may hold values from 0 to 255
- models: float32 [16, 36], replicated, may hold values from -1 to 1
Outputs:
- fit: float32 [16, 1024, 1024], P(None, 'sec', 'swath')
The draws below stay inside these ranges and needn't reach their ends.
Inputs may be any that keep to these rules, and one draw needn't show every extreme that they name: `owner_l`: within the tiles of one device, each owner is named by at most 24 tiles. `owner_s`: within the tiles of one device, each owner is named by at most 16 tiles.
All inputs are finite; a program needn't handle non-finite values.
Results may differ from the reference program's by a relative error of at most 0.0038.
Values may be sent and summed in bfloat16 or wider, within the bound.
No kernel may reach another device: no remote copies, remote signals or barrier semaphores. Data moves between devices by JAX's collectives and lax.ppermute only.
A program may use at most 192 MiB of HBM per device.

```python
import math
import jax
import jax.numpy as jnp
import numpy as np
from jax import lax

PIX = 128
TL_DEV = 384
TS_DEV = 256
NMODEL = 16
FIT_ITERS = 4
CAP_L = 24
CAP_S = 16
LINES_L = 1536
LINES_S = 1024
COLS = 1024
TILES_L = 12288
TILES_S = 8192
N_SEC = 4
N_SWATH = 8
DEVICES = 32


def place_ends(entries, key, low, largest):
    place = [jax.random.randint(jax.random.fold_in(key, axis), (), 0, length) for axis, length in enumerate(entries.shape)]
    longest = entries.shape.index(max(entries.shape))
    beside = place[:longest] + [(place[longest] + 1) % entries.shape[longest]] + place[longest + 1:]
    return entries.at[tuple(place)].set(low).at[tuple(beside)].set(largest)


def block_levels(rng, dims, split, least, top_value):
    level = 1.0
    for dim, blocks in split:
        steps = jax.random.uniform(jax.random.fold_in(jax.random.fold_in(rng, 6), dim), (blocks,), jnp.float32, least / len(split), top_value / len(split))
        level = level * jnp.repeat(jnp.exp(steps), dims[dim] // blocks).reshape((-1,) + (1,) * (len(dims) - 1 - dim))
    return level


def deal_out(stream_key, own, number, rows, count, top, most, skew):
    order = jax.random.permutation(stream_key, count)
    packed, usual = shares(count, rows * top, most, skew, True), shares(count, rows * top, most, skew, False)
    places = jnp.arange(count)

    def named(lengths, offset_by):
        used = int((lengths > 0).sum())
        fixed = max(1, used // 4)
        shifted = fixed + (places - fixed + offset_by * (used - fixed)) % max(1, count - fixed)
        return jnp.zeros((count,), jnp.int32).at[order[jnp.where(places < fixed, places, shifted)]].set(jnp.asarray(lengths, jnp.int32))

    lengths = jnp.where(number % 4 == 0, named(packed, number // 4), named(usual, number - number // 4 - 1))
    mixed = jax.random.permutation(jax.random.fold_in(own, 3), count)
    donor, sink = mixed[0:count // 2 * 2:2], mixed[1:count // 2 * 2:2]
    slack = jnp.minimum(lengths[donor] - 1, most - lengths[sink]) // 2
    slack = jnp.where((donor == order[0]) | (sink == order[0]) | (lengths[sink] == 0), 0, jnp.maximum(slack, 0))
    shifted = jax.random.randint(jax.random.fold_in(own, 4), (count // 2,), 0, 1 << 20) % (slack + 1)
    lengths = lengths.at[donor].add(-shifted).at[sink].add(shifted)
    members = jnp.searchsorted(jnp.cumsum(lengths), jnp.arange(rows * top), side="right").astype(jnp.int32)
    table = members.reshape(top, rows).T
    table = table[jax.random.permutation(jax.random.fold_in(own, 1), rows)]
    offset_by = jax.random.randint(jax.random.fold_in(own, 2), (rows, 1), 0, top)
    return jnp.take_along_axis(table, (jnp.arange(top)[None, :] + offset_by) % top, axis=1)


def shares(number_of, total, reach, skew, full):
    portions = [(1 << 20) // math.isqrt(grade ** skew) + 1 for grade in range(1, number_of + 1)]
    largest = reach if full else min(reach, max(-(-total // number_of), total * portions[0] // sum(portions)))
    least = 1 if total - largest >= number_of - 1 else 0
    holding, surplus = [largest] + [least] * (number_of - 1), total - largest - least * (number_of - 1)
    while surplus > 0:
        free = [i for i in range(1, number_of) if holding[i] < largest] or [i for i in range(1, number_of) if holding[i] < reach]
        mass, remaining = sum([portions[i] for i in free]), surplus
        for i in free:
            more = min(reach - holding[i], max(1, remaining * portions[i] // mass), surplus)
            holding[i] = holding[i] + more
            surplus = surplus - more
    return np.array(holding)


def gaussian(rng, shape, width, bound, shards=(), dtype=jnp.bfloat16):
    values = width * jax.random.normal(rng, shape, jnp.float32)
    if shards:
        values = values * block_levels(rng, shape, shards, -0.22, 0.18)
    return jnp.clip(values, -bound, bound).astype(dtype)


def setup_inputs(seed: int = 0) -> dict:
    arg_keys = jax.random.split(jax.random.key(seed), 10)
    radar_l = gaussian(arg_keys[0], (6, LINES_L, COLS), 1.0, 6.0, ((1, 4), (2, 8)))
    radar_s = gaussian(arg_keys[1], (6, LINES_S, COLS), 1.0, 6.0, ((1, 4), (2, 8)))
    weights_l = gaussian(arg_keys[2], (TILES_L, PIX, PIX), PIX ** -0.5, 0.5, ((0, 32),))
    weights_s = gaussian(arg_keys[3], (TILES_S, PIX, PIX), PIX ** -0.5, 0.5, ((0, 32),))
    owner_l_keys = jax.random.split(jax.random.fold_in(arg_keys[4], 1), TILES_L // TL_DEV)
    owner_l_turns = jax.random.permutation(jax.random.fold_in(arg_keys[4], 3), TILES_L // TL_DEV)
    owner_l = jax.vmap(lambda own, number: deal_out(jax.random.fold_in(arg_keys[4], 2), own, number, TL_DEV, DEVICES, 1, CAP_L, 2))(owner_l_keys, owner_l_turns).reshape((TILES_L, 1))
    owner_s_keys = jax.random.split(jax.random.fold_in(arg_keys[5], 1), TILES_S // TS_DEV)
    owner_s_turns = jax.random.permutation(jax.random.fold_in(arg_keys[5], 3), TILES_S // TS_DEV)
    owner_s = jax.vmap(lambda own, number: deal_out(jax.random.fold_in(arg_keys[5], 2), own, number, TS_DEV, DEVICES, 1, CAP_S, 2))(owner_s_keys, owner_s_turns).reshape((TILES_S, 1))
    slot_l = place_ends(jax.random.randint(arg_keys[6], (TILES_L,), 0, TS_DEV), jax.random.fold_in(arg_keys[6], 1), 0, TS_DEV - 1).astype(jnp.int32)
    slot_s = place_ends(jax.random.randint(arg_keys[7], (TILES_S,), 0, TS_DEV), jax.random.fold_in(arg_keys[7], 1), 0, TS_DEV - 1).astype(jnp.int32)
    models = gaussian(arg_keys[8], (NMODEL, 36), 36 ** -0.5, 1.0, (), jnp.float32)
    return dict(radar_l=radar_l, radar_s=radar_s, weights_l=weights_l, weights_s=weights_s, owner_l=owner_l, owner_s=owner_s, slot_l=slot_l, slot_s=slot_s, models=models)


cu_square = 0.25
fit_rate = 0.25
upper_pairs = [(first, second) for first in range(6) for second in range(first, 6)]
strict_pairs = [(first, second) for first in range(6) for second in range(first + 1, 6)]


def window_sum(padded):
    height = padded.shape[-2] - 2
    breadth = padded.shape[-1] - 2
    total = padded[..., 0:height, 0:breadth]
    for row_off in range(3):
        for col_off in range(3):
            if row_off + col_off > 0:
                total = total + padded[..., row_off:row_off + height, col_off:col_off + breadth]
    return total


def kuan_filter(padded):
    vectors = padded.astype(jnp.float32)
    height = vectors.shape[1] - 2
    breadth = vectors.shape[2] - 2
    local_mean = window_sum(vectors) / 9.0
    power = jnp.sum(vectors * vectors, axis=0)
    mean_power = window_sum(power) / 9.0
    spread = jnp.zeros_like(mean_power)
    for row_off in range(3):
        for col_off in range(3):
            spread = spread + (power[row_off:row_off + height, col_off:col_off + breadth] - mean_power) ** 2
    spread = spread / 9.0
    kuan_gain = spread / (spread + cu_square * mean_power * mean_power + 1.0)
    centre = vectors[:, 1:-1, 1:-1]
    return (local_mean + kuan_gain * (centre - local_mean)).astype(jnp.bfloat16)


def coherency(band_l, band_s):
    real_part = jnp.concatenate([band_l[0:3], band_s[0:3]], axis=0)
    imag_part = jnp.concatenate([band_l[3:6], band_s[3:6]], axis=0)
    parts = [real_part[first] * real_part[second] + imag_part[first] * imag_part[second] for first, second in upper_pairs]
    parts = parts + [imag_part[first] * real_part[second] - real_part[first] * imag_part[second] for first, second in strict_pairs]
    return jnp.stack(parts, axis=0)


def model_fit(smooth, models):
    powers = jnp.zeros((models.shape[0],) + smooth.shape[1:], jnp.float32)
    for iteration in range(FIT_ITERS):
        predicted = jnp.einsum('kc,klm->clm', models, powers, precision=lax.Precision.HIGHEST)
        powers = powers + fit_rate * jnp.einsum('kc,clm->klm', models, smooth - predicted, precision=lax.Precision.HIGHEST)
    return powers


def band_map(radar, weights, owner, slot, per_device):
    padded = jnp.pad(radar, ((0, 0), (1, 1), (1, 1)))
    filtered = kuan_filter(padded)
    device_total = N_SEC * N_SWATH
    tiles = filtered.reshape(6, N_SEC, per_device, N_SWATH, PIX).transpose(1, 3, 2, 0, 4).reshape(device_total, per_device, 6, PIX)
    weight_blocks = weights.reshape(device_total, per_device, PIX, PIX)

    def one_device(pair):
        weight_block, vector_block = pair
        return jnp.einsum('tqp,tcp->tcq', weight_block.astype(jnp.float32), vector_block.astype(jnp.float32)).astype(jnp.bfloat16)

    contribution = lax.map(one_device, (weight_blocks, tiles))
    flat_terms = contribution.reshape(device_total * per_device, 6 * PIX).astype(jnp.float32)
    segment = owner[:, 0].astype(jnp.int32) * TS_DEV + slot.astype(jnp.int32)
    summed = jax.ops.segment_sum(flat_terms, segment, num_segments=device_total * TS_DEV)
    return summed.reshape(N_SEC, N_SWATH, TS_DEV, 6, PIX).transpose(3, 0, 2, 1, 4).reshape(6, N_SEC * TS_DEV, N_SWATH * PIX)


def reference(radar_l, radar_s, weights_l, weights_s, owner_l, owner_s, slot_l, slot_s, models):
    map_l = band_map(radar_l, weights_l, owner_l, slot_l, TL_DEV)
    map_s = band_map(radar_s, weights_s, owner_s, slot_s, TS_DEV)
    joint = coherency(map_l, map_s)
    smooth = window_sum(jnp.pad(joint, ((0, 0), (1, 1), (1, 1)))) / 9.0
    return model_fit(smooth, models)
```

```python
import jax
import jax.numpy as jnp
from jax import lax
from jax.experimental import pallas as pl
from jax.experimental.pallas import tpu as pltpu
from jax.sharding import PartitionSpec as P

FIT_ITERS = 4
AXES = ("sec", "swath")

cu_square = 0.25
fit_rate = 0.25
upper_pairs = [(first, second) for first in range(6) for second in range(first, 6)]
strict_pairs = [(first, second) for first in range(6) for second in range(first + 1, 6)]
CHANNELS = len(upper_pairs) + len(strict_pairs)
NT = (((1,), (1,)), ((), ()))
NN = (((1,), (0,)), ((), ()))
TN = (((0,), (0,)), ((), ()))
HI = lax.Precision.HIGHEST
F32 = jnp.float32
BF16 = jnp.bfloat16
SUB = 8
LANES = 128


def params(mib):
    return pltpu.CompilerParams(vmem_limit_bytes=mib << 20)


def iota(shape, dim):
    return lax.broadcasted_iota(jnp.int32, shape, dim)


def ring(axis):
    peers = lax.axis_size(axis)
    up = [(i, (i + 1) % peers) for i in range(peers - 1)]
    return up, [(j, i) for i, j in up]


def whole(shape):
    return pl.BlockSpec(shape, lambda *_: (0,) * len(shape))


def plan_kernel(rows, caps, owner_l, slot_l, owner_s, slot_s, models, base_l, base_s, marks, kron):
    devices = marks.shape[0]
    total = jnp.zeros(marks.shape, F32)
    shift = 0
    bands = ((owner_l, slot_l, base_l), (owner_s, slot_s, base_s))
    for (owner, slot, base), row_count, capacity in zip(bands, rows, caps):
        tiles = owner.shape[1]
        hit = iota((devices, tiles), 0) == owner[...]
        hits = jnp.where(hit, 1.0, 0.0).astype(BF16)
        earlier = jnp.where(iota((tiles, tiles), 0) < iota((tiles, tiles), 1), 1.0, 0.0).astype(BF16)
        before = lax.dot_general(hits, earlier, NN, preferred_element_type=F32)
        rank = jnp.sum(jnp.where(hit, before, 0.0), axis=0, keepdims=True).astype(jnp.int32)
        base[...] = owner[...] * row_count + rank
        line = jnp.where(hit, slot[...] + 1, 0).astype(F32).astype(BF16)
        place = jnp.where(iota((LANES, tiles), 0) == rank + shift, 1.0, 0.0).astype(BF16)
        total = total + lax.dot_general(line, place, NT, preferred_element_type=F32)
        shift += capacity
    marks[...] = total
    m = models[...]
    eye = jnp.where(iota((CHANNELS, CHANNELS), 0) == iota((CHANNELS, CHANNELS), 1), 1.0, 0.0)
    powers = jnp.zeros(m.shape, F32)
    for _ in range(FIT_ITERS):
        predicted = lax.dot_general(m, powers, TN, precision=HI, preferred_element_type=F32)
        powers = powers + fit_rate * lax.dot_general(
            m, eye - predicted, NN, precision=HI, preferred_element_type=F32
        )
    powers = powers / 9.0
    wide_k, wide_c = kron.shape[0], kron.shape[1] // 3
    n_model = m.shape[0]
    left = jnp.where(iota((wide_k, n_model), 0) // SUB == iota((wide_k, n_model), 1), 1.0, 0.0)
    right = jnp.where(iota((CHANNELS, wide_c), 1) // SUB == iota((CHANNELS, wide_c), 0), 1.0, 0.0)
    spread = lax.dot_general(left, powers, NN, precision=HI, preferred_element_type=F32)
    spread = lax.dot_general(spread, right, NN, precision=HI, preferred_element_type=F32)
    same = iota((wide_k, wide_c), 0) % SUB == iota((wide_k, wide_c), 1) % SUB
    spread = jnp.where(same, spread, 0.0)
    high = spread.astype(BF16)
    low = (spread - high.astype(F32)).astype(BF16)
    kron[...] = jnp.concatenate([high, high, low], axis=1)


def with_sides(x, left, right):
    lane = iota(x.shape, 1)
    width = x.shape[1]
    before = jnp.where(lane == 0, left, pltpu.roll(x, 1, 1))
    after = jnp.where(lane == width - 1, right, pltpu.roll(x, width - 1, 1))
    return before, after


def send_kernel(
    rows, capacity, chunk, base, radar, sides, ends, corners, marks, weights, out,
    wbuf, sems, padded, power, filtered, packed,
):
    tiles = radar.shape[1]
    devices = out.shape[0]
    chunks = tiles // chunk

    def copy(i):
        return pltpu.make_async_copy(
            weights.at[pl.ds(i * chunk, chunk)], wbuf.at[pl.ds(i * chunk, chunk)], sems.at[i]
        )

    for i in range(chunks):
        copy(i).start()
    packed[...] = jnp.zeros_like(packed)
    comps = 6
    side = sides[...].astype(F32).T
    for c in range(comps):
        x = radar[c].astype(F32)
        padded[c, pl.ds(SUB, tiles), :] = x
        padded[c, pl.ds(SUB - 1, 1), :] = ends[c : c + 1, :].astype(F32)
        padded[c, pl.ds(SUB + tiles, 1), :] = ends[comps + c : comps + c + 1, :].astype(F32)
    corner = corners[...].astype(F32)
    lane = iota((SUB, LANES), 1)
    block = SUB

    def column(c, which, r):
        return side[r : r + block, which * SUB + c : which * SUB + c + 1]

    def one(c, rows_x, left, right):
        before, after = with_sides(rows_x, left, right)
        return rows_x + before + after

    for c in range(comps):
        pass
    hsum = padded
    def powers_of(get, lefts, rights):
        p = jnp.zeros(get(0).shape, F32)
        pl_, pr_ = jnp.zeros(lefts[0].shape, F32), jnp.zeros(rights[0].shape, F32)
        for c in range(comps):
            p = p + get(c) * get(c)
            pl_ = pl_ + lefts[c] * lefts[c]
            pr_ = pr_ + rights[c] * rights[c]
        before, after = with_sides(p, pl_, pr_)
        return p, before, after

    sums = filtered
    lefts = [side[:, c : c + 1] for c in range(comps)]
    rights = [side[:, SUB + c : SUB + c + 1] for c in range(comps)]
    body = [padded[c, pl.ds(SUB, tiles), :] for c in range(comps)]
    p, before, after = powers_of(lambda c: body[c], lefts, rights)
    power[0, pl.ds(SUB, tiles), :] = p
    power[1, pl.ds(SUB, tiles), :] = before
    power[2, pl.ds(SUB, tiles), :] = after
    for end, row in ((0, SUB - 1), (1, SUB + tiles)):
        get = [ends[end * comps + c : end * comps + c + 1, :].astype(F32) for c in range(comps)]
        cl = [corner[c : c + 1, 2 * end : 2 * end + 1] for c in range(comps)]
        cr = [corner[c : c + 1, 2 * end + 1 : 2 * end + 2] for c in range(comps)]
        p, before, after = powers_of(lambda c: get[c], cl, cr)
        power[0, pl.ds(row, 1), :] = p
        power[1, pl.ds(row, 1), :] = before
        power[2, pl.ds(row, 1), :] = after
    near = [power[k, pl.ds(SUB + d, tiles), :] for k in range(3) for d in (-1, 0, 1)]
    mean_power = sum(near[1:], near[0]) / 9.0
    spread = jnp.zeros_like(mean_power)
    for q in near:
        spread = spread + (q - mean_power) ** 2
    spread = spread / 9.0
    gain = spread / (spread + cu_square * mean_power * mean_power + 1.0)
    for c in range(comps):
        before, after = with_sides(body[c], lefts[c], rights[c])
        power[0, pl.ds(SUB, tiles), :] = body[c] + before + after
        for end, row in ((0, SUB - 1), (1, SUB + tiles)):
            x = ends[end * comps + c : end * comps + c + 1, :].astype(F32)
            before, after = with_sides(
                x, corner[c : c + 1, 2 * end : 2 * end + 1], corner[c : c + 1, 2 * end + 1 : 2 * end + 2]
            )
            power[0, pl.ds(row, 1), :] = x + before + after
        mean = power[0, pl.ds(SUB - 1, tiles), :] + power[0, pl.ds(SUB, tiles), :]
        mean = (mean + power[0, pl.ds(SUB + 1, tiles), :]) / 9.0
        filtered[pl.ds(c, tiles, stride=SUB), :] = mean + gain * (body[c] - mean)

    def step(i, _):
        copy(i).wait()
        for t in range(0, chunk, 2):
            tile = i * chunk + t
            at = pl.multiple_of(tile * SUB, SUB)
            lines = filtered[pl.ds(at, 2 * SUB), :].astype(BF16)
            matrix = wbuf[pl.ds(tile, 2)].reshape(2 * LANES, LANES)
            result = lax.dot_general(lines, matrix, NT, preferred_element_type=F32)
            first, second = base[tile], base[tile + 1]
            packed[pl.ds(first, comps, stride=capacity), :] = result[0:comps, 0:LANES]
            packed[pl.ds(second, comps, stride=capacity), :] = result[SUB : SUB + comps, LANES:]
        return _

    lax.fori_loop(0, chunks, step, 0)
    out[:, 0:rows, :] = packed[0 : devices * rows, :].reshape(devices, rows, LANES).astype(BF16)
    if out.shape[1] > rows:
        extra = jnp.broadcast_to(marks[...][:, None, :], (devices, SUB, LANES))
        out[:, rows:, :] = extra.astype(BF16)


def send(base, radar, sides, ends, corners, marks, weights, rows, capacity, with_marks):
    comps, tiles, _ = radar.shape
    devices = marks.shape[0]
    chunk = 32
    body = lambda *refs: send_kernel(rows, capacity, chunk, *refs)
    out_rows = rows + (SUB if with_marks else 0)
    vm = lambda x: pl.BlockSpec(x.shape, lambda i, b: (0,) * x.ndim)
    grid_spec = pltpu.PrefetchScalarGridSpec(
        num_scalar_prefetch=1,
        grid=(1,),
        in_specs=[vm(radar), vm(sides), vm(ends), vm(corners), vm(marks), pl.BlockSpec(memory_space=pl.ANY)],
        out_specs=pl.BlockSpec((devices, out_rows, LANES), lambda i, b: (0, 0, 0)),
        scratch_shapes=[
            pltpu.VMEM(weights.shape, BF16),
            pltpu.SemaphoreType.DMA((tiles // chunk,)),
            pltpu.VMEM((comps, tiles + 2 * SUB, LANES), F32),
            pltpu.VMEM((3, tiles + 2 * SUB, LANES), F32),
            pltpu.VMEM((tiles * SUB, LANES), F32),
            pltpu.VMEM((devices * rows + SUB, LANES), F32),
        ],
    )
    return pl.pallas_call(
        body,
        grid_spec=grid_spec,
        out_shape=jax.ShapeDtypeStruct((devices, out_rows, LANES), BF16),
        compiler_params=params(48),
        cost_estimate=pl.CostEstimate(
            flops=2 * tiles * 8 * LANES * LANES, bytes_accessed=weights.size * 2, transcendentals=0
        ),
    )(base, radar, sides, ends, corners, marks, weights)


def merge_kernel(rows, caps, got_l, got_s, pick_l, pick_s, kron, out, rim_rows, rim_cols, stage, line_marks, maps):
    devices = got_l.shape[0]
    map_lines = out.shape[1]
    for s in range(devices):
        line_marks[s : s + 1, :] = got_s[s, rows[1] : rows[1] + SUB, :].astype(F32)[0:1, :]
    marks = line_marks[...].astype(BF16)
    for band, (got, pick) in enumerate(((got_l, pick_l), (got_s, pick_s))):
        capacity = caps[band]
        places = devices * capacity
        for s in range(devices):
            block = got[s].astype(F32)
            for c in range(6):
                stage[s * capacity : (s + 1) * capacity, c * LANES : (c + 1) * LANES] = block[
                    c * capacity : (c + 1) * capacity, :
                ]
        wide = lax.dot_general(marks, pick[...], NN, preferred_element_type=F32)
        low = iota((devices, places), 0) * capacity
        at = iota((devices, places), 1)
        mine = (at >= low) & (at < low + capacity)
        line = jnp.sum(jnp.where(mine, wide, 0.0), axis=0, keepdims=True).astype(jnp.int32)
        table = jnp.where(iota((map_lines, places), 0) + 1 == line, 1.0, 0.0).astype(BF16)
        summed = lax.dot_general(
            table, stage[0:places, :].astype(BF16), NN, preferred_element_type=F32
        )
        for c in range(6):
            maps[band * 6 + c] = summed[:, c * LANES : (c + 1) * LANES]

    matrix = kron[...]

    def step(i, _):
        halves_high, halves_low = [], []
        for h in range(2):
            r = pl.multiple_of((2 * i + h) * SUB, SUB)
            real = [maps[b * 6 + c, pl.ds(r, SUB), :] for b in range(2) for c in range(3)]
            imag = [maps[b * 6 + 3 + c, pl.ds(r, SUB), :] for b in range(2) for c in range(3)]
            joint = [real[f] * real[g] + imag[f] * imag[g] for f, g in upper_pairs]
            joint += [imag[f] * real[g] - real[f] * imag[g] for f, g in strict_pairs]
            x = jnp.concatenate(joint, axis=0)
            high = x.astype(BF16)
            halves_high.append(high)
            halves_low.append((x - high.astype(F32)).astype(BF16))
        high = jnp.concatenate(halves_high, axis=1)
        low = jnp.concatenate(halves_low, axis=1)
        x = jnp.concatenate([high, low, high], axis=0)
        result = lax.dot_general(matrix, x, NN, preferred_element_type=F32)
        for h in range(2):
            r = pl.multiple_of((2 * i + h) * SUB, SUB)
            for k in range(out.shape[0]):
                out[k, pl.ds(r, SUB), :] = result[k * SUB : (k + 1) * SUB, h * LANES : (h + 1) * LANES]
        return _

    lax.fori_loop(0, map_lines // (2 * SUB), step, 0)
    for k in range(out.shape[0]):
        rim_rows[0, k : k + 1, :] = out[k, 0:1, :]
        rim_rows[1, k : k + 1, :] = out[k, map_lines - 1 : map_lines, :]
        turned = out[k].T
        rim_cols[0, k : k + 1, :] = turned[0:1, :]
        rim_cols[1, k : k + 1, :] = turned[LANES - 1 : LANES, :]


def merge(got_l, got_s, kron, rows, caps, map_lines, n_model):
    devices = got_l.shape[0]

    def picks(capacity, shift):
        e = jnp.arange(devices * capacity, dtype=jnp.int32) % capacity
        return (jnp.arange(LANES, dtype=jnp.int32)[:, None] == e[None, :] + shift).astype(BF16)

    args = (got_l, got_s, picks(caps[0], 0), picks(caps[1], caps[0]), kron)
    shapes = [
        jax.ShapeDtypeStruct((n_model, map_lines, LANES), F32),
        jax.ShapeDtypeStruct((2, n_model, LANES), F32),
        jax.ShapeDtypeStruct((2, n_model, map_lines), F32),
    ]
    return pl.pallas_call(
        lambda *refs: merge_kernel(rows, caps, *refs),
        grid=(1,),
        in_specs=[whole(x.shape) for x in args],
        out_specs=[whole(x.shape) for x in shapes],
        out_shape=shapes,
        scratch_shapes=[
            pltpu.VMEM((devices * max(caps), 6 * LANES), F32),
            pltpu.VMEM((devices, LANES), F32),
            pltpu.VMEM((12, map_lines, LANES), F32),
        ],
        compiler_params=params(48),
    )(*args)


def smooth_kernel(fit, sides, ends, corners, out, padded):
    n_model, map_lines, _ = fit.shape
    side = sides[...].T
    corner = corners[...]
    for k in range(n_model):
        x = fit[k]
        before, after = with_sides(x, side[:, k : k + 1], side[:, n_model + k : n_model + k + 1])
        padded[pl.ds(SUB, map_lines), :] = x + before + after
        for end, row in ((0, SUB - 1), (1, SUB + map_lines)):
            y = ends[end, k : k + 1, :]
            before, after = with_sides(
                y, corner[end, k : k + 1, 0:1], corner[end, k : k + 1, 1:2]
            )
            padded[pl.ds(row, 1), :] = y + before + after
        total = padded[pl.ds(SUB - 1, map_lines), :] + padded[pl.ds(SUB, map_lines), :]
        out[k] = total + padded[pl.ds(SUB + 1, map_lines), :]


def smooth(fit, sides, ends, corners):
    args = (fit, sides, ends, corners)
    return pl.pallas_call(
        smooth_kernel,
        grid=(1,),
        in_specs=[whole(x.shape) for x in args],
        out_specs=whole(fit.shape),
        out_shape=jax.ShapeDtypeStruct(fit.shape, F32),
        scratch_shapes=[pltpu.VMEM((fit.shape[1] + 2 * SUB, LANES), F32)],
        compiler_params=params(48),
    )(*args)


def exchange(first, last, axis):
    up, down = ring(axis)
    return lax.ppermute(last, axis, up), lax.ppermute(first, axis, down)


def body(radar_l, radar_s, weights_l, weights_s, owner_l, owner_s, slot_l, slot_s, models):
    devices = lax.axis_size(AXES)
    lines_l = radar_l.shape[1]
    map_lines = radar_s.shape[1]
    n_model = models.shape[0]
    caps = (max(2, 2 * lines_l // devices), max(2, 2 * map_lines // devices))
    rows = tuple(-(-6 * capacity // SUB) * SUB for capacity in caps)

    plan_args = (
        owner_l.reshape(1, -1), slot_l.reshape(1, -1), owner_s.reshape(1, -1), slot_s.reshape(1, -1), models,
    )
    plan_shapes = [
        jax.ShapeDtypeStruct((1, lines_l), jnp.int32),
        jax.ShapeDtypeStruct((1, map_lines), jnp.int32),
        jax.ShapeDtypeStruct((devices, LANES), F32),
        jax.ShapeDtypeStruct((n_model * SUB, 3 * CHANNELS * SUB), BF16),
    ]
    base_l, base_s, marks, kron = pl.pallas_call(
        lambda *refs: plan_kernel(rows, caps, *refs),
        grid=(1,),
        in_specs=[whole(x.shape) for x in plan_args],
        out_specs=[whole(x.shape) for x in plan_shapes],
        out_shape=plan_shapes,
        compiler_params=params(32),
        cost_estimate=pl.CostEstimate(flops=50_000_000, bytes_accessed=4_000_000, transcendentals=0),
    )(*plan_args)

    both = lambda f: jnp.concatenate([f(radar_l), f(radar_s)], axis=1)
    before, after = exchange(both(lambda r: r[:, :, 0]), both(lambda r: r[:, :, -1]), "swath")
    edge = lambda line_l, line_s: jnp.concatenate(
        [
            jnp.concatenate([radar_l[:, line_l], radar_s[:, line_s]], axis=0),
            jnp.pad(
                jnp.concatenate(
                    [
                        jnp.stack([before[:, line_l], after[:, line_l]], axis=1),
                        jnp.stack([before[:, lines_l + line_s], after[:, lines_l + line_s]], axis=1),
                    ],
                    axis=0,
                ),
                ((0, 0), (0, LANES - 2)),
            ),
        ],
        axis=0,
    )
    above, below = exchange(edge(0, 0), edge(lines_l - 1, map_lines - 1), "sec")

    def halo(band):
        part = slice(0, lines_l) if band == 0 else slice(lines_l, None)
        pad = jnp.zeros((2, before[:, part].shape[1]), BF16)
        sides = jnp.concatenate([before[:, part], pad, after[:, part], pad], axis=0)
        r = 6 * band
        ends = jnp.concatenate([above[r : r + 6], below[r : r + 6]], axis=0)
        corners = jnp.concatenate([above[12 + r : 18 + r, 0:2], below[12 + r : 18 + r, 0:2]], axis=1)
        return sides, ends, corners

    sent_s = send(base_s.reshape(-1), radar_s, *halo(1), marks, weights_s, rows[1], caps[1], True)
    got_s = lax.all_to_all(sent_s, AXES, split_axis=0, concat_axis=0, tiled=True)
    sent_l = send(base_l.reshape(-1), radar_l, *halo(0), marks, weights_l, rows[0], caps[0], False)
    got_l = lax.all_to_all(sent_l, AXES, split_axis=0, concat_axis=0, tiled=True)

    fit, rim_rows, rim_cols = merge(got_l, got_s, kron, rows, caps, map_lines, n_model)
    before, after = exchange(rim_cols[0], rim_cols[1], "swath")
    edge = lambda k: jnp.concatenate(
        [rim_rows[k], jnp.pad(jnp.stack([before[:, -k], after[:, -k]], axis=1), ((0, 0), (0, LANES - 2)))], axis=0
    )
    above, below = exchange(edge(0), edge(1), "sec")
    ends = jnp.stack([above[:n_model], below[:n_model]], axis=0)
    corners = jnp.stack([above[n_model:, 0:2], below[n_model:, 0:2]], axis=0)
    return smooth(fit, jnp.concatenate([before, after], axis=0), ends, corners)


def solution(mesh):
    in_specs = (
        P(None, "sec", "swath"),
        P(None, "sec", "swath"),
        P(("sec", "swath"), None, None),
        P(("sec", "swath"), None, None),
        P(("sec", "swath"), None),
        P(("sec", "swath"), None),
        P(("sec", "swath")),
        P(("sec", "swath")),
        P(),
    )
    out_specs = P(None, "sec", "swath")
    return jax.shard_map(body, mesh=mesh, in_specs=in_specs, out_specs=out_specs, check_vma=False)
```

```python
import jax
import jax.numpy as jnp
from jax import lax
from jax.experimental import pallas as pl
from jax.experimental.pallas import tpu as pltpu
from jax.sharding import PartitionSpec as P

FIT_ITERS = 4
AXES = ("sec", "swath")

cu_square = 0.25
fit_rate = 0.25
upper_pairs = [(first, second) for first in range(6) for second in range(first, 6)]
strict_pairs = [(first, second) for first in range(6) for second in range(first + 1, 6)]
CHANNELS = len(upper_pairs) + len(strict_pairs)
COMPS = 6
NT = (((1,), (1,)), ((), ()))
NN = (((1,), (0,)), ((), ()))
TN = (((0,), (0,)), ((), ()))
HI = lax.Precision.HIGHEST
F32 = jnp.float32
BF16 = jnp.bfloat16
SUB = 8
LANES = 128
EXTRA = 5


def params(mib):
    return pltpu.CompilerParams(vmem_limit_bytes=mib << 20)


def iota(shape, dim):
    return lax.broadcasted_iota(jnp.int32, shape, dim)


def dot(a, b, dims, precision=None):
    return lax.dot_general(a, b, dims, precision=precision, preferred_element_type=F32)


def ones_where(mask, dtype=BF16):
    return jnp.where(mask, 1.0, 0.0).astype(dtype)


def exchange(first, last, axis):
    peers = lax.axis_size(axis)
    up = [(i, i + 1) for i in range(peers - 1)]
    down = [(j, i) for i, j in up]
    return lax.ppermute(last, axis, up), lax.ppermute(first, axis, down)


VMEM = pl.BlockSpec(memory_space=pltpu.VMEM)
SMEM = pl.BlockSpec(memory_space=pltpu.SMEM)


def up_to(n, multiple):
    return -(-n // multiple) * multiple


class Sizes:
    def __init__(self, lines_l, map_lines, n_model):
        self.devices = lax.axis_size(AXES)
        self.swath = lax.axis_size("swath")
        self.lines = (lines_l, map_lines)
        self.map_lines = map_lines
        self.n_model = n_model
        self.caps = tuple(max(2, 2 * lines // self.devices) for lines in self.lines)
        self.starts = (0, COMPS * self.caps[0])
        self.rows = up_to(COMPS * sum(self.caps), SUB)
        self.stride = up_to(self.rows + SUB, LANES)
        self.lanes = up_to(self.rows, LANES)


def first_kernel(z, radar_l, radar_s, owner_l, slot_l, owner_s, slot_s, first, last, base_l, base_s, marks):
    wide = COMPS * LANES
    pick = iota((2 * SUB, wide), 1) == jnp.where(
        iota((2 * SUB, wide), 0) < SUB,
        iota((2 * SUB, wide), 0) * LANES,
        (iota((2 * SUB, wide), 0) - SUB) * LANES + LANES - 1,
    )
    pick = ones_where(pick)
    at = 0
    for radar, lines in ((radar_l, z.lines[0]), (radar_s, z.lines[1])):
        rows = jnp.concatenate([radar[c] for c in range(COMPS)], axis=1)
        both = dot(pick, rows, NT)
        first[:, at : at + lines] = both[0:SUB].astype(BF16)
        last[:, at : at + lines] = both[SUB:].astype(BF16)
        at += lines
    total = jnp.zeros((z.devices, LANES), F32)
    shift = 0
    for band, (owner, slot, base) in enumerate(((owner_l, slot_l, base_l), (owner_s, slot_s, base_s))):
        tiles = z.lines[band]
        hit = iota((z.devices, tiles), 0) == owner[...]
        earlier = ones_where(iota((tiles, tiles), 0) < iota((tiles, tiles), 1))
        before = dot(ones_where(hit), earlier, NN)
        rank = jnp.sum(jnp.where(hit, before, 0.0), axis=0, keepdims=True).astype(jnp.int32)
        base[...] = owner[...] * z.stride + z.starts[band] + rank
        line = jnp.where(hit, slot[...] + 1, 0).astype(F32).astype(BF16)
        place = ones_where(iota((LANES, tiles), 0) == rank + shift)
        total = total + dot(line, place, NT)
        shift += z.caps[band]
    me, other = iota((z.devices, z.devices), 0), iota((z.devices, z.devices), 1)
    swath = z.swath
    inner = iota((z.devices, z.devices), 0) % swath
    own = total.astype(BF16)
    before = dot(ones_where((other == me - 1) & (inner > 0)), own, NN)
    after = dot(ones_where((other == me + 1) & (inner < swath - 1)), own, NN)
    marks[...] = total + pltpu.roll(before, shift, 1) + pltpu.roll(after, 2 * shift, 1)


def second_kernel(z, top_l, top_s, bottom_l, bottom_s, before, after, first, last):
    lines_l, lines_s = z.lines
    ends = (
        (first, top_l, top_s, 0, 0, lines_l),
        (last, bottom_l, bottom_s, top_l.shape[1] - 1, lines_l - 1, lines_l + lines_s - 1),
    )
    for out, rows_l, rows_s, row, at_l, at_s in ends:
        parts = [rows_l[...].astype(F32)[:, row, :], rows_s[...].astype(F32)[:, row, :]]
        for side in (before, after):
            for at in (at_l, at_s):
                tile = at // LANES * LANES
                column = side[:, tile : tile + LANES].astype(F32)[0:COMPS, at - tile : at - tile + 1]
                parts.append(jnp.broadcast_to(column, (COMPS, LANES)))
        parts.append(jnp.zeros((out.shape[0] - 6 * COMPS, LANES), F32))
        out[...] = jnp.concatenate(parts, axis=0).astype(BF16)


def with_sides(x, left, right):
    lane = iota(x.shape, 1)
    width = x.shape[1]
    before = jnp.where(lane == 0, left, pltpu.roll(x, 1, 1))
    after = jnp.where(lane == width - 1, right, pltpu.roll(x, width - 1, 1))
    return before, after


def filter_band(band, tiles, radar, left, right, above, below, work, filtered):
    inner = pl.ds(SUB, tiles)
    ends = ((SUB - 1, above), (SUB + tiles, below))

    def end_values(strip, c):
        row = band * COMPS + c
        corner = 2 * COMPS + row
        return strip[row : row + 1], strip[corner : corner + 1, 0:1], strip[corner + 2 * COMPS : corner + 2 * COMPS + 1, 0:1]

    def power_of(values):
        total = [0.0, 0.0, 0.0]
        for triple in values:
            total = [t + v * v for t, v in zip(total, triple)]
        return (total[0],) + with_sides(*total)

    body = [radar[c].astype(F32) for c in range(COMPS)]
    lefts = [left[:, c : c + 1] for c in range(COMPS)]
    rights = [right[:, c : c + 1] for c in range(COMPS)]
    for plane, value in enumerate(power_of(zip(body, lefts, rights))):
        work[plane, inner, :] = value
    for row, strip in ends:
        for plane, value in enumerate(power_of([end_values(strip, c) for c in range(COMPS)])):
            work[plane, pl.ds(row, 1), :] = value
    near = [work[plane, pl.ds(SUB + d, tiles), :] for plane in range(3) for d in (-1, 0, 1)]
    mean_power = sum(near[1:], near[0]) / 9.0
    spread = jnp.zeros_like(mean_power)
    for q in near:
        spread = spread + (q - mean_power) ** 2
    spread = spread / 9.0
    gain = spread / (spread + cu_square * mean_power * mean_power + 1.0)
    for c in range(COMPS):
        plane = c % 3
        before, after = with_sides(body[c], lefts[c], rights[c])
        work[plane, inner, :] = body[c] + before + after
        for row, strip in ends:
            x, corner_left, corner_right = end_values(strip, c)
            before, after = with_sides(x, corner_left, corner_right)
            work[plane, pl.ds(row, 1), :] = x + before + after
        mean = work[plane, pl.ds(SUB - 1, tiles), :] + work[plane, inner, :]
        mean = (mean + work[plane, pl.ds(SUB + 1, tiles), :]) / 9.0
        filtered[pl.ds(c, tiles, stride=SUB), :] = mean + gain * (body[c] - mean)


def send_kernel(
    z, base_l, base_s, radar_l, radar_s, before, after, above, below, marks, weights_l, weights_s,
    out, work, filtered, packed, held_l, held_s, arrived,
):
    chunks = []
    for source, held, lines in ((weights_l, held_l, z.lines[0]), (weights_s, held_s, z.lines[1])):
        size = 64 if lines % 64 == 0 else lines
        copies = []
        for at in range(0, lines, size):
            part = pl.ds(at, size)
            copies.append(
                pltpu.make_async_copy(source.at[part], held.at[part], arrived.at[sum(map(len, chunks)) + len(copies)])
            )
            copies[-1].start()
        chunks.append(copies)
    packed[...] = jnp.zeros_like(packed)
    left, right = before[...].astype(F32).T, after[...].astype(F32).T
    up, down = above[...].astype(F32), below[...].astype(F32)
    at = 0
    for band, (radar, base, weights) in enumerate(
        ((radar_l, base_l, held_l), (radar_s, base_s, held_s))
    ):
        tiles, capacity = z.lines[band], z.caps[band]
        filter_band(
            band, tiles, radar, left[at : at + tiles], right[at : at + tiles], up, down, work, filtered
        )
        at += tiles

        size = tiles // len(chunks[band])
        for i, copy in enumerate(chunks[band]):
            copy.wait()
            for t in range(0, size, 2):
                tile = i * size + t
                lines = filtered[pl.ds(tile * SUB, 2 * SUB), :].astype(BF16)
                matrix = weights[pl.ds(tile, 2)].reshape(2 * LANES, LANES)
                result = dot(lines, matrix, NT)
                first, second = base[0, tile], base[0, tile + 1]
                packed[pl.ds(first, COMPS, stride=capacity), :] = result[0:COMPS, 0:LANES]
                packed[pl.ds(second, COMPS, stride=capacity), :] = result[SUB : SUB + COMPS, LANES:]

    steps = z.lanes // LANES
    row, lane = iota((SUB, LANES), 0), iota((SUB, LANES), 1)
    pick = ones_where(
        ((row >= 1) & (row <= steps) & (lane == LANES - 1)) | ((row > steps) & (row <= 2 * steps) & (lane == 0))
    )
    columns = []
    for o in range(z.devices):
        columns.append(dot(pick, packed[o * z.stride : o * z.stride + z.lanes, :].astype(BF16), NT))
    for o in range(z.devices):
        extra = jnp.broadcast_to(marks[o : o + 1, :], (SUB, LANES))
        one_less, one_more = max(o - 1, 0), min(o + 1, z.devices - 1)
        for k in range(steps):
            part = slice(k * LANES, (k + 1) * LANES)
            extra = jnp.where(row == 1 + k, columns[one_less][:, part], extra)
            extra = jnp.where(row == 1 + steps + k, columns[one_more][:, part], extra)
        packed[o * z.stride + z.rows : o * z.stride + z.rows + SUB, :] = extra
    for o in range(z.devices):
        out[o] = packed[o * z.stride : o * z.stride + z.rows + SUB, :].astype(BF16)


def matrix_kernel(models, small, wide):
    m = models[...]
    n_model = m.shape[0]
    eye = ones_where(iota((CHANNELS, CHANNELS), 0) == iota((CHANNELS, CHANNELS), 1), F32)
    powers = jnp.zeros(m.shape, F32)
    for _ in range(FIT_ITERS):
        predicted = dot(m, powers, TN, HI)
        powers = powers + fit_rate * dot(m, eye - predicted, NN, HI)
    powers = powers / 9.0
    small[...] = powers
    rows, columns = wide.shape[0], wide.shape[1] // 3
    left = ones_where(iota((rows, n_model), 0) // SUB == iota((rows, n_model), 1), F32)
    right = ones_where(iota((CHANNELS, columns), 1) // SUB == iota((CHANNELS, columns), 0), F32)
    spread = dot(dot(left, powers, NN, HI), right, NN, HI)
    same = iota((rows, columns), 0) % SUB == iota((rows, columns), 1) % SUB
    spread = jnp.where(same, spread, 0.0)
    high = spread.astype(BF16)
    low = (spread - high.astype(F32)).astype(BF16)
    wide[...] = jnp.concatenate([high, high, low], axis=1)


def coherency(real, imag):
    joint = [real[f] * real[g] + imag[f] * imag[g] for f, g in upper_pairs]
    return joint + [imag[f] * real[g] - real[f] * imag[g] for f, g in strict_pairs]


def split_parts(maps):
    pick = lambda at: [maps(band * COMPS + at + c) for band in range(2) for c in range(3)]
    return pick(0), pick(3)


def merge_kernel(z, got, small, wide, out, rim_first, rim_last, stage, extras, maps, fits):
    map_lines, n_model, devices = z.map_lines, z.n_model, z.devices
    steps = z.lanes // LANES
    for s in range(devices):
        extras[s * SUB : (s + 1) * SUB, :] = got[s, z.rows : z.rows + SUB, :].astype(F32)
    piece = lambda r: extras[pl.ds(r, devices, stride=SUB), :]
    marks = piece(0)
    sides = [
        jnp.concatenate([piece(1 + side * steps + k) for k in range(steps)], axis=1) for side in range(2)
    ]
    shift = sum(z.caps)
    edges = [[None] * (2 * COMPS) for _ in range(2)]
    at_mark = 0
    for band in range(2):
        capacity = z.caps[band]
        places = devices * capacity
        for s in range(devices):
            block = got[s, 0 : z.rows, :].astype(F32)
            for c in range(COMPS):
                low = z.starts[band] + c * capacity
                stage[s * capacity : (s + 1) * capacity, c * LANES : (c + 1) * LANES] = block[
                    low : low + capacity, :
                ]
        turned = lambda x, by: pltpu.roll(x, (x.shape[1] - by) % x.shape[1], 1)[:, 0:LANES]
        rows = [turned(marks, at_mark + k * shift) for k in range(3)]
        for side in range(2):
            rows += [turned(sides[side], z.starts[band] + c * capacity) for c in range(COMPS)]
        at_mark += capacity
        place = iota((devices, places), 1)
        low = iota((devices, places), 0) * capacity
        mine = (place >= low) & (place < low + capacity)
        offset = jnp.sum(jnp.where(mine, place - low, 0), axis=0, keepdims=True)
        pick = ones_where(iota((LANES, places), 0) == offset)
        spread = dot(jnp.concatenate(rows, axis=0).astype(BF16), pick, NN)
        flat = [
            jnp.sum(jnp.where(mine, spread[k * devices : (k + 1) * devices], 0.0), axis=0, keepdims=True)
            for k in range(len(rows))
        ]
        lines = iota((map_lines, places), 0) + 1
        tables = [ones_where(lines == flat[k].astype(jnp.int32)) for k in range(3)]
        summed = dot(tables[0], stage[0:places, :].astype(BF16), NN)
        for c in range(COMPS):
            maps[band * COMPS + c] = summed[:, c * LANES : (c + 1) * LANES]
        for side in range(2):
            values = flat[3 + side * COMPS : 3 + (side + 1) * COMPS]
            values = jnp.concatenate(values + [jnp.zeros((SUB - COMPS, places), F32)], axis=0).astype(BF16)
            column = dot(values, tables[1 + side], NT)
            for c in range(COMPS):
                edges[side][band * COMPS + c] = column[c : c + 1, :]
    turned = []
    for side in range(2):
        joint = jnp.concatenate(coherency(*split_parts(lambda i: edges[side][i])), axis=0)
        turned.append(dot(small[...], joint, NN, HI).T)

    matrix = wide[...]

    def step(i, _):
        halves = []
        for h in range(2):
            r = pl.multiple_of((2 * i + h) * SUB, SUB)
            x = jnp.concatenate(coherency(*split_parts(lambda n: maps[n, pl.ds(r, SUB), :])), axis=0)
            halves.append(x)
        x = jnp.concatenate(halves, axis=1)
        high = x.astype(BF16)
        low = (x - high.astype(F32)).astype(BF16)
        result = dot(matrix, jnp.concatenate([high, low, high], axis=0), NN)
        for h in range(2):
            r = pl.multiple_of((2 * i + h) * SUB, SUB)
            for k in range(n_model):
                fits[k, pl.ds(SUB + r, SUB), :] = result[
                    k * SUB : (k + 1) * SUB, h * LANES : (h + 1) * LANES
                ]
        return _

    lax.fori_loop(0, map_lines // (2 * SUB), step, 0)
    blank = jnp.zeros((1, LANES), F32)
    inner = pl.ds(SUB, map_lines)
    for k in range(n_model):
        x = fits[k, inner, :]
        before, after = with_sides(x, turned[0][:, k : k + 1], turned[1][:, k : k + 1])
        x = x + before + after
        fits[k, inner, :] = x
        fits[k, SUB - 1 : SUB, :] = blank
        fits[k, SUB + map_lines : SUB + map_lines + 1, :] = blank
        rim_first[k : k + 1, :] = x[0:1, :]
        rim_last[k : k + 1, :] = x[map_lines - 1 :, :]
        out[k] = fits[k, pl.ds(SUB - 1, map_lines), :] + x + fits[k, pl.ds(SUB + 1, map_lines), :]


def finish_kernel(fit, above, below, out):
    end = pl.program_id(0)
    line = iota(fit.shape[1:], 0)
    height = fit.shape[1]
    for k in range(fit.shape[0]):
        upper = jnp.where((line == 0) & (end == 0), above[k : k + 1, :], 0.0)
        lower = jnp.where((line == height - 1) & (end == 1), below[k : k + 1, :], 0.0)
        out[k] = fit[k] + upper + lower


def body(radar_l, radar_s, weights_l, weights_s, owner_l, owner_s, slot_l, slot_s, models):
    z = Sizes(radar_l.shape[1], radar_s.shape[1], models.shape[0])
    lines_l, lines_s = z.lines
    shape = jax.ShapeDtypeStruct

    def call(kernel, args, shapes, mib, scratch=(), specs=None, flops=0, size=0):
        return pl.pallas_call(
            lambda *refs: kernel(z, *refs) if kernel is not matrix_kernel else kernel(*refs),
            in_specs=specs or [VMEM] * len(args),
            out_specs=[VMEM] * len(shapes),
            out_shape=shapes,
            scratch_shapes=scratch,
            compiler_params=params(mib),
            cost_estimate=pl.CostEstimate(flops=flops, bytes_accessed=size, transcendentals=0),
        )(*args)

    row = lambda x: x.reshape(1, -1)
    column = shape((SUB, lines_l + lines_s), BF16)
    first, last, base_l, base_s, marks = call(
        first_kernel,
        (radar_l, radar_s, row(owner_l), row(slot_l), row(owner_s), row(slot_s)),
        [column, column, shape((1, lines_l), jnp.int32), shape((1, lines_s), jnp.int32), shape((z.devices, LANES), F32)],
        16, flops=30_000_000, size=2_000_000,
    )
    before, after = exchange(first, last, "swath")
    strip = shape((5 * SUB, LANES), BF16)
    tall = 2 * SUB
    edge = lambda lines, end: pl.BlockSpec(
        (COMPS, tall, LANES), lambda i: (0, end * (lines // tall - 1), 0)
    )
    side = pl.BlockSpec(before.shape, lambda i: (0, 0))
    first, last = pl.pallas_call(
        lambda *refs: second_kernel(z, *refs),
        grid=(1,),
        in_specs=[edge(lines, end) for end in range(2) for lines in z.lines] + [side, side],
        out_specs=[pl.BlockSpec(strip.shape, lambda i: (0, 0))] * 2,
        out_shape=[strip, strip],
        compiler_params=params(16),
    )(radar_l, radar_s, radar_l, radar_s, before, after)
    above, below = exchange(first, last, "sec")
    args = (base_l, base_s, radar_l, radar_s, before, after, above, below, marks, weights_l, weights_s)
    (sent,) = call(
        send_kernel,
        args,
        [shape((z.devices, z.rows + SUB, LANES), BF16)],
        44,
        specs=[SMEM, SMEM] + [VMEM] * (len(args) - 4) + [pl.BlockSpec(memory_space=pl.ANY)] * 2,
        scratch=[
            pltpu.VMEM((3, max(z.lines) + 2 * SUB, LANES), F32),
            pltpu.VMEM((max(z.lines) * SUB, LANES), F32),
            pltpu.VMEM((z.devices * z.stride + up_to(COMPS * max(z.caps), SUB), LANES), F32),
            pltpu.VMEM(weights_l.shape, BF16),
            pltpu.VMEM(weights_s.shape, BF16),
            pltpu.SemaphoreType.DMA((-(-lines_l // 64) - (-lines_s // 64),)),
        ],
        flops=2 * sum(z.lines) * 16 * LANES * LANES,
        size=2 * (weights_l.size + weights_s.size),
    )
    got = lax.all_to_all(sent, AXES, split_axis=0, concat_axis=0, tiled=True)

    small, wide = call(
        matrix_kernel,
        (models,),
        [shape((z.n_model, CHANNELS), F32), shape((z.n_model * SUB, 3 * CHANNELS * SUB), BF16)],
        16, flops=50_000_000, size=1_000_000,
    )
    rim = shape((z.n_model, LANES), F32)
    fit, rim_first, rim_last = call(
        merge_kernel,
        (got, small, wide),
        [shape((z.n_model, z.map_lines, LANES), F32), rim, rim],
        32,
        scratch=[
            pltpu.VMEM((z.devices * max(z.caps), COMPS * LANES), F32),
            pltpu.VMEM((z.devices * SUB, LANES), F32),
            pltpu.VMEM((2 * COMPS, z.map_lines, LANES), F32),
            pltpu.VMEM((z.n_model, z.map_lines + 2 * SUB, LANES), F32),
        ],
        flops=1_000_000_000,
        size=4_000_000,
    )
    above, below = exchange(rim_first, rim_last, "sec")
    ends = pl.BlockSpec((z.n_model, SUB, LANES), lambda i: (0, i * (z.map_lines // SUB - 1), 0))
    edge = pl.BlockSpec((z.n_model, LANES), lambda i: (0, 0))
    return pl.pallas_call(
        finish_kernel,
        grid=(2,),
        in_specs=[ends, edge, edge],
        out_specs=ends,
        out_shape=shape(fit.shape, F32),
        input_output_aliases={0: 0},
        compiler_params=params(16),
    )(fit, above, below)


def solution(mesh):
    in_specs = (
        P(None, "sec", "swath"),
        P(None, "sec", "swath"),
        P(("sec", "swath"), None, None),
        P(("sec", "swath"), None, None),
        P(("sec", "swath"), None),
        P(("sec", "swath"), None),
        P(("sec", "swath")),
        P(("sec", "swath")),
        P(),
    )
    out_specs = P(None, "sec", "swath")
    return jax.shard_map(body, mesh=mesh, in_specs=in_specs, out_specs=out_specs, check_vma=False)
```

```python
import jax
import jax.numpy as jnp
from jax import lax
from jax.experimental import pallas as pl
from jax.experimental.pallas import tpu as pltpu
from jax.sharding import PartitionSpec as P

FIT_ITERS = 4
AXES = ("sec", "swath")

cu_square = 0.25
fit_rate = 0.25
upper_pairs = [(first, second) for first in range(6) for second in range(first, 6)]
strict_pairs = [(first, second) for first in range(6) for second in range(first + 1, 6)]
CHANNELS = len(upper_pairs) + len(strict_pairs)
COMPS = 6
NT = (((1,), (1,)), ((), ()))
NN = (((1,), (0,)), ((), ()))
TN = (((0,), (0,)), ((), ()))
HI = lax.Precision.HIGHEST
F32 = jnp.float32
BF16 = jnp.bfloat16
SUB = 8
LANES = 128
EXTRA = 5


def params(mib):
    return pltpu.CompilerParams(vmem_limit_bytes=mib << 20)


def iota(shape, dim):
    return lax.broadcasted_iota(jnp.int32, shape, dim)


def dot(a, b, dims, precision=None):
    return lax.dot_general(a, b, dims, precision=precision, preferred_element_type=F32)


def ones_where(mask, dtype=BF16):
    return jnp.where(mask, 1.0, 0.0).astype(dtype)


def exchange(first, last, axis):
    peers = lax.axis_size(axis)
    up = [(i, i + 1) for i in range(peers - 1)]
    down = [(j, i) for i, j in up]
    return lax.ppermute(last, axis, up), lax.ppermute(first, axis, down)


VMEM = pl.BlockSpec(memory_space=pltpu.VMEM)
SMEM = pl.BlockSpec(memory_space=pltpu.SMEM)
ANY = pl.BlockSpec(memory_space=pl.ANY)


def whole(shape):
    return pl.BlockSpec(shape, lambda i: (0,) * len(shape))


def up_to(n, multiple):
    return -(-n // multiple) * multiple


class Sizes:
    def __init__(self, lines_l, map_lines, n_model):
        self.devices = lax.axis_size(AXES)
        self.swath = lax.axis_size("swath")
        self.lines = (lines_l, map_lines)
        self.map_lines = map_lines
        self.n_model = n_model
        self.caps = tuple(max(2, 2 * lines // self.devices) for lines in self.lines)
        self.starts = (0, COMPS * self.caps[0])
        self.rows = up_to(COMPS * sum(self.caps), SUB)
        self.stride = up_to(self.rows + SUB, LANES)
        self.lanes = up_to(self.rows, LANES)
        self.part = 64 if lines_l % 64 == 0 and map_lines % 64 == 0 else 2


def first_kernel(z, radar_l, radar_s, first, last):
    shape = (2 * SUB, COMPS * LANES)
    row, at = iota(shape, 0), iota(shape, 1)
    pick = ones_where(at == jnp.where(row < SUB, row * LANES, (row - SUB) * LANES + LANES - 1))
    start = 0
    for radar, lines in ((radar_l, z.lines[0]), (radar_s, z.lines[1])):
        rows = jnp.concatenate([radar[c] for c in range(COMPS)], axis=1)
        both = dot(pick, rows, NT)
        first[:, start : start + lines] = both[0:SUB].astype(BF16)
        last[:, start : start + lines] = both[SUB:].astype(BF16)
        start += lines


def plan_kernel(z, owner_l, slot_l, owner_s, slot_s, base_l, base_s, marks):
    total = jnp.zeros((z.devices, LANES), F32)
    shift = 0
    for band, (owner, slot, base) in enumerate(((owner_l, slot_l, base_l), (owner_s, slot_s, base_s))):
        tiles = z.lines[band]
        hit = iota((z.devices, tiles), 0) == owner[...]
        earlier = ones_where(iota((tiles, tiles), 0) < iota((tiles, tiles), 1))
        before = dot(ones_where(hit), earlier, NN)
        rank = jnp.sum(jnp.where(hit, before, 0.0), axis=0, keepdims=True).astype(jnp.int32)
        base[...] = owner[...] * z.stride + z.starts[band] + rank
        line = jnp.where(hit, slot[...] + 1, 0).astype(F32).astype(BF16)
        place = ones_where(iota((LANES, tiles), 0) == rank + shift)
        total = total + dot(line, place, NT)
        shift += z.caps[band]
    me, other = iota((z.devices, z.devices), 0), iota((z.devices, z.devices), 1)
    inner = me % z.swath
    own = total.astype(BF16)
    before = dot(ones_where((other == me - 1) & (inner > 0)), own, NN)
    after = dot(ones_where((other == me + 1) & (inner < z.swath - 1)), own, NN)
    marks[...] = total + pltpu.roll(before, shift, 1) + pltpu.roll(after, 2 * shift, 1)


def second_kernel(z, top_l, top_s, bottom_l, bottom_s, before, after, first, last):
    lines_l, lines_s = z.lines
    ends = (
        (first, top_l, top_s, 0, 0, lines_l),
        (last, bottom_l, bottom_s, top_l.shape[1] - 1, lines_l - 1, lines_l + lines_s - 1),
    )
    for out, rows_l, rows_s, row, at_l, at_s in ends:
        parts = [rows_l[...].astype(F32)[:, row, :], rows_s[...].astype(F32)[:, row, :]]
        for side in (before, after):
            for at in (at_l, at_s):
                tile = at // LANES * LANES
                column = side[:, tile : tile + LANES].astype(F32)[0:COMPS, at - tile : at - tile + 1]
                parts.append(jnp.broadcast_to(column, (COMPS, LANES)))
        parts.append(jnp.zeros((out.shape[0] - 6 * COMPS, LANES), F32))
        out[...] = jnp.concatenate(parts, axis=0).astype(BF16)


def with_sides(x, left, right):
    lane = iota(x.shape, 1)
    width = x.shape[1]
    before = jnp.where(lane == 0, left, pltpu.roll(x, 1, 1))
    after = jnp.where(lane == width - 1, right, pltpu.roll(x, width - 1, 1))
    return before, after


def filter_band(tiles, radar, left, right, work, filtered):
    inner = pl.ds(SUB, tiles)
    blank = jnp.zeros((1, LANES), F32)
    for plane in range(3):
        work[plane, SUB - 1 : SUB, :] = blank
        work[plane, SUB + tiles : SUB + tiles + 1, :] = blank
    body = [radar[c].astype(F32) for c in range(COMPS)]
    lefts = [left[:, c : c + 1] for c in range(COMPS)]
    rights = [right[:, c : c + 1] for c in range(COMPS)]
    squares = lambda values: sum(v * v for v in values)
    power = squares(body)
    for plane, value in enumerate((power,) + with_sides(power, squares(lefts), squares(rights))):
        work[plane, inner, :] = value
    near = [work[plane, pl.ds(SUB + d, tiles), :] for plane in range(3) for d in (-1, 0, 1)]
    gain = gain_of(near)
    for c in range(COMPS):
        plane = c % 3
        before, after = with_sides(body[c], lefts[c], rights[c])
        work[plane, inner, :] = body[c] + before + after
        mean = work[plane, pl.ds(SUB - 1, tiles), :] + work[plane, inner, :]
        mean = (mean + work[plane, pl.ds(SUB + 1, tiles), :]) / 9.0
        filtered[pl.ds(c, tiles, stride=SUB), :] = mean + gain * (body[c] - mean)


def gain_of(near):
    mean_power = sum(near[1:], near[0]) / 9.0
    spread = jnp.zeros_like(mean_power)
    for q in near:
        spread = spread + (q - mean_power) ** 2
    spread = spread / 9.0
    return spread / (spread + cu_square * mean_power * mean_power + 1.0)


def send_kernel(
    z, base_l, base_s, radar_l, radar_s, before, after, weights_l, weights_s,
    packed, edge_lines, edge_tiles, work, filtered, held_l, held_s, arrived,
):
    chunks, count = [], 0
    for source, held, lines in ((weights_l, held_l, z.lines[0]), (weights_s, held_s, z.lines[1])):
        copies = []
        for at in range(0, lines, z.part):
            part = pl.ds(at, z.part)
            copies.append(pltpu.make_async_copy(source.at[part], held.at[part], arrived.at[count]))
            copies[-1].start()
            count += 1
        chunks.append(copies)
    packed[...] = jnp.zeros_like(packed)
    tall = edge_lines.shape[3]
    for band, radar in enumerate((radar_l, radar_s)):
        edge_lines[band, 0] = radar[:, 0:tall, :]
        edge_lines[band, 1] = radar[:, z.lines[band] - tall :, :]
    left, right = before[...].astype(F32).T, after[...].astype(F32).T
    at = 0
    for band, (radar, base, held) in enumerate(((radar_l, base_l, held_l), (radar_s, base_s, held_s))):
        tiles, capacity = z.lines[band], z.caps[band]
        filter_band(tiles, radar, left[at : at + tiles], right[at : at + tiles], work, filtered)
        at += tiles
        for i, copy in enumerate(chunks[band]):
            copy.wait()
            for t in range(0, z.part, 2):
                tile = i * z.part + t
                lines = filtered[pl.ds(tile * SUB, 2 * SUB), :].astype(BF16)
                matrix = held[pl.ds(tile, 2)].reshape(2 * LANES, LANES)
                result = dot(lines, matrix, NT)
                first, second = base[0, tile], base[0, tile + 1]
                packed[pl.ds(first, COMPS, stride=capacity), :] = result[0:COMPS, 0:LANES]
                packed[pl.ds(second, COMPS, stride=capacity), :] = result[SUB : SUB + COMPS, LANES:]
        edge_tiles[band, 0] = held[0]
        edge_tiles[band, 1] = held[tiles - 1]


def tail_kernel(
    z, base_l, base_s, given, above, below, before, after, marks,
    lines_held, tiles_held, out, packed,
):
    del given
    tall = lines_held.shape[3]
    up, down = above[...].astype(F32), below[...].astype(F32)
    shift = 0
    for band, base in enumerate((base_l, base_s)):
        lines = z.lines[band]
        for end in range(2):
            rows = lines_held[band, end].astype(F32)
            strip = (up, down)[end]
            first = 0 if end == 0 else lines - 2
            near_row = 0 if end == 0 else tall - 2
            tile = (shift + first) // LANES * LANES
            columns = [side[:, tile : tile + LANES].astype(F32) for side in (before, after)]
            values, sides = [], [[], []]
            for c in range(COMPS):
                row = band * COMPS + c
                far = strip[row : row + 1]
                near = rows[c, near_row : near_row + 2]
                values.append(jnp.concatenate([far, near] if end == 0 else [near, far], axis=0))
                for side in range(2):
                    corner = 2 * COMPS * (1 + side) + row
                    far = strip[corner : corner + 1, 0:1]
                    near = [
                        columns[side][c : c + 1, shift + first - tile + k : shift + first - tile + k + 1]
                        for k in range(2)
                    ]
                    sides[side].append(jnp.concatenate([far] + near if end == 0 else near + [far], axis=0))
            squares = lambda parts: sum(v * v for v in parts)
            power = squares(values)
            planes = (power,) + with_sides(power, squares(sides[0]), squares(sides[1]))
            gain = gain_of([plane[k : k + 1] for plane in planes for k in range(3)])
            lines_out = []
            for c in range(COMPS):
                left, right = with_sides(values[c], sides[0][c], sides[1][c])
                total = values[c] + left + right
                mean = (total[0:1] + total[1:2] + total[2:3]) / 9.0
                lines_out.append(mean + gain * (values[c][1:2] - mean))
            lines_out.append(jnp.zeros((SUB - COMPS, LANES), F32))
            result = dot(jnp.concatenate(lines_out, axis=0).astype(BF16), tiles_held[band, end], NT)
            target = base[0, 0 if end == 0 else lines - 1]
            packed[pl.ds(target, COMPS, stride=z.caps[band]), :] = result[0:COMPS]
        shift += lines

    steps = z.lanes // LANES
    row, lane = iota((SUB, LANES), 0), iota((SUB, LANES), 1)
    pick = ones_where(
        ((row >= 1) & (row <= steps) & (lane == LANES - 1)) | ((row > steps) & (row <= 2 * steps) & (lane == 0))
    )
    columns = [
        dot(pick, packed[o * z.stride : o * z.stride + z.lanes, :].astype(BF16), NT) for o in range(z.devices)
    ]
    for o in range(z.devices):
        extra = jnp.broadcast_to(marks[o : o + 1, :], (SUB, LANES))
        one_less, one_more = max(o - 1, 0), min(o + 1, z.devices - 1)
        for k in range(steps):
            part = slice(k * LANES, (k + 1) * LANES)
            extra = jnp.where(row == 1 + k, columns[one_less][:, part], extra)
            extra = jnp.where(row == 1 + steps + k, columns[one_more][:, part], extra)
        out[o, 0 : z.rows, :] = packed[o * z.stride : o * z.stride + z.rows, :].astype(BF16)
        out[o, z.rows :, :] = extra.astype(BF16)


def matrix_kernel(models, small, wide):
    m = models[...]
    n_model = m.shape[0]
    eye = ones_where(iota((CHANNELS, CHANNELS), 0) == iota((CHANNELS, CHANNELS), 1), F32)
    powers = jnp.zeros(m.shape, F32)
    for _ in range(FIT_ITERS):
        predicted = dot(m, powers, TN, HI)
        powers = powers + fit_rate * dot(m, eye - predicted, NN, HI)
    powers = powers / 9.0
    small[...] = powers
    rows, columns = wide.shape[0] // 2, wide.shape[1]
    left = ones_where(iota((rows, n_model), 0) // SUB == iota((rows, n_model), 1), F32)
    right = ones_where(iota((CHANNELS, columns), 1) // SUB == iota((CHANNELS, columns), 0), F32)
    spread = dot(dot(left, powers, NN, HI), right, NN, HI)
    same = iota((rows, columns), 0) % SUB == iota((rows, columns), 1) % SUB
    spread = jnp.where(same, spread, 0.0)
    high = spread.astype(BF16)
    low = (spread - high.astype(F32)).astype(BF16)
    wide[...] = jnp.concatenate([high, low], axis=0)


def coherency(real, imag):
    joint = [real[f] * real[g] + imag[f] * imag[g] for f, g in upper_pairs]
    return joint + [imag[f] * real[g] - real[f] * imag[g] for f, g in strict_pairs]


def split_parts(maps):
    pick = lambda at: [maps(band * COMPS + at + c) for band in range(2) for c in range(3)]
    return pick(0), pick(3)


def merge_kernel(z, got, small, wide, out, rim_first, rim_last, stage, extras, maps, fits):
    map_lines, n_model, devices = z.map_lines, z.n_model, z.devices
    steps = z.lanes // LANES
    for s in range(devices):
        extras[s * SUB : (s + 1) * SUB, :] = got[s, z.rows : z.rows + SUB, :].astype(F32)
    piece = lambda r: extras[pl.ds(r, devices, stride=SUB), :]
    marks = piece(0)
    sides = [
        jnp.concatenate([piece(1 + side * steps + k) for k in range(steps)], axis=1) for side in range(2)
    ]
    shift = sum(z.caps)
    edges = [[None] * (2 * COMPS) for _ in range(2)]
    at_mark = 0
    for band in range(2):
        capacity = z.caps[band]
        places = devices * capacity
        for s in range(devices):
            block = got[s, 0 : z.rows, :].astype(F32)
            for c in range(COMPS):
                low = z.starts[band] + c * capacity
                stage[s * capacity : (s + 1) * capacity, c * LANES : (c + 1) * LANES] = block[
                    low : low + capacity, :
                ]
        turned = lambda x, by: pltpu.roll(x, (x.shape[1] - by) % x.shape[1], 1)[:, 0:LANES]
        rows = [turned(marks, at_mark + k * shift) for k in range(3)]
        for side in range(2):
            rows += [turned(sides[side], z.starts[band] + c * capacity) for c in range(COMPS)]
        at_mark += capacity
        place = iota((devices, places), 1)
        low = iota((devices, places), 0) * capacity
        mine = (place >= low) & (place < low + capacity)
        offset = jnp.sum(jnp.where(mine, place - low, 0), axis=0, keepdims=True)
        pick = ones_where(iota((LANES, places), 0) == offset)
        spread = dot(jnp.concatenate(rows, axis=0).astype(BF16), pick, NN)
        flat = [
            jnp.sum(jnp.where(mine, spread[k * devices : (k + 1) * devices], 0.0), axis=0, keepdims=True)
            for k in range(len(rows))
        ]
        lines = iota((map_lines, places), 0) + 1
        tables = [ones_where(lines == flat[k].astype(jnp.int32)) for k in range(3)]
        summed = dot(tables[0], stage[0:places, :].astype(BF16), NN)
        for c in range(COMPS):
            maps[band * COMPS + c] = summed[:, c * LANES : (c + 1) * LANES]
        for side in range(2):
            values = flat[3 + side * COMPS : 3 + (side + 1) * COMPS]
            values = jnp.concatenate(values + [jnp.zeros((SUB - COMPS, places), F32)], axis=0).astype(BF16)
            column = dot(values, tables[1 + side], NT)
            for c in range(COMPS):
                edges[side][band * COMPS + c] = column[c : c + 1, :]
    turned = []
    for side in range(2):
        joint = jnp.concatenate(coherency(*split_parts(lambda i: edges[side][i])), axis=0)
        turned.append(dot(small[...], joint, NN, HI))
    x = jnp.concatenate(turned, axis=0)
    high = x.astype(BF16)
    x = jnp.concatenate([high, (x - high.astype(F32)).astype(BF16)], axis=0)
    at = iota((4 * n_model, n_model * LANES), 0) % (2 * n_model)
    to = iota((4 * n_model, n_model * LANES), 1)
    target = jnp.where(at < n_model, at * LANES + LANES - 1, (at - n_model) * LANES)
    planes = dot(x, ones_where(to == target), TN)

    matrix = wide[...]

    def step(i, _):
        halves = []
        for h in range(2):
            r = pl.multiple_of((2 * i + h) * SUB, SUB)
            x = jnp.concatenate(coherency(*split_parts(lambda n: maps[n, pl.ds(r, SUB), :])), axis=0)
            halves.append(x.astype(BF16))
        result = dot(matrix, jnp.concatenate(halves, axis=1), NN)
        result = result[0 : n_model * SUB] + result[n_model * SUB :]
        for h in range(2):
            r = pl.multiple_of((2 * i + h) * SUB, SUB)
            for k in range(n_model):
                fits[k, pl.ds(SUB + r, SUB), :] = result[
                    k * SUB : (k + 1) * SUB, h * LANES : (h + 1) * LANES
                ]
        return _

    lax.fori_loop(0, map_lines // (2 * SUB), step, 0, unroll=True)
    blank = jnp.zeros((1, LANES), F32)
    inner = pl.ds(SUB, map_lines)
    for k in range(n_model):
        x = fits[k, inner, :]
        side = planes[:, k * LANES : (k + 1) * LANES]
        lane = iota(x.shape, 1)
        before = pltpu.roll(jnp.where(lane == LANES - 1, side, x), 1, 1)
        after = pltpu.roll(jnp.where(lane == 0, side, x), LANES - 1, 1)
        x = x + before + after
        fits[k, inner, :] = x
        fits[k, SUB - 1 : SUB, :] = blank
        fits[k, SUB + map_lines : SUB + map_lines + 1, :] = blank
        rim_first[k : k + 1, :] = x[0:1, :]
        rim_last[k : k + 1, :] = x[map_lines - 1 :, :]
        out[k] = fits[k, pl.ds(SUB - 1, map_lines), :] + x + fits[k, pl.ds(SUB + 1, map_lines), :]


def finish_kernel(fit, above, below, out):
    end = pl.program_id(0)
    line = iota(fit.shape[1:], 0)
    height = fit.shape[1]
    for k in range(fit.shape[0]):
        upper = jnp.where((line == 0) & (end == 0), above[k : k + 1, :], 0.0)
        lower = jnp.where((line == height - 1) & (end == 1), below[k : k + 1, :], 0.0)
        out[k] = fit[k] + upper + lower


def body(radar_l, radar_s, weights_l, weights_s, owner_l, owner_s, slot_l, slot_s, models):
    z = Sizes(radar_l.shape[1], radar_s.shape[1], models.shape[0])
    lines_l, lines_s = z.lines
    shape = jax.ShapeDtypeStruct

    def call(kernel, args, shapes, mib, scratch=(), specs=None, flops=0, size=0):
        return pl.pallas_call(
            lambda *refs: kernel(z, *refs) if kernel is not matrix_kernel else kernel(*refs),
            in_specs=specs or [VMEM] * len(args),
            out_specs=[VMEM] * len(shapes),
            out_shape=shapes,
            scratch_shapes=scratch,
            compiler_params=params(mib),
            cost_estimate=pl.CostEstimate(flops=flops, bytes_accessed=size, transcendentals=0),
        )(*args)

    def call_one(kernel, args, specs, shapes, mib, scratch=(), aliases={}, flops=0, size=0):
        return pl.pallas_call(
            lambda *refs: kernel(z, *refs),
            grid=(1,),
            in_specs=specs,
            out_specs=[whole(x.shape) for x in shapes],
            out_shape=shapes,
            scratch_shapes=scratch,
            input_output_aliases=aliases,
            compiler_params=params(mib),
            cost_estimate=pl.CostEstimate(flops=flops, bytes_accessed=size, transcendentals=0),
        )(*args)

    row = lambda x: x.reshape(1, -1)
    radar = (radar_l, radar_s)
    column = shape((SUB, lines_l + lines_s), BF16)
    first, last = call_one(
        first_kernel, radar, [whole(x.shape) for x in radar], [column, column], 60,
        flops=10_000_000, size=1_000_000,
    )
    before, after = exchange(first, last, "swath")
    owners = (row(owner_l), row(slot_l), row(owner_s), row(slot_s))
    base_l, base_s, marks = call_one(
        plan_kernel,
        owners,
        [whole(x.shape) for x in owners],
        [shape((1, lines_l), jnp.int32), shape((1, lines_s), jnp.int32), shape((z.devices, LANES), F32)],
        16, flops=1_000_000_000, size=1_000_000,
    )
    strip = shape((5 * SUB, LANES), BF16)
    tall = 2 * SUB
    edge = lambda lines, end: pl.BlockSpec(
        (COMPS, tall, LANES), lambda i: (0, end * (lines // tall - 1), 0)
    )
    edges = [edge(lines, end) for end in range(2) for lines in z.lines]
    side = whole(column.shape)
    first, last = call_one(
        second_kernel, radar * 2 + (before, after), edges + [side, side], [strip, strip], 32,
    )
    above, below = exchange(first, last, "sec")
    smem = lambda x: pl.BlockSpec(x.shape, lambda i: (0, 0), memory_space=pltpu.SMEM)
    bases = [smem(base_l), smem(base_s)]
    buffer = shape((z.devices * z.stride + up_to(COMPS * max(z.caps), SUB), LANES), F32)
    packed, edge_lines, edge_tiles = call(
        send_kernel,
        (base_l, base_s, radar_l, radar_s, before, after, weights_l, weights_s),
        [
            buffer,
            shape((2, 2, COMPS, tall, LANES), BF16),
            shape((2, 2, LANES, LANES), BF16),
        ],
        44,
        specs=[SMEM, SMEM] + [VMEM] * 4 + [ANY] * 2,
        scratch=[
            pltpu.VMEM((3, max(z.lines) + 2 * SUB, LANES), F32),
            pltpu.VMEM((max(z.lines) * SUB, LANES), F32),
            pltpu.VMEM(weights_l.shape, BF16),
            pltpu.VMEM(weights_s.shape, BF16),
            pltpu.SemaphoreType.DMA((sum(z.lines) // z.part,)),
        ],
        flops=10_000_000_000,
        size=2 * (weights_l.size + weights_s.size),
    )
    args = (base_l, base_s, packed, above, below, before, after, marks, edge_lines, edge_tiles)
    sent, _ = pl.pallas_call(
        lambda *refs: tail_kernel(z, *refs),
        in_specs=[SMEM, SMEM] + [VMEM] * 8,
        out_specs=[VMEM, VMEM],
        out_shape=[shape((z.devices, z.rows + SUB, LANES), BF16), buffer],
        input_output_aliases={2: 1},
        compiler_params=params(24),
    )(*args)
    got = lax.all_to_all(sent, AXES, split_axis=0, concat_axis=0, tiled=True)

    small, wide = call(
        matrix_kernel,
        (models,),
        [shape((z.n_model, CHANNELS), F32), shape((2 * z.n_model * SUB, CHANNELS * SUB), BF16)],
        16, flops=50_000_000, size=1_000_000,
    )
    rim = shape((z.n_model, LANES), F32)
    fit, rim_first, rim_last = call(
        merge_kernel,
        (got, small, wide),
        [shape((z.n_model, z.map_lines, LANES), F32), rim, rim],
        32,
        scratch=[
            pltpu.VMEM((z.devices * max(z.caps), COMPS * LANES), F32),
            pltpu.VMEM((z.devices * SUB, LANES), F32),
            pltpu.VMEM((2 * COMPS, z.map_lines, LANES), F32),
            pltpu.VMEM((z.n_model, z.map_lines + 2 * SUB, LANES), F32),
        ],
        flops=1_000_000_000,
        size=4_000_000,
    )
    above, below = exchange(rim_first, rim_last, "sec")
    ends = pl.BlockSpec((z.n_model, SUB, LANES), lambda i: (0, i * (z.map_lines // SUB - 1), 0))
    edge = pl.BlockSpec((z.n_model, LANES), lambda i: (0, 0))
    return pl.pallas_call(
        finish_kernel,
        grid=(2,),
        in_specs=[ends, edge, edge],
        out_specs=ends,
        out_shape=shape(fit.shape, F32),
        input_output_aliases={0: 0},
        compiler_params=params(16),
    )(fit, above, below)


def solution(mesh):
    in_specs = (
        P(None, "sec", "swath"),
        P(None, "sec", "swath"),
        P(("sec", "swath"), None, None),
        P(("sec", "swath"), None, None),
        P(("sec", "swath"), None),
        P(("sec", "swath"), None),
        P(("sec", "swath")),
        P(("sec", "swath")),
        P(),
    )
    out_specs = P(None, "sec", "swath")
    return jax.shard_map(body, mesh=mesh, in_specs=in_specs, out_specs=out_specs, check_vma=False)
```

```python
import jax
import jax.numpy as jnp
from jax import lax
from jax.experimental import pallas as pl
from jax.experimental.pallas import tpu as pltpu
from jax.sharding import PartitionSpec as P

FIT_ITERS = 4
AXES = ("sec", "swath")

cu_square = 0.25
fit_rate = 0.25
upper_pairs = [(first, second) for first in range(6) for second in range(first, 6)]
strict_pairs = [(first, second) for first in range(6) for second in range(first + 1, 6)]
CHANNELS = len(upper_pairs) + len(strict_pairs)
COMPS = 6
NT = (((1,), (1,)), ((), ()))
NN = (((1,), (0,)), ((), ()))
TN = (((0,), (0,)), ((), ()))
HI = lax.Precision.HIGHEST
F32 = jnp.float32
BF16 = jnp.bfloat16
SUB = 8
LANES = 128
EXTRA = 5


def params(mib):
    return pltpu.CompilerParams(vmem_limit_bytes=mib << 20)


def iota(shape, dim):
    return lax.broadcasted_iota(jnp.int32, shape, dim)


def dot(a, b, dims, precision=None):
    return lax.dot_general(a, b, dims, precision=precision, preferred_element_type=F32)


def ones_where(mask, dtype=BF16):
    return jnp.where(mask, 1.0, 0.0).astype(dtype)


def swap(even_pairs, odd_pairs, axis):
    peers = lax.axis_size(axis)
    pairs = lambda start: [p for i in range(start, peers - 1, 2) for p in ((i, i + 1), (i + 1, i))]
    return lax.ppermute(even_pairs, axis, pairs(0)), lax.ppermute(odd_pairs, axis, pairs(1))


def by_parity(axis, one, other):
    even = lax.axis_index(axis) % 2 == 0
    return jnp.where(even, one, other), jnp.where(even, other, one)


VMEM = pl.BlockSpec(memory_space=pltpu.VMEM)
SMEM = pl.BlockSpec(memory_space=pltpu.SMEM)
ANY = pl.BlockSpec(memory_space=pl.ANY)


def whole(shape):
    return pl.BlockSpec(shape, lambda i: (0,) * len(shape))


def up_to(n, multiple):
    return -(-n // multiple) * multiple


class Sizes:
    def __init__(self, lines_l, map_lines, n_model):
        self.devices = lax.axis_size(AXES)
        self.swath = lax.axis_size("swath")
        self.lines = (lines_l, map_lines)
        self.map_lines = map_lines
        self.n_model = n_model
        self.caps = tuple(max(2, 2 * lines // self.devices) for lines in self.lines)
        self.starts = (0, COMPS * self.caps[0])
        self.rows = up_to(COMPS * sum(self.caps), SUB)
        self.stride = up_to(self.rows + SUB, LANES)
        self.lanes = up_to(self.rows, LANES)
        self.part = 64 if lines_l % 64 == 0 and map_lines % 64 == 0 else 2


def first_kernel(
    z, radar_l, radar_s, owner_l, slot_l, owner_s, slot_s, even_pairs, odd_pairs, base_l, base_s, marks
):
    plan(z, owner_l, slot_l, owner_s, slot_s, base_l, base_s, marks)
    shape = (2 * SUB, COMPS * LANES)
    row, at = iota(shape, 0), iota(shape, 1)
    pick = ones_where(at == jnp.where(row < SUB, row * LANES, (row - SUB) * LANES + LANES - 1))
    start = 0
    for radar, lines in ((radar_l, z.lines[0]), (radar_s, z.lines[1])):
        rows = jnp.concatenate([radar[c] for c in range(COMPS)], axis=1)
        both = dot(pick, rows, NT)
        one, other = by_parity("swath", both[SUB:], both[0:SUB])
        even_pairs[:, start : start + lines] = one.astype(BF16)
        odd_pairs[:, start : start + lines] = other.astype(BF16)
        start += lines


def plan(z, owner_l, slot_l, owner_s, slot_s, base_l, base_s, marks):
    total = jnp.zeros((z.devices, LANES), F32)
    shift = 0
    for band, (owner, slot, base) in enumerate(((owner_l, slot_l, base_l), (owner_s, slot_s, base_s))):
        tiles = z.lines[band]
        hit = iota((z.devices, tiles), 0) == owner[...]
        earlier = ones_where(iota((tiles, tiles), 0) < iota((tiles, tiles), 1))
        before = dot(ones_where(hit), earlier, NN)
        rank = jnp.sum(jnp.where(hit, before, 0.0), axis=0, keepdims=True).astype(jnp.int32)
        base[...] = owner[...] * z.stride + z.starts[band] + rank
        line = jnp.where(hit, slot[...].reshape(1, tiles) + 1, 0).astype(F32).astype(BF16)
        place = ones_where(iota((LANES, tiles), 0) == rank + shift)
        total = total + dot(line, place, NT)
        shift += z.caps[band]
    me, other = iota((z.devices, z.devices), 0), iota((z.devices, z.devices), 1)
    inner = me % z.swath
    own = total.astype(BF16)
    before = dot(ones_where((other == me - 1) & (inner > 0)), own, NN)
    after = dot(ones_where((other == me + 1) & (inner < z.swath - 1)), own, NN)
    marks[...] = total + pltpu.roll(before, shift, 1) + pltpu.roll(after, 2 * shift, 1)


def second_kernel(z, top_l, top_s, bottom_l, bottom_s, swap_a, swap_b, even_pairs, odd_pairs):
    after, before = by_parity("swath", swap_a[...].astype(F32), swap_b[...].astype(F32))
    strips = []
    lines_l, lines_s = z.lines
    ends = (
        (top_l, top_s, 0, 0, lines_l),
        (bottom_l, bottom_s, top_l.shape[1] - 1, lines_l - 1, lines_l + lines_s - 1),
    )
    for rows_l, rows_s, row, at_l, at_s in ends:
        parts = [rows_l[...].astype(F32)[:, row, :], rows_s[...].astype(F32)[:, row, :]]
        for side in (before, after):
            for at in (at_l, at_s):
                column = side[0:COMPS, at : at + 1]
                parts.append(jnp.broadcast_to(column, (COMPS, LANES)))
        parts.append(jnp.zeros((even_pairs.shape[0] - 6 * COMPS, LANES), F32))
        strips.append(jnp.concatenate(parts, axis=0))
    one, other = by_parity("sec", strips[1], strips[0])
    even_pairs[...] = one.astype(BF16)
    odd_pairs[...] = other.astype(BF16)


def with_sides(x, left, right):
    lane = iota(x.shape, 1)
    width = x.shape[1]
    before = jnp.where(lane == 0, left, pltpu.roll(x, 1, 1))
    after = jnp.where(lane == width - 1, right, pltpu.roll(x, width - 1, 1))
    return before, after


def filter_band(tiles, radar, left, right, work, filtered):
    inner = pl.ds(SUB, tiles)
    blank = jnp.zeros((1, LANES), F32)
    for plane in range(3):
        work[plane, SUB - 1 : SUB, :] = blank
        work[plane, SUB + tiles : SUB + tiles + 1, :] = blank
    body = [radar[c].astype(F32) for c in range(COMPS)]
    lefts = [left[:, c : c + 1] for c in range(COMPS)]
    rights = [right[:, c : c + 1] for c in range(COMPS)]
    squares = lambda values: sum(v * v for v in values)
    power = squares(body)
    for plane, value in enumerate((power,) + with_sides(power, squares(lefts), squares(rights))):
        work[plane, inner, :] = value
    near = [work[plane, pl.ds(SUB + d, tiles), :] for plane in range(3) for d in (-1, 0, 1)]
    gain = gain_of(near)
    for c in range(COMPS):
        plane = c % 3
        before, after = with_sides(body[c], lefts[c], rights[c])
        work[plane, inner, :] = body[c] + before + after
        mean = work[plane, pl.ds(SUB - 1, tiles), :] + work[plane, inner, :]
        mean = (mean + work[plane, pl.ds(SUB + 1, tiles), :]) / 9.0
        filtered[pl.ds(c, tiles, stride=SUB), :] = mean + gain * (body[c] - mean)


def gain_of(near):
    mean_power = sum(near[1:], near[0]) / 9.0
    spread = jnp.zeros_like(mean_power)
    for q in near:
        spread = spread + (q - mean_power) ** 2
    spread = spread / 9.0
    return spread / (spread + cu_square * mean_power * mean_power + 1.0)


def send_kernel(
    z, base_l, base_s, radar_l, radar_s, swap_a, swap_b, weights_l, weights_s,
    packed, edge_lines, edge_tiles, work, filtered, held_l, held_s, arrived,
):
    chunks, count = [], 0
    for source, held, lines in ((weights_l, held_l, z.lines[0]), (weights_s, held_s, z.lines[1])):
        copies = []
        for at in range(0, lines, z.part):
            part = pl.ds(at, z.part)
            copies.append(pltpu.make_async_copy(source.at[part], held.at[part], arrived.at[count]))
            copies[-1].start()
            count += 1
        chunks.append(copies)
    packed[...] = jnp.zeros_like(packed)
    tall = edge_lines.shape[3]
    for band, radar in enumerate((radar_l, radar_s)):
        edge_lines[band, 0] = radar[:, 0:tall, :]
        edge_lines[band, 1] = radar[:, z.lines[band] - tall :, :]
    after, before = by_parity("swath", swap_a[...].astype(F32), swap_b[...].astype(F32))
    left, right = before.T, after.T
    at = 0
    for band, (radar, base, held) in enumerate(((radar_l, base_l, held_l), (radar_s, base_s, held_s))):
        tiles, capacity = z.lines[band], z.caps[band]
        filter_band(tiles, radar, left[at : at + tiles], right[at : at + tiles], work, filtered)
        at += tiles
        for i, copy in enumerate(chunks[band]):
            copy.wait()
            for t in range(0, z.part, 2):
                tile = i * z.part + t
                lines = filtered[pl.ds(tile * SUB, 2 * SUB), :].astype(BF16)
                matrix = held[pl.ds(tile, 2)].reshape(2 * LANES, LANES)
                result = dot(lines, matrix, NT)
                first, second = base[0, tile], base[0, tile + 1]
                packed[pl.ds(first, COMPS, stride=capacity), :] = result[0:COMPS, 0:LANES]
                packed[pl.ds(second, COMPS, stride=capacity), :] = result[SUB : SUB + COMPS, LANES:]
        edge_tiles[band, 0] = held[0]
        edge_tiles[band, 1] = held[tiles - 1]


def tail_kernel(
    z, base_l, base_s, given, sec_a, sec_b, swap_a, swap_b, marks,
    lines_held, tiles_held, out, packed,
):
    del given
    tall = lines_held.shape[3]
    after, before = by_parity("swath", swap_a[...].astype(F32), swap_b[...].astype(F32))
    down, up = by_parity("sec", sec_a[...].astype(F32), sec_b[...].astype(F32))
    shift = 0
    for band, base in enumerate((base_l, base_s)):
        lines = z.lines[band]
        for end in range(2):
            rows = lines_held[band, end].astype(F32)
            strip = (up, down)[end]
            first = 0 if end == 0 else lines - 2
            near_row = 0 if end == 0 else tall - 2
            columns = (before, after)
            values, sides = [], [[], []]
            for c in range(COMPS):
                row = band * COMPS + c
                far = strip[row : row + 1]
                near = rows[c, near_row : near_row + 2]
                values.append(jnp.concatenate([far, near] if end == 0 else [near, far], axis=0))
                for side in range(2):
                    corner = 2 * COMPS * (1 + side) + row
                    far = strip[corner : corner + 1, 0:1]
                    near = [
                        columns[side][c : c + 1, shift + first + k : shift + first + k + 1]
                        for k in range(2)
                    ]
                    sides[side].append(jnp.concatenate([far] + near if end == 0 else near + [far], axis=0))
            squares = lambda parts: sum(v * v for v in parts)
            power = squares(values)
            planes = (power,) + with_sides(power, squares(sides[0]), squares(sides[1]))
            gain = gain_of([plane[k : k + 1] for plane in planes for k in range(3)])
            lines_out = []
            for c in range(COMPS):
                left, right = with_sides(values[c], sides[0][c], sides[1][c])
                total = values[c] + left + right
                mean = (total[0:1] + total[1:2] + total[2:3]) / 9.0
                lines_out.append(mean + gain * (values[c][1:2] - mean))
            lines_out.append(jnp.zeros((SUB - COMPS, LANES), F32))
            result = dot(jnp.concatenate(lines_out, axis=0).astype(BF16), tiles_held[band, end], NT)
            target = base[0, 0 if end == 0 else lines - 1]
            packed[pl.ds(target, COMPS, stride=z.caps[band]), :] = result[0:COMPS]
        shift += lines

    steps = z.lanes // LANES
    row, lane = iota((SUB, LANES), 0), iota((SUB, LANES), 1)
    pick = ones_where(
        ((row >= 1) & (row <= steps) & (lane == LANES - 1)) | ((row > steps) & (row <= 2 * steps) & (lane == 0))
    )
    columns = [
        dot(pick, packed[o * z.stride : o * z.stride + z.lanes, :].astype(BF16), NT) for o in range(z.devices)
    ]
    for o in range(z.devices):
        extra = jnp.broadcast_to(marks[o : o + 1, :], (SUB, LANES))
        one_less, one_more = max(o - 1, 0), min(o + 1, z.devices - 1)
        for k in range(steps):
            part = slice(k * LANES, (k + 1) * LANES)
            extra = jnp.where(row == 1 + k, columns[one_less][:, part], extra)
            extra = jnp.where(row == 1 + steps + k, columns[one_more][:, part], extra)
        out[o, 0 : z.rows, :] = packed[o * z.stride : o * z.stride + z.rows, :].astype(BF16)
        out[o, z.rows :, :] = extra.astype(BF16)


def matrix_kernel(models, small, wide):
    m = models[...]
    n_model = m.shape[0]
    eye = ones_where(iota((CHANNELS, CHANNELS), 0) == iota((CHANNELS, CHANNELS), 1), F32)
    powers = jnp.zeros(m.shape, F32)
    for _ in range(FIT_ITERS):
        predicted = dot(m, powers, TN, HI)
        powers = powers + fit_rate * dot(m, eye - predicted, NN, HI)
    powers = powers / 9.0
    small[...] = powers
    rows, columns = wide.shape[0] // 2, wide.shape[1]
    left = ones_where(iota((rows, n_model), 0) // SUB == iota((rows, n_model), 1), F32)
    right = ones_where(iota((CHANNELS, columns), 1) // SUB == iota((CHANNELS, columns), 0), F32)
    spread = dot(dot(left, powers, NN, HI), right, NN, HI)
    same = iota((rows, columns), 0) % SUB == iota((rows, columns), 1) % SUB
    spread = jnp.where(same, spread, 0.0)
    high = spread.astype(BF16)
    low = (spread - high.astype(F32)).astype(BF16)
    wide[...] = jnp.concatenate([high, low], axis=0)


def coherency(real, imag):
    joint = [real[f] * real[g] + imag[f] * imag[g] for f, g in upper_pairs]
    return joint + [imag[f] * real[g] - real[f] * imag[g] for f, g in strict_pairs]


def split_parts(maps):
    pick = lambda at: [maps(band * COMPS + at + c) for band in range(2) for c in range(3)]
    return pick(0), pick(3)


def merge_kernel(z, got, small, wide, out, even_pairs, odd_pairs, stage, extras, maps, fits):
    map_lines, n_model, devices = z.map_lines, z.n_model, z.devices
    steps = z.lanes // LANES
    for s in range(devices):
        extras[s * SUB : (s + 1) * SUB, :] = got[s, z.rows : z.rows + SUB, :].astype(F32)
    piece = lambda r: extras[pl.ds(r, devices, stride=SUB), :]
    marks = piece(0)
    sides = [
        jnp.concatenate([piece(1 + side * steps + k) for k in range(steps)], axis=1) for side in range(2)
    ]
    shift = sum(z.caps)
    edges = [[None] * (2 * COMPS) for _ in range(2)]
    at_mark = 0
    for band in range(2):
        capacity = z.caps[band]
        places = devices * capacity
        for s in range(devices):
            block = got[s, 0 : z.rows, :].astype(F32)
            for c in range(COMPS):
                low = z.starts[band] + c * capacity
                stage[s * capacity : (s + 1) * capacity, c * LANES : (c + 1) * LANES] = block[
                    low : low + capacity, :
                ]
        turned = lambda x, by: pltpu.roll(x, (x.shape[1] - by) % x.shape[1], 1)[:, 0:LANES]
        rows = [turned(marks, at_mark + k * shift) for k in range(3)]
        for side in range(2):
            rows += [turned(sides[side], z.starts[band] + c * capacity) for c in range(COMPS)]
        at_mark += capacity
        place = iota((devices, places), 1)
        low = iota((devices, places), 0) * capacity
        mine = (place >= low) & (place < low + capacity)
        offset = jnp.sum(jnp.where(mine, place - low, 0), axis=0, keepdims=True)
        pick = ones_where(iota((LANES, places), 0) == offset)
        spread = dot(jnp.concatenate(rows, axis=0).astype(BF16), pick, NN)
        flat = [
            jnp.sum(jnp.where(mine, spread[k * devices : (k + 1) * devices], 0.0), axis=0, keepdims=True)
            for k in range(len(rows))
        ]
        lines = iota((map_lines, places), 0) + 1
        tables = [ones_where(lines == flat[k].astype(jnp.int32)) for k in range(3)]
        summed = dot(tables[0], stage[0:places, :].astype(BF16), NN)
        for c in range(COMPS):
            maps[band * COMPS + c] = summed[:, c * LANES : (c + 1) * LANES]
        for side in range(2):
            values = flat[3 + side * COMPS : 3 + (side + 1) * COMPS]
            values = jnp.concatenate(values + [jnp.zeros((SUB - COMPS, places), F32)], axis=0).astype(BF16)
            column = dot(values, tables[1 + side], NT)
            for c in range(COMPS):
                edges[side][band * COMPS + c] = column[c : c + 1, :]
    turned = []
    for side in range(2):
        joint = jnp.concatenate(coherency(*split_parts(lambda i: edges[side][i])), axis=0)
        turned.append(dot(small[...], joint, NN, HI))
    x = jnp.concatenate(turned, axis=0)
    high = x.astype(BF16)
    x = jnp.concatenate([high, (x - high.astype(F32)).astype(BF16)], axis=0)
    at = iota((4 * n_model, n_model * LANES), 0) % (2 * n_model)
    to = iota((4 * n_model, n_model * LANES), 1)
    target = jnp.where(at < n_model, at * LANES + LANES - 1, (at - n_model) * LANES)
    planes = dot(x, ones_where(to == target), TN)

    matrix = wide[...]

    def step(i, _):
        halves = []
        for h in range(2):
            r = pl.multiple_of((2 * i + h) * SUB, SUB)
            x = jnp.concatenate(coherency(*split_parts(lambda n: maps[n, pl.ds(r, SUB), :])), axis=0)
            halves.append(x.astype(BF16))
        result = dot(matrix, jnp.concatenate(halves, axis=1), NN)
        result = result[0 : n_model * SUB] + result[n_model * SUB :]
        for h in range(2):
            r = pl.multiple_of((2 * i + h) * SUB, SUB)
            for k in range(n_model):
                fits[k, pl.ds(SUB + r, SUB), :] = result[
                    k * SUB : (k + 1) * SUB, h * LANES : (h + 1) * LANES
                ]
        return _

    lax.fori_loop(0, map_lines // (2 * SUB), step, 0, unroll=True)
    blank = jnp.zeros((1, LANES), F32)
    inner = pl.ds(SUB, map_lines)
    for k in range(n_model):
        x = fits[k, inner, :]
        side = planes[:, k * LANES : (k + 1) * LANES]
        lane = iota(x.shape, 1)
        before = pltpu.roll(jnp.where(lane == LANES - 1, side, x), 1, 1)
        after = pltpu.roll(jnp.where(lane == 0, side, x), LANES - 1, 1)
        x = x + before + after
        fits[k, inner, :] = x
        fits[k, SUB - 1 : SUB, :] = blank
        fits[k, SUB + map_lines : SUB + map_lines + 1, :] = blank
        one, other = by_parity("sec", x[map_lines - 1 :, :], x[0:1, :])
        even_pairs[k : k + 1, :] = one
        odd_pairs[k : k + 1, :] = other
        out[k] = fits[k, pl.ds(SUB - 1, map_lines), :] + x + fits[k, pl.ds(SUB + 1, map_lines), :]


def finish_kernel(z, given, sec_a, sec_b, out, ends, moving):
    parts = (pl.ds(0, SUB), pl.ds(z.map_lines - SUB, SUB))
    copies = [pltpu.make_async_copy(given.at[:, p, :], ends.at[k], moving.at[k]) for k, p in enumerate(parts)]
    for copy in copies:
        copy.start()
    below, above = by_parity("sec", sec_a[...], sec_b[...])
    line = iota((SUB, LANES), 0)
    for copy in copies:
        copy.wait()
    copies = [pltpu.make_async_copy(ends.at[k], out.at[:, p, :], moving.at[2 + k]) for k, p in enumerate(parts)]
    for end, (at, row) in enumerate(((0, above), (SUB - 1, below))):
        for k in range(z.n_model):
            ends[end, k] = ends[end, k] + jnp.where(line == at, row[k : k + 1, :], 0.0)
        copies[end].start()
    for copy in copies:
        copy.wait()


def body(radar_l, radar_s, weights_l, weights_s, owner_l, owner_s, slot_l, slot_s, models):
    z = Sizes(radar_l.shape[1], radar_s.shape[1], models.shape[0])
    lines_l, lines_s = z.lines
    shape = jax.ShapeDtypeStruct

    def call(kernel, args, shapes, mib, scratch=(), specs=None, flops=0, size=0):
        return pl.pallas_call(
            lambda *refs: kernel(z, *refs) if kernel is not matrix_kernel else kernel(*refs),
            in_specs=specs or [VMEM] * len(args),
            out_specs=[VMEM] * len(shapes),
            out_shape=shapes,
            scratch_shapes=scratch,
            compiler_params=params(mib),
            cost_estimate=pl.CostEstimate(flops=flops, bytes_accessed=size, transcendentals=0),
        )(*args)

    def call_one(kernel, args, specs, shapes, mib, scratch=(), aliases={}, flops=0, size=0):
        return pl.pallas_call(
            lambda *refs: kernel(z, *refs),
            grid=(1,),
            in_specs=specs,
            out_specs=[whole(x.shape) for x in shapes],
            out_shape=shapes,
            scratch_shapes=scratch,
            input_output_aliases=aliases,
            compiler_params=params(mib),
            cost_estimate=pl.CostEstimate(flops=flops, bytes_accessed=size, transcendentals=0),
        )(*args)

    row = lambda x: x.reshape(1, -1)
    radar = (radar_l, radar_s)
    column = shape((SUB, lines_l + lines_s), BF16)
    args = radar + (row(owner_l), slot_l, row(owner_s), slot_s)
    even, odd, base_l, base_s, marks = call_one(
        first_kernel,
        args,
        [whole(x.shape) for x in args],
        [column, column, shape((1, lines_l), jnp.int32), shape((1, lines_s), jnp.int32), shape((z.devices, LANES), F32)],
        58,
        flops=10_000_000_000,
        size=1_000_000,
    )
    swap_a, swap_b = swap(even, odd, "swath")
    strip = shape((5 * SUB, LANES), BF16)
    tall = 2 * SUB
    edge = lambda lines, end: pl.BlockSpec(
        (COMPS, tall, LANES), lambda i: (0, end * (lines // tall - 1), 0)
    )
    edges = [edge(lines, end) for end in range(2) for lines in z.lines]
    side = whole(column.shape)
    even, odd = call_one(
        second_kernel, radar * 2 + (swap_a, swap_b), edges + [side, side], [strip, strip], 32, flops=10_000_000_000, size=1_000_000,
    )
    sec_a, sec_b = swap(even, odd, "sec")
    buffer = shape((z.devices * z.stride + up_to(COMPS * max(z.caps), SUB), LANES), F32)
    packed, edge_lines, edge_tiles = call(
        send_kernel,
        (base_l, base_s, radar_l, radar_s, swap_a, swap_b, weights_l, weights_s),
        [
            buffer,
            shape((2, 2, COMPS, tall, LANES), BF16),
            shape((2, 2, LANES, LANES), BF16),
        ],
        44,
        specs=[SMEM, SMEM] + [VMEM] * 4 + [ANY] * 2,
        scratch=[
            pltpu.VMEM((3, max(z.lines) + 2 * SUB, LANES), F32),
            pltpu.VMEM((max(z.lines) * SUB, LANES), F32),
            pltpu.VMEM(weights_l.shape, BF16),
            pltpu.VMEM(weights_s.shape, BF16),
            pltpu.SemaphoreType.DMA((sum(z.lines) // z.part,)),
        ],
        flops=10_000_000_000,
        size=2 * (weights_l.size + weights_s.size),
    )
    args = (base_l, base_s, packed, sec_a, sec_b, swap_a, swap_b, marks, edge_lines, edge_tiles)
    sent, _ = pl.pallas_call(
        lambda *refs: tail_kernel(z, *refs),
        in_specs=[SMEM, SMEM] + [VMEM] * 8,
        out_specs=[VMEM, VMEM],
        out_shape=[shape((z.devices, z.rows + SUB, LANES), BF16), buffer],
        input_output_aliases={2: 1},
        compiler_params=params(24),
    )(*args)
    got = lax.all_to_all(sent, AXES, split_axis=0, concat_axis=0, tiled=True)

    small, wide = call(
        matrix_kernel,
        (models,),
        [shape((z.n_model, CHANNELS), F32), shape((2 * z.n_model * SUB, CHANNELS * SUB), BF16)],
        16, flops=50_000_000, size=1_000_000,
    )
    rim = shape((z.n_model, LANES), F32)
    fit, even, odd = call(
        merge_kernel,
        (got, small, wide),
        [shape((z.n_model, z.map_lines, LANES), F32), rim, rim],
        32,
        scratch=[
            pltpu.VMEM((z.devices * max(z.caps), COMPS * LANES), F32),
            pltpu.VMEM((z.devices * SUB, LANES), F32),
            pltpu.VMEM((2 * COMPS, z.map_lines, LANES), F32),
            pltpu.VMEM((z.n_model, z.map_lines + 2 * SUB, LANES), F32),
        ],
        flops=1_000_000_000,
        size=4_000_000,
    )
    sec_a, sec_b = swap(even, odd, "sec")
    return pl.pallas_call(
        lambda *refs: finish_kernel(z, *refs),
        in_specs=[ANY, VMEM, VMEM],
        out_specs=ANY,
        out_shape=shape(fit.shape, F32),
        scratch_shapes=[pltpu.VMEM((2, z.n_model, SUB, LANES), F32), pltpu.SemaphoreType.DMA((4,))],
        input_output_aliases={0: 0},
        compiler_params=params(16),
    )(fit, sec_a, sec_b)


def solution(mesh):
    in_specs = (
        P(None, "sec", "swath"),
        P(None, "sec", "swath"),
        P(("sec", "swath"), None, None),
        P(("sec", "swath"), None, None),
        P(("sec", "swath"), None),
        P(("sec", "swath"), None),
        P(("sec", "swath")),
        P(("sec", "swath")),
        P(),
    )
    out_specs = P(None, "sec", "swath")
    return jax.shard_map(body, mesh=mesh, in_specs=in_specs, out_specs=out_specs, check_vma=False)
```

```python
import jax
import jax.numpy as jnp
from jax import lax
from jax.experimental import pallas as pl
from jax.experimental.pallas import tpu as pltpu
from jax.sharding import PartitionSpec as P

FIT_ITERS = 4
AXES = ("sec", "swath")

cu_square = 0.25
fit_rate = 0.25
upper_pairs = [(first, second) for first in range(6) for second in range(first, 6)]
strict_pairs = [(first, second) for first in range(6) for second in range(first + 1, 6)]
CHANNELS = len(upper_pairs) + len(strict_pairs)
COMPS = 6
NT = (((1,), (1,)), ((), ()))
NN = (((1,), (0,)), ((), ()))
TN = (((0,), (0,)), ((), ()))
HI = lax.Precision.HIGHEST
F32 = jnp.float32
BF16 = jnp.bfloat16
SUB = 8
LANES = 128
EXTRA = 5


def params(mib):
    return pltpu.CompilerParams(vmem_limit_bytes=mib << 20)


def iota(shape, dim):
    return lax.broadcasted_iota(jnp.int32, shape, dim)


def dot(a, b, dims, precision=None):
    return lax.dot_general(a, b, dims, precision=precision, preferred_element_type=F32)


def ones_where(mask, dtype=BF16):
    return jnp.where(mask, 1.0, 0.0).astype(dtype)


def swap(even_pairs, odd_pairs, axis):
    peers = lax.axis_size(axis)
    pairs = lambda start: [p for i in range(start, peers - 1, 2) for p in ((i, i + 1), (i + 1, i))]
    return lax.ppermute(even_pairs, axis, pairs(0)), lax.ppermute(odd_pairs, axis, pairs(1))


def by_parity(axis, one, other):
    even = lax.axis_index(axis) % 2 == 0
    return jnp.where(even, one, other), jnp.where(even, other, one)


VMEM = pl.BlockSpec(memory_space=pltpu.VMEM)
SMEM = pl.BlockSpec(memory_space=pltpu.SMEM)
ANY = pl.BlockSpec(memory_space=pl.ANY)


def whole(shape):
    return pl.BlockSpec(shape, lambda i: (0,) * len(shape))


def up_to(n, multiple):
    return -(-n // multiple) * multiple


class Sizes:
    def __init__(self, lines_l, map_lines, n_model):
        self.devices = lax.axis_size(AXES)
        self.swath = lax.axis_size("swath")
        self.lines = (lines_l, map_lines)
        self.map_lines = map_lines
        self.n_model = n_model
        self.caps = tuple(max(2, 2 * lines // self.devices) for lines in self.lines)
        self.starts = (0, COMPS * self.caps[0])
        self.rows = up_to(COMPS * sum(self.caps), SUB)
        self.stride = up_to(self.rows + SUB, LANES)
        self.lanes = up_to(self.rows, LANES)
        self.part = 64 if lines_l % 64 == 0 and map_lines % 64 == 0 else 2


def first_kernel(
    z, radar_l, radar_s, owner_l, slot_l, owner_s, slot_s, even_pairs, odd_pairs, base_l, base_s, marks,
    held_l, held_s, arrived,
):
    copies = [
        pltpu.make_async_copy(source, held, arrived.at[k])
        for k, (source, held) in enumerate(((radar_l, held_l), (radar_s, held_s)))
    ]
    for copy in copies:
        copy.start()
    plan(z, owner_l, slot_l, owner_s, slot_s, base_l, base_s, marks)
    shape = (2 * SUB, COMPS * LANES)
    row, at = iota(shape, 0), iota(shape, 1)
    pick = ones_where(at == jnp.where(row < SUB, row * LANES, (row - SUB) * LANES + LANES - 1))
    start = 0
    for radar, lines, copy in zip((held_l, held_s), z.lines, copies):
        copy.wait()
        rows = jnp.concatenate([radar[c] for c in range(COMPS)], axis=1)
        both = dot(pick, rows, NT)
        one, other = by_parity("swath", both[SUB:], both[0:SUB])
        even_pairs[:, start : start + lines] = one.astype(BF16)
        odd_pairs[:, start : start + lines] = other.astype(BF16)
        start += lines


def plan(z, owner_l, slot_l, owner_s, slot_s, base_l, base_s, marks):
    total = jnp.zeros((z.devices, LANES), F32)
    shift = 0
    for band, (owner, slot, base) in enumerate(((owner_l, slot_l, base_l), (owner_s, slot_s, base_s))):
        tiles = z.lines[band]
        hit = iota((z.devices, tiles), 0) == owner[...]
        earlier = ones_where(iota((tiles, tiles), 0) < iota((tiles, tiles), 1))
        before = dot(ones_where(hit), earlier, NN)
        rank = jnp.sum(jnp.where(hit, before, 0.0), axis=0, keepdims=True).astype(jnp.int32)
        base[...] = owner[...] * z.stride + z.starts[band] + rank
        line = jnp.where(hit, slot[...].reshape(1, tiles) + 1, 0).astype(F32).astype(BF16)
        place = ones_where(iota((LANES, tiles), 0) == rank + shift)
        total = total + dot(line, place, NT)
        shift += z.caps[band]
    me, other = iota((z.devices, z.devices), 0), iota((z.devices, z.devices), 1)
    inner = me % z.swath
    own = total.astype(BF16)
    before = dot(ones_where((other == me - 1) & (inner > 0)), own, NN)
    after = dot(ones_where((other == me + 1) & (inner < z.swath - 1)), own, NN)
    marks[...] = total + pltpu.roll(before, shift, 1) + pltpu.roll(after, 2 * shift, 1)


def second_kernel(z, top_l, top_s, bottom_l, bottom_s, swap_a, swap_b, even_pairs, odd_pairs):
    after, before = by_parity("swath", swap_a[...].astype(F32), swap_b[...].astype(F32))
    strips = []
    lines_l, lines_s = z.lines
    ends = (
        (top_l, top_s, 0, 0, lines_l),
        (bottom_l, bottom_s, top_l.shape[1] - 1, lines_l - 1, lines_l + lines_s - 1),
    )
    for rows_l, rows_s, row, at_l, at_s in ends:
        parts = [rows_l[...].astype(F32)[:, row, :], rows_s[...].astype(F32)[:, row, :]]
        for side in (before, after):
            for at in (at_l, at_s):
                column = side[0:COMPS, at : at + 1]
                parts.append(jnp.broadcast_to(column, (COMPS, LANES)))
        parts.append(jnp.zeros((even_pairs.shape[0] - 6 * COMPS, LANES), F32))
        strips.append(jnp.concatenate(parts, axis=0))
    one, other = by_parity("sec", strips[1], strips[0])
    even_pairs[...] = one.astype(BF16)
    odd_pairs[...] = other.astype(BF16)


def with_sides(x, left, right):
    lane = iota(x.shape, 1)
    width = x.shape[1]
    before = jnp.where(lane == 0, left, pltpu.roll(x, 1, 1))
    after = jnp.where(lane == width - 1, right, pltpu.roll(x, width - 1, 1))
    return before, after


def filter_band(tiles, radar, left, right, work, filtered):
    inner = pl.ds(SUB, tiles)
    blank = jnp.zeros((1, LANES), F32)
    for plane in range(3):
        work[plane, SUB - 1 : SUB, :] = blank
        work[plane, SUB + tiles : SUB + tiles + 1, :] = blank
    body = [radar[c].astype(F32) for c in range(COMPS)]
    lefts = [left[:, c : c + 1] for c in range(COMPS)]
    rights = [right[:, c : c + 1] for c in range(COMPS)]
    squares = lambda values: sum(v * v for v in values)
    power = squares(body)
    for plane, value in enumerate((power,) + with_sides(power, squares(lefts), squares(rights))):
        work[plane, inner, :] = value
    near = [work[plane, pl.ds(SUB + d, tiles), :] for plane in range(3) for d in (-1, 0, 1)]
    gain = gain_of(near)
    for c in range(COMPS):
        plane = c % 3
        before, after = with_sides(body[c], lefts[c], rights[c])
        work[plane, inner, :] = body[c] + before + after
        mean = work[plane, pl.ds(SUB - 1, tiles), :] + work[plane, inner, :]
        mean = (mean + work[plane, pl.ds(SUB + 1, tiles), :]) / 9.0
        filtered[pl.ds(c, tiles, stride=SUB), :] = mean + gain * (body[c] - mean)


def gain_of(near):
    mean_power = sum(near[1:], near[0]) / 9.0
    spread = jnp.zeros_like(mean_power)
    for q in near:
        spread = spread + (q - mean_power) ** 2
    spread = spread / 9.0
    return spread / (spread + cu_square * mean_power * mean_power + 1.0)


def send_kernel(
    z, base_l, base_s, radar_l, radar_s, swap_a, swap_b, weights_l, weights_s,
    packed, edge_lines, edge_tiles, work, filtered, held_l, held_s, arrived,
):
    chunks, count = [], 0
    for source, held, lines in ((weights_l, held_l, z.lines[0]), (weights_s, held_s, z.lines[1])):
        copies = []
        for at in range(0, lines, z.part):
            part = pl.ds(at, z.part)
            copies.append(pltpu.make_async_copy(source.at[part], held.at[part], arrived.at[count]))
            copies[-1].start()
            count += 1
        chunks.append(copies)
    packed[...] = jnp.zeros_like(packed)
    tall = edge_lines.shape[3]
    for band, radar in enumerate((radar_l, radar_s)):
        edge_lines[band, 0] = radar[:, 0:tall, :]
        edge_lines[band, 1] = radar[:, z.lines[band] - tall :, :]
    after, before = by_parity("swath", swap_a[...].astype(F32), swap_b[...].astype(F32))
    left, right = before.T, after.T
    at = 0
    for band, (radar, base, held) in enumerate(((radar_l, base_l, held_l), (radar_s, base_s, held_s))):
        tiles, capacity = z.lines[band], z.caps[band]
        filter_band(tiles, radar, left[at : at + tiles], right[at : at + tiles], work, filtered)
        at += tiles
        for i, copy in enumerate(chunks[band]):
            copy.wait()
            for t in range(0, z.part, 2):
                tile = i * z.part + t
                lines = filtered[pl.ds(tile * SUB, 2 * SUB), :].astype(BF16)
                matrix = held[pl.ds(tile, 2)].reshape(2 * LANES, LANES)
                result = dot(lines, matrix, NT)
                first, second = base[0, tile], base[0, tile + 1]
                packed[pl.ds(first, COMPS, stride=capacity), :] = result[0:COMPS, 0:LANES]
                packed[pl.ds(second, COMPS, stride=capacity), :] = result[SUB : SUB + COMPS, LANES:]
        edge_tiles[band, 0] = held[0]
        edge_tiles[band, 1] = held[tiles - 1]


def tail_kernel(
    z, base_l, base_s, given, sec_a, sec_b, swap_a, swap_b, marks,
    lines_held, tiles_held, sent, packed, out, leaving,
):
    del given
    tall = lines_held.shape[3]
    after, before = by_parity("swath", swap_a[...].astype(F32), swap_b[...].astype(F32))
    down, up = by_parity("sec", sec_a[...].astype(F32), sec_b[...].astype(F32))
    shift = 0
    for band, base in enumerate((base_l, base_s)):
        lines = z.lines[band]
        for end in range(2):
            rows = lines_held[band, end].astype(F32)
            strip = (up, down)[end]
            first = 0 if end == 0 else lines - 2
            near_row = 0 if end == 0 else tall - 2
            columns = (before, after)
            values, sides = [], [[], []]
            for c in range(COMPS):
                row = band * COMPS + c
                far = strip[row : row + 1]
                near = rows[c, near_row : near_row + 2]
                values.append(jnp.concatenate([far, near] if end == 0 else [near, far], axis=0))
                for side in range(2):
                    corner = 2 * COMPS * (1 + side) + row
                    far = strip[corner : corner + 1, 0:1]
                    near = [
                        columns[side][c : c + 1, shift + first + k : shift + first + k + 1]
                        for k in range(2)
                    ]
                    sides[side].append(jnp.concatenate([far] + near if end == 0 else near + [far], axis=0))
            squares = lambda parts: sum(v * v for v in parts)
            power = squares(values)
            planes = (power,) + with_sides(power, squares(sides[0]), squares(sides[1]))
            gain = gain_of([plane[k : k + 1] for plane in planes for k in range(3)])
            lines_out = []
            for c in range(COMPS):
                left, right = with_sides(values[c], sides[0][c], sides[1][c])
                total = values[c] + left + right
                mean = (total[0:1] + total[1:2] + total[2:3]) / 9.0
                lines_out.append(mean + gain * (values[c][1:2] - mean))
            lines_out.append(jnp.zeros((SUB - COMPS, LANES), F32))
            result = dot(jnp.concatenate(lines_out, axis=0).astype(BF16), tiles_held[band, end], NT)
            target = base[0, 0 if end == 0 else lines - 1]
            packed[pl.ds(target, COMPS, stride=z.caps[band]), :] = result[0:COMPS]
        shift += lines

    steps = z.lanes // LANES
    row, lane = iota((SUB, LANES), 0), iota((SUB, LANES), 1)
    pick = ones_where(
        ((row >= 1) & (row <= steps) & (lane == LANES - 1)) | ((row > steps) & (row <= 2 * steps) & (lane == 0))
    )
    columns = [
        dot(pick, packed[o * z.stride : o * z.stride + z.lanes, :].astype(BF16), NT) for o in range(z.devices)
    ]
    group, copies = z.devices // 4, []
    for o in range(z.devices):
        extra = jnp.broadcast_to(marks[o : o + 1, :], (SUB, LANES))
        one_less, one_more = max(o - 1, 0), min(o + 1, z.devices - 1)
        for k in range(steps):
            part = slice(k * LANES, (k + 1) * LANES)
            extra = jnp.where(row == 1 + k, columns[one_less][:, part], extra)
            extra = jnp.where(row == 1 + steps + k, columns[one_more][:, part], extra)
        out[o, 0 : z.rows, :] = packed[o * z.stride : o * z.stride + z.rows, :].astype(BF16)
        out[o, z.rows :, :] = extra.astype(BF16)
        if (o + 1) % group == 0:
            part = pl.ds(o + 1 - group, group)
            copies.append(pltpu.make_async_copy(out.at[part], sent.at[part], leaving.at[o // group]))
            copies[-1].start()
    for copy in copies:
        copy.wait()


def matrix_kernel(models, small, wide):
    m = models[...]
    n_model = m.shape[0]
    eye = ones_where(iota((CHANNELS, CHANNELS), 0) == iota((CHANNELS, CHANNELS), 1), F32)
    powers = jnp.zeros(m.shape, F32)
    for _ in range(FIT_ITERS):
        predicted = dot(m, powers, TN, HI)
        powers = powers + fit_rate * dot(m, eye - predicted, NN, HI)
    powers = powers / 9.0
    small[...] = powers
    rows, columns = wide.shape[0] // 2, wide.shape[1]
    left = ones_where(iota((rows, n_model), 0) // SUB == iota((rows, n_model), 1), F32)
    right = ones_where(iota((CHANNELS, columns), 1) // SUB == iota((CHANNELS, columns), 0), F32)
    spread = dot(dot(left, powers, NN, HI), right, NN, HI)
    same = iota((rows, columns), 0) % SUB == iota((rows, columns), 1) % SUB
    spread = jnp.where(same, spread, 0.0)
    high = spread.astype(BF16)
    low = (spread - high.astype(F32)).astype(BF16)
    wide[...] = jnp.concatenate([high, low], axis=0)


def coherency(real, imag):
    joint = [real[f] * real[g] + imag[f] * imag[g] for f, g in upper_pairs]
    return joint + [imag[f] * real[g] - real[f] * imag[g] for f, g in strict_pairs]


def split_parts(maps):
    pick = lambda at: [maps(band * COMPS + at + c) for band in range(2) for c in range(3)]
    return pick(0), pick(3)


def merge_kernel(z, got, small, wide, maps, planes, even_pairs, odd_pairs, stage, extras, two):
    map_lines, n_model, devices = z.map_lines, z.n_model, z.devices
    steps = z.lanes // LANES
    for s in range(devices):
        extras[s * SUB : (s + 1) * SUB, :] = got[s, z.rows : z.rows + SUB, :].astype(F32)
    piece = lambda r: extras[pl.ds(r, devices, stride=SUB), :]
    marks = piece(0)
    sides = [
        jnp.concatenate([piece(1 + side * steps + k) for k in range(steps)], axis=1) for side in range(2)
    ]
    shift = sum(z.caps)
    edges = [[None] * (2 * COMPS) for _ in range(2)]
    at_mark = 0
    for band in range(2):
        capacity = z.caps[band]
        places = devices * capacity
        for s in range(devices):
            block = got[s, 0 : z.rows, :].astype(F32)
            for c in range(COMPS):
                low = z.starts[band] + c * capacity
                stage[s * capacity : (s + 1) * capacity, c * LANES : (c + 1) * LANES] = block[
                    low : low + capacity, :
                ]
        turned = lambda x, by: pltpu.roll(x, (x.shape[1] - by) % x.shape[1], 1)[:, 0:LANES]
        rows = [turned(marks, at_mark + k * shift) for k in range(3)]
        for side in range(2):
            rows += [turned(sides[side], z.starts[band] + c * capacity) for c in range(COMPS)]
        at_mark += capacity
        place = iota((devices, places), 1)
        low = iota((devices, places), 0) * capacity
        mine = (place >= low) & (place < low + capacity)
        offset = jnp.sum(jnp.where(mine, place - low, 0), axis=0, keepdims=True)
        pick = ones_where(iota((LANES, places), 0) == offset)
        spread = dot(jnp.concatenate(rows, axis=0).astype(BF16), pick, NN)
        flat = [
            jnp.sum(jnp.where(mine, spread[k * devices : (k + 1) * devices], 0.0), axis=0, keepdims=True)
            for k in range(len(rows))
        ]
        lines = iota((map_lines, places), 0) + 1
        tables = [ones_where(lines == flat[k].astype(jnp.int32)) for k in range(3)]
        summed = dot(tables[0], stage[0:places, :].astype(BF16), NN)
        for c in range(COMPS):
            maps[band * COMPS + c] = summed[:, c * LANES : (c + 1) * LANES]
        for side in range(2):
            values = flat[3 + side * COMPS : 3 + (side + 1) * COMPS]
            values = jnp.concatenate(values + [jnp.zeros((SUB - COMPS, places), F32)], axis=0).astype(BF16)
            column = dot(values, tables[1 + side], NT)
            for c in range(COMPS):
                edges[side][band * COMPS + c] = column[c : c + 1, :]
    turned = []
    for side in range(2):
        joint = jnp.concatenate(coherency(*split_parts(lambda i: edges[side][i])), axis=0)
        turned.append(dot(small[...], joint, NN, HI))
    x = jnp.concatenate(turned, axis=0)
    high = x.astype(BF16)
    x = jnp.concatenate([high, (x - high.astype(F32)).astype(BF16)], axis=0)
    at = iota((4 * n_model, n_model * LANES), 0) % (2 * n_model)
    to = iota((4 * n_model, n_model * LANES), 1)
    target = jnp.where(at < n_model, at * LANES + LANES - 1, (at - n_model) * LANES)
    planes[...] = dot(x, ones_where(to == target), TN)

    ends = (0, map_lines - SUB)
    two[...] = fit_block(wide, maps, ends, n_model)
    for k in range(n_model):
        part = slice(k * LANES, (k + 1) * LANES)
        top = two[k * SUB : k * SUB + 1, 0:LANES]
        bottom = two[k * SUB + SUB - 1 : (k + 1) * SUB, LANES:]
        top = three_lanes(top, planes[0:1, part])
        bottom = three_lanes(bottom, planes[map_lines - 1 : map_lines, part])
        one, other = by_parity("sec", bottom, top)
        even_pairs[k : k + 1, :] = one
        odd_pairs[k : k + 1, :] = other


def fit_block(wide, maps, starts, n_model):
    halves = []
    for r in starts:
        x = jnp.concatenate(coherency(*split_parts(lambda n: maps[n, pl.ds(r, SUB), :])), axis=0)
        halves.append(x.astype(BF16))
    result = dot(wide[...], jnp.concatenate(halves, axis=1), NN)
    return result[0 : n_model * SUB] + result[n_model * SUB :]


def three_lanes(x, side):
    lane = iota(x.shape, 1)
    before = pltpu.roll(jnp.where(lane == LANES - 1, side, x), 1, 1)
    after = pltpu.roll(jnp.where(lane == 0, side, x), LANES - 1, 1)
    return x + before + after


def spread_kernel(z, maps, planes, wide, out, ends, fits):
    map_lines, n_model = z.map_lines, z.n_model
    for i in range(map_lines // (2 * SUB)):
        starts = (2 * i * SUB, (2 * i + 1) * SUB)
        result = fit_block(wide, maps, starts, n_model)
        for h, r in enumerate(starts):
            for k in range(n_model):
                fits[k, pl.ds(SUB + r, SUB), :] = result[
                    k * SUB : (k + 1) * SUB, h * LANES : (h + 1) * LANES
                ]
    blank = jnp.zeros((1, LANES), F32)
    inner = pl.ds(SUB, map_lines)
    for k in range(n_model):
        x = three_lanes(fits[k, inner, :], planes[:, k * LANES : (k + 1) * LANES])
        fits[k, inner, :] = x
        fits[k, SUB - 1 : SUB, :] = blank
        fits[k, SUB + map_lines : SUB + map_lines + 1, :] = blank
        x = fits[k, pl.ds(SUB - 1, map_lines), :] + x + fits[k, pl.ds(SUB + 1, map_lines), :]
        out[k] = x
        ends[0, k] = x[0:SUB]
        ends[1, k] = x[map_lines - SUB :]


def finish_kernel(z, given, ends, sec_a, sec_b, out, held, moving):
    del given
    below, above = by_parity("sec", sec_a[...], sec_b[...])
    line = iota((SUB, LANES), 0)
    copies = []
    for end, (at, row, start) in enumerate(((0, above, 0), (SUB - 1, below, z.map_lines - SUB))):
        for k in range(z.n_model):
            held[end, k] = ends[end, k] + jnp.where(line == at, row[k : k + 1, :], 0.0)
        copies.append(pltpu.make_async_copy(held.at[end], out.at[:, pl.ds(start, SUB), :], moving.at[end]))
        copies[-1].start()
    for copy in copies:
        copy.wait()


def body(radar_l, radar_s, weights_l, weights_s, owner_l, owner_s, slot_l, slot_s, models):
    z = Sizes(radar_l.shape[1], radar_s.shape[1], models.shape[0])
    lines_l, lines_s = z.lines
    shape = jax.ShapeDtypeStruct

    def call(kernel, args, shapes, mib, scratch=(), specs=None, flops=0, size=0):
        return pl.pallas_call(
            lambda *refs: kernel(z, *refs) if kernel is not matrix_kernel else kernel(*refs),
            in_specs=specs or [VMEM] * len(args),
            out_specs=[VMEM] * len(shapes),
            out_shape=shapes,
            scratch_shapes=scratch,
            compiler_params=params(mib),
            cost_estimate=pl.CostEstimate(flops=flops, bytes_accessed=size, transcendentals=0),
        )(*args)

    def call_one(kernel, args, specs, shapes, mib, scratch=(), aliases={}, flops=0, size=0):
        return pl.pallas_call(
            lambda *refs: kernel(z, *refs),
            grid=(1,),
            in_specs=specs,
            out_specs=[whole(x.shape) for x in shapes],
            out_shape=shapes,
            scratch_shapes=scratch,
            input_output_aliases=aliases,
            compiler_params=params(mib),
            cost_estimate=pl.CostEstimate(flops=flops, bytes_accessed=size, transcendentals=0),
        )(*args)

    row = lambda x: x.reshape(1, -1)
    radar = (radar_l, radar_s)
    column = shape((SUB, lines_l + lines_s), BF16)
    args = radar + (row(owner_l), slot_l, row(owner_s), slot_s)
    even, odd, base_l, base_s, marks = call_one(
        first_kernel,
        args,
        [ANY, ANY] + [whole(x.shape) for x in args[2:]],
        [column, column, shape((1, lines_l), jnp.int32), shape((1, lines_s), jnp.int32), shape((z.devices, LANES), F32)],
        58,
        scratch=[pltpu.VMEM(x.shape, BF16) for x in radar] + [pltpu.SemaphoreType.DMA((2,))],
        flops=10_000_000_000,
        size=1_000_000,
    )
    swap_a, swap_b = swap(even, odd, "swath")
    strip = shape((5 * SUB, LANES), BF16)
    tall = 2 * SUB
    edge = lambda lines, end: pl.BlockSpec(
        (COMPS, tall, LANES), lambda i: (0, end * (lines // tall - 1), 0)
    )
    edges = [edge(lines, end) for end in range(2) for lines in z.lines]
    side = whole(column.shape)
    even, odd = call_one(
        second_kernel, radar * 2 + (swap_a, swap_b), edges + [side, side], [strip, strip], 32, flops=10_000_000_000, size=1_000_000,
    )
    sec_a, sec_b = swap(even, odd, "sec")
    buffer = shape((z.devices * z.stride + up_to(COMPS * max(z.caps), SUB), LANES), F32)
    packed, edge_lines, edge_tiles = call(
        send_kernel,
        (base_l, base_s, radar_l, radar_s, swap_a, swap_b, weights_l, weights_s),
        [
            buffer,
            shape((2, 2, COMPS, tall, LANES), BF16),
            shape((2, 2, LANES, LANES), BF16),
        ],
        44,
        specs=[SMEM, SMEM] + [VMEM] * 4 + [ANY] * 2,
        scratch=[
            pltpu.VMEM((3, max(z.lines) + 2 * SUB, LANES), F32),
            pltpu.VMEM((max(z.lines) * SUB, LANES), F32),
            pltpu.VMEM(weights_l.shape, BF16),
            pltpu.VMEM(weights_s.shape, BF16),
            pltpu.SemaphoreType.DMA((sum(z.lines) // z.part,)),
        ],
        flops=10_000_000_000,
        size=2 * (weights_l.size + weights_s.size),
    )
    args = (base_l, base_s, packed, sec_a, sec_b, swap_a, swap_b, marks, edge_lines, edge_tiles)
    sent, _ = pl.pallas_call(
        lambda *refs: tail_kernel(z, *refs),
        in_specs=[SMEM, SMEM] + [VMEM] * 8,
        out_specs=[ANY, VMEM],
        out_shape=[shape((z.devices, z.rows + SUB, LANES), BF16), buffer],
        scratch_shapes=[pltpu.VMEM((z.devices, z.rows + SUB, LANES), BF16), pltpu.SemaphoreType.DMA((4,))],
        input_output_aliases={2: 1},
        compiler_params=params(24),
    )(*args)
    got = lax.all_to_all(sent, AXES, split_axis=0, concat_axis=0, tiled=True)

    small, wide = call(
        matrix_kernel,
        (models,),
        [shape((z.n_model, CHANNELS), F32), shape((2 * z.n_model * SUB, CHANNELS * SUB), BF16)],
        16, flops=50_000_000, size=1_000_000,
    )
    rim = shape((z.n_model, LANES), F32)
    maps, planes, even, odd = call(
        merge_kernel,
        (got, small, wide),
        [
            shape((2 * COMPS, z.map_lines, LANES), F32),
            shape((z.map_lines, z.n_model * LANES), F32),
            rim,
            rim,
        ],
        24,
        scratch=[
            pltpu.VMEM((z.devices * max(z.caps), COMPS * LANES), F32),
            pltpu.VMEM((z.devices * SUB, LANES), F32),
            pltpu.VMEM((z.n_model * SUB, 2 * LANES), F32),
        ],
        flops=1_000_000_000,
        size=4_000_000,
    )
    sec_a, sec_b = swap(even, odd, "sec")
    edge = shape((2, z.n_model, SUB, LANES), F32)
    fit, ends = call(
        spread_kernel,
        (maps, planes, wide),
        [shape((z.n_model, z.map_lines, LANES), F32), edge],
        24,
        scratch=[pltpu.VMEM((z.n_model, z.map_lines + 2 * SUB, LANES), F32)],
        flops=10_000_000_000,
        size=4_000_000,
    )
    return pl.pallas_call(
        lambda *refs: finish_kernel(z, *refs),
        in_specs=[ANY, VMEM, VMEM, VMEM],
        out_specs=ANY,
        out_shape=shape(fit.shape, F32),
        scratch_shapes=[pltpu.VMEM(edge.shape, F32), pltpu.SemaphoreType.DMA((2,))],
        input_output_aliases={0: 0},
        compiler_params=params(16),
    )(fit, ends, sec_a, sec_b)


def solution(mesh):
    in_specs = (
        P(None, "sec", "swath"),
        P(None, "sec", "swath"),
        P(("sec", "swath"), None, None),
        P(("sec", "swath"), None, None),
        P(("sec", "swath"), None),
        P(("sec", "swath"), None),
        P(("sec", "swath")),
        P(("sec", "swath")),
        P(),
    )
    out_specs = P(None, "sec", "swath")
    return jax.shard_map(body, mesh=mesh, in_specs=in_specs, out_specs=out_specs, check_vma=False)
```

```python
import jax
import jax.numpy as jnp
from jax import lax
from jax.experimental import pallas as pl
from jax.experimental.pallas import tpu as pltpu
from jax.sharding import PartitionSpec as P

FIT_ITERS = 4
AXES = ("sec", "swath")

cu_square = 0.25
fit_rate = 0.25
upper_pairs = [(first, second) for first in range(6) for second in range(first, 6)]
strict_pairs = [(first, second) for first in range(6) for second in range(first + 1, 6)]
CHANNELS = len(upper_pairs) + len(strict_pairs)
COMPS = 6
NT = (((1,), (1,)), ((), ()))
NN = (((1,), (0,)), ((), ()))
TN = (((0,), (0,)), ((), ()))
HI = lax.Precision.HIGHEST
F32 = jnp.float32
BF16 = jnp.bfloat16
SUB = 8
LANES = 128
EXTRA = 5


def params(mib):
    return pltpu.CompilerParams(vmem_limit_bytes=mib << 20)


def iota(shape, dim):
    return lax.broadcasted_iota(jnp.int32, shape, dim)


def dot(a, b, dims, precision=None):
    return lax.dot_general(a, b, dims, precision=precision, preferred_element_type=F32)


def ones_where(mask, dtype=BF16):
    return jnp.where(mask, 1.0, 0.0).astype(dtype)


def swap(even_pairs, odd_pairs, axis):
    peers = lax.axis_size(axis)
    pairs = lambda start: [p for i in range(start, peers - 1, 2) for p in ((i, i + 1), (i + 1, i))]
    return lax.ppermute(even_pairs, axis, pairs(0)), lax.ppermute(odd_pairs, axis, pairs(1))


def by_parity(axis, one, other):
    even = lax.axis_index(axis) % 2 == 0
    return jnp.where(even, one, other), jnp.where(even, other, one)


VMEM = pl.BlockSpec(memory_space=pltpu.VMEM)
SMEM = pl.BlockSpec(memory_space=pltpu.SMEM)
ANY = pl.BlockSpec(memory_space=pl.ANY)


def whole(shape):
    return pl.BlockSpec(shape, lambda i: (0,) * len(shape))


def up_to(n, multiple):
    return -(-n // multiple) * multiple


class Sizes:
    def __init__(self, lines_l, map_lines, n_model):
        self.devices = lax.axis_size(AXES)
        self.swath = lax.axis_size("swath")
        self.lines = (lines_l, map_lines)
        self.map_lines = map_lines
        self.n_model = n_model
        self.caps = tuple(max(2, 2 * lines // self.devices) for lines in self.lines)
        self.starts = (0, COMPS * self.caps[0])
        self.rows = up_to(COMPS * sum(self.caps), SUB)
        self.stride = up_to(self.rows + SUB, LANES)
        self.lanes = up_to(self.rows, LANES)
        self.part = 64 if lines_l % 64 == 0 and map_lines % 64 == 0 else 2


def first_kernel(
    z, radar_l, radar_s, owner_l, slot_l, owner_s, slot_s, even_pairs, odd_pairs, base_l, base_s, marks,
    held_l, held_s, arrived,
):
    copies = [
        pltpu.make_async_copy(source, held, arrived.at[k])
        for k, (source, held) in enumerate(((radar_l, held_l), (radar_s, held_s)))
    ]
    for copy in copies:
        copy.start()
    plan(z, owner_l, slot_l, owner_s, slot_s, base_l, base_s, marks)
    shape = (2 * SUB, COMPS * LANES)
    row, at = iota(shape, 0), iota(shape, 1)
    pick = ones_where(at == jnp.where(row < SUB, row * LANES, (row - SUB) * LANES + LANES - 1))
    start = 0
    for radar, lines, copy in zip((held_l, held_s), z.lines, copies):
        copy.wait()
        rows = jnp.concatenate([radar[c] for c in range(COMPS)], axis=1)
        both = dot(pick, rows, NT)
        one, other = by_parity("swath", both[SUB:], both[0:SUB])
        even_pairs[:, start : start + lines] = one.astype(BF16)
        odd_pairs[:, start : start + lines] = other.astype(BF16)
        start += lines


def plan(z, owner_l, slot_l, owner_s, slot_s, base_l, base_s, marks):
    total = jnp.zeros((z.devices, LANES), F32)
    shift = 0
    for band, (owner, slot, base) in enumerate(((owner_l, slot_l, base_l), (owner_s, slot_s, base_s))):
        tiles = z.lines[band]
        hit = iota((z.devices, tiles), 0) == owner[...]
        earlier = ones_where(iota((tiles, tiles), 0) < iota((tiles, tiles), 1))
        before = dot(ones_where(hit), earlier, NN)
        rank = jnp.sum(jnp.where(hit, before, 0.0), axis=0, keepdims=True).astype(jnp.int32)
        base[...] = owner[...] * z.stride + z.starts[band] + rank
        line = jnp.where(hit, slot[...].reshape(1, tiles) + 1, 0).astype(F32).astype(BF16)
        place = ones_where(iota((LANES, tiles), 0) == rank + shift)
        total = total + dot(line, place, NT)
        shift += z.caps[band]
    me, other = iota((z.devices, z.devices), 0), iota((z.devices, z.devices), 1)
    inner = me % z.swath
    own = total.astype(BF16)
    before = dot(ones_where((other == me - 1) & (inner > 0)), own, NN)
    after = dot(ones_where((other == me + 1) & (inner < z.swath - 1)), own, NN)
    marks[...] = total + pltpu.roll(before, shift, 1) + pltpu.roll(after, 2 * shift, 1)


def second_kernel(z, top_l, top_s, bottom_l, bottom_s, swap_a, swap_b, even_pairs, odd_pairs):
    after, before = by_parity("swath", swap_a[...].astype(F32), swap_b[...].astype(F32))
    strips = []
    lines_l, lines_s = z.lines
    ends = (
        (top_l, top_s, 0, 0, lines_l),
        (bottom_l, bottom_s, top_l.shape[1] - 1, lines_l - 1, lines_l + lines_s - 1),
    )
    for rows_l, rows_s, row, at_l, at_s in ends:
        parts = [rows_l[...].astype(F32)[:, row, :], rows_s[...].astype(F32)[:, row, :]]
        for side in (before, after):
            for at in (at_l, at_s):
                column = side[0:COMPS, at : at + 1]
                parts.append(jnp.broadcast_to(column, (COMPS, LANES)))
        parts.append(jnp.zeros((even_pairs.shape[0] - 6 * COMPS, LANES), F32))
        strips.append(jnp.concatenate(parts, axis=0))
    one, other = by_parity("sec", strips[1], strips[0])
    even_pairs[...] = one.astype(BF16)
    odd_pairs[...] = other.astype(BF16)


def with_sides(x, left, right):
    lane = iota(x.shape, 1)
    width = x.shape[1]
    before = jnp.where(lane == 0, left, pltpu.roll(x, 1, 1))
    after = jnp.where(lane == width - 1, right, pltpu.roll(x, width - 1, 1))
    return before, after


def filter_planes(tiles, radar, left, right, planes):
    inner = pl.ds(SUB, tiles)
    blank = jnp.zeros((1, LANES), F32)
    for plane in range(3 + COMPS):
        planes[plane, SUB - 1 : SUB, :] = blank
        planes[plane, SUB + tiles : SUB + tiles + 1, :] = blank
    squares = lambda values: sum(v * v for v in values)
    lefts = [left[:, c : c + 1] for c in range(COMPS)]
    rights = [right[:, c : c + 1] for c in range(COMPS)]
    total = jnp.zeros((tiles, LANES), F32)
    for c in range(COMPS):
        x = radar[c].astype(F32)
        total = total + x * x
        before, after = with_sides(x, lefts[c], rights[c])
        planes[3 + c, inner, :] = x + before + after
    for plane, value in enumerate((total,) + with_sides(total, squares(lefts), squares(rights))):
        planes[plane, inner, :] = value


def filter_lines(start, lines, radar, planes, filtered):
    at = lambda plane, shift: planes[plane, pl.ds(SUB + start + shift, lines), :]
    gain = gain_of([at(plane, d) for plane in range(3) for d in (-1, 0, 1)])
    for c in range(COMPS):
        mean = (at(3 + c, -1) + at(3 + c, 0) + at(3 + c, 1)) / 9.0
        x = radar[c, pl.ds(start, lines), :].astype(F32)
        filtered[pl.ds(start * SUB + c, lines, stride=SUB), :] = mean + gain * (x - mean)


def gain_of(near):
    mean_power = sum(near[1:], near[0]) / 9.0
    spread = jnp.zeros_like(mean_power)
    for q in near:
        spread = spread + (q - mean_power) ** 2
    spread = spread / 9.0
    return spread / (spread + cu_square * mean_power * mean_power + 1.0)


def send_kernel(
    z, base_l, base_s, radar_l, radar_s, swap_a, swap_b, weights_l, weights_s,
    packed, edge_lines, edge_tiles, planes_l, planes_s, filtered_l, filtered_s, held_l, arrived,
):
    copies = []
    for at in range(0, z.lines[0], z.part):
        part = pl.ds(at, z.part)
        copies.append(pltpu.make_async_copy(weights_l.at[part], held_l.at[part], arrived.at[len(copies)]))
        copies[-1].start()
    packed[...] = jnp.zeros_like(packed)
    tall = edge_lines.shape[3]
    for band, radar in enumerate((radar_l, radar_s)):
        edge_lines[band, 0] = radar[:, 0:tall, :]
        edge_lines[band, 1] = radar[:, z.lines[band] - tall :, :]
    after, before = by_parity("swath", swap_a[...].astype(F32), swap_b[...].astype(F32))
    left, right = before.T, after.T
    bands = (
        (radar_l, base_l, held_l, planes_l, filtered_l),
        (radar_s, base_s, weights_s, planes_s, filtered_s),
    )
    at = (0, z.lines[0])
    for band in (1, 0):
        radar, _, _, planes, _ = bands[band]
        part = slice(at[band], at[band] + z.lines[band])
        filter_planes(z.lines[band], radar, left[part], right[part], planes)
    todo = [(band, start) for band in (1, 0) for start in range(0, z.lines[band], z.part)]

    def lines_of(band, start):
        radar, _, _, planes, filtered = bands[band]
        filter_lines(start, z.part, radar, planes, filtered)

    lines_of(*todo[0])
    for i, (band, start) in enumerate(todo):
        _, base, held, _, filtered = bands[band]
        if band == 0:
            copies[start // z.part].wait()
        if i + 1 < len(todo):
            lines_of(*todo[i + 1])
        for tile in range(start, start + z.part, 2):
            lines = filtered[pl.ds(tile * SUB, 2 * SUB), :].astype(BF16)
            matrix = held[pl.ds(tile, 2)].reshape(2 * LANES, LANES)
            result = dot(lines, matrix, NT)
            first, second = base[0, tile], base[0, tile + 1]
            packed[pl.ds(first, COMPS, stride=z.caps[band]), :] = result[0:COMPS, 0:LANES]
            packed[pl.ds(second, COMPS, stride=z.caps[band]), :] = result[SUB : SUB + COMPS, LANES:]
    for band, (_, _, held, _, _) in enumerate(bands):
        edge_tiles[band, 0] = held[0]
        edge_tiles[band, 1] = held[z.lines[band] - 1]


def tail_kernel(
    z, base_l, base_s, given, sec_a, sec_b, swap_a, swap_b, marks,
    lines_held, tiles_held, sent, packed, out, leaving,
):
    del given
    tall = lines_held.shape[3]
    after, before = by_parity("swath", swap_a[...].astype(F32), swap_b[...].astype(F32))
    down, up = by_parity("sec", sec_a[...].astype(F32), sec_b[...].astype(F32))
    shift = 0
    for band, base in enumerate((base_l, base_s)):
        lines = z.lines[band]
        for end in range(2):
            rows = lines_held[band, end].astype(F32)
            strip = (up, down)[end]
            first = 0 if end == 0 else lines - 2
            near_row = 0 if end == 0 else tall - 2
            columns = (before, after)
            values, sides = [], [[], []]
            for c in range(COMPS):
                row = band * COMPS + c
                far = strip[row : row + 1]
                near = rows[c, near_row : near_row + 2]
                values.append(jnp.concatenate([far, near] if end == 0 else [near, far], axis=0))
                for side in range(2):
                    corner = 2 * COMPS * (1 + side) + row
                    far = strip[corner : corner + 1, 0:1]
                    near = [
                        columns[side][c : c + 1, shift + first + k : shift + first + k + 1]
                        for k in range(2)
                    ]
                    sides[side].append(jnp.concatenate([far] + near if end == 0 else near + [far], axis=0))
            squares = lambda parts: sum(v * v for v in parts)
            power = squares(values)
            planes = (power,) + with_sides(power, squares(sides[0]), squares(sides[1]))
            gain = gain_of([plane[k : k + 1] for plane in planes for k in range(3)])
            lines_out = []
            for c in range(COMPS):
                left, right = with_sides(values[c], sides[0][c], sides[1][c])
                total = values[c] + left + right
                mean = (total[0:1] + total[1:2] + total[2:3]) / 9.0
                lines_out.append(mean + gain * (values[c][1:2] - mean))
            lines_out.append(jnp.zeros((SUB - COMPS, LANES), F32))
            result = dot(jnp.concatenate(lines_out, axis=0).astype(BF16), tiles_held[band, end], NT)
            target = base[0, 0 if end == 0 else lines - 1]
            packed[pl.ds(target, COMPS, stride=z.caps[band]), :] = result[0:COMPS]
        shift += lines

    steps = z.lanes // LANES
    row, lane = iota((SUB, LANES), 0), iota((SUB, LANES), 1)
    pick = ones_where(
        ((row >= 1) & (row <= steps) & (lane == LANES - 1)) | ((row > steps) & (row <= 2 * steps) & (lane == 0))
    )
    columns = [
        dot(pick, packed[o * z.stride : o * z.stride + z.lanes, :].astype(BF16), NT) for o in range(z.devices)
    ]
    group, copies = z.devices // 4, []
    for o in range(z.devices):
        extra = jnp.broadcast_to(marks[o : o + 1, :], (SUB, LANES))
        one_less, one_more = max(o - 1, 0), min(o + 1, z.devices - 1)
        for k in range(steps):
            part = slice(k * LANES, (k + 1) * LANES)
            extra = jnp.where(row == 1 + k, columns[one_less][:, part], extra)
            extra = jnp.where(row == 1 + steps + k, columns[one_more][:, part], extra)
        out[o, 0 : z.rows, :] = packed[o * z.stride : o * z.stride + z.rows, :].astype(BF16)
        out[o, z.rows :, :] = extra.astype(BF16)
        if (o + 1) % group == 0:
            part = pl.ds(o + 1 - group, group)
            copies.append(pltpu.make_async_copy(out.at[part], sent.at[part], leaving.at[o // group]))
            copies[-1].start()
    for copy in copies:
        copy.wait()


def matrix_kernel(models, small, wide):
    m = models[...]
    n_model = m.shape[0]
    eye = ones_where(iota((CHANNELS, CHANNELS), 0) == iota((CHANNELS, CHANNELS), 1), F32)
    powers = jnp.zeros(m.shape, F32)
    for _ in range(FIT_ITERS):
        predicted = dot(m, powers, TN, HI)
        powers = powers + fit_rate * dot(m, eye - predicted, NN, HI)
    powers = powers / 9.0
    small[...] = powers
    rows, columns = wide.shape[0] // 2, wide.shape[1]
    left = ones_where(iota((rows, n_model), 0) // SUB == iota((rows, n_model), 1), F32)
    right = ones_where(iota((CHANNELS, columns), 1) // SUB == iota((CHANNELS, columns), 0), F32)
    spread = dot(dot(left, powers, NN, HI), right, NN, HI)
    same = iota((rows, columns), 0) % SUB == iota((rows, columns), 1) % SUB
    spread = jnp.where(same, spread, 0.0)
    high = spread.astype(BF16)
    low = (spread - high.astype(F32)).astype(BF16)
    wide[...] = jnp.concatenate([high, low], axis=0)


def coherency(real, imag):
    joint = [real[f] * real[g] + imag[f] * imag[g] for f, g in upper_pairs]
    return joint + [imag[f] * real[g] - real[f] * imag[g] for f, g in strict_pairs]


def split_parts(maps):
    pick = lambda at: [maps(band * COMPS + at + c) for band in range(2) for c in range(3)]
    return pick(0), pick(3)


def merge_kernel(z, got, small, wide, maps, planes, even_pairs, odd_pairs, stage, extras, two):
    map_lines, n_model, devices = z.map_lines, z.n_model, z.devices
    steps = z.lanes // LANES
    for s in range(devices):
        extras[s * SUB : (s + 1) * SUB, :] = got[s, z.rows : z.rows + SUB, :].astype(F32)
    piece = lambda r: extras[pl.ds(r, devices, stride=SUB), :]
    marks = piece(0)
    sides = [
        jnp.concatenate([piece(1 + side * steps + k) for k in range(steps)], axis=1) for side in range(2)
    ]
    shift = sum(z.caps)
    edges = [[None] * (2 * COMPS) for _ in range(2)]
    at_mark = 0
    for band in range(2):
        capacity = z.caps[band]
        places = devices * capacity
        for s in range(devices):
            block = got[s, 0 : z.rows, :].astype(F32)
            for c in range(COMPS):
                low = z.starts[band] + c * capacity
                stage[s * capacity : (s + 1) * capacity, c * LANES : (c + 1) * LANES] = block[
                    low : low + capacity, :
                ]
        turned = lambda x, by: pltpu.roll(x, (x.shape[1] - by) % x.shape[1], 1)[:, 0:LANES]
        rows = [turned(marks, at_mark + k * shift) for k in range(3)]
        for side in range(2):
            rows += [turned(sides[side], z.starts[band] + c * capacity) for c in range(COMPS)]
        at_mark += capacity
        place = iota((devices, places), 1)
        low = iota((devices, places), 0) * capacity
        mine = (place >= low) & (place < low + capacity)
        offset = jnp.sum(jnp.where(mine, place - low, 0), axis=0, keepdims=True)
        pick = ones_where(iota((LANES, places), 0) == offset)
        spread = dot(jnp.concatenate(rows, axis=0).astype(BF16), pick, NN)
        flat = [
            jnp.sum(jnp.where(mine, spread[k * devices : (k + 1) * devices], 0.0), axis=0, keepdims=True)
            for k in range(len(rows))
        ]
        lines = iota((map_lines, places), 0) + 1
        tables = [ones_where(lines == flat[k].astype(jnp.int32)) for k in range(3)]
        summed = dot(tables[0], stage[0:places, :].astype(BF16), NN)
        for c in range(COMPS):
            maps[band * COMPS + c] = summed[:, c * LANES : (c + 1) * LANES]
        for side in range(2):
            values = flat[3 + side * COMPS : 3 + (side + 1) * COMPS]
            values = jnp.concatenate(values + [jnp.zeros((SUB - COMPS, places), F32)], axis=0).astype(BF16)
            column = dot(values, tables[1 + side], NT)
            for c in range(COMPS):
                edges[side][band * COMPS + c] = column[c : c + 1, :]
    turned = []
    for side in range(2):
        joint = jnp.concatenate(coherency(*split_parts(lambda i: edges[side][i])), axis=0)
        turned.append(dot(small[...], joint, NN, HI))
    x = jnp.concatenate(turned, axis=0)
    high = x.astype(BF16)
    x = jnp.concatenate([high, (x - high.astype(F32)).astype(BF16)], axis=0)
    at = iota((4 * n_model, n_model * LANES), 0) % (2 * n_model)
    to = iota((4 * n_model, n_model * LANES), 1)
    target = jnp.where(at < n_model, at * LANES + LANES - 1, (at - n_model) * LANES)
    planes[...] = dot(x, ones_where(to == target), TN)

    ends = (0, map_lines - SUB)
    two[...] = fit_block(wide, maps, ends, n_model)
    for k in range(n_model):
        part = slice(k * LANES, (k + 1) * LANES)
        top = two[k * SUB : k * SUB + 1, 0:LANES]
        bottom = two[k * SUB + SUB - 1 : (k + 1) * SUB, LANES:]
        top = three_lanes(top, planes[0:1, part])
        bottom = three_lanes(bottom, planes[map_lines - 1 : map_lines, part])
        one, other = by_parity("sec", bottom, top)
        even_pairs[k : k + 1, :] = one
        odd_pairs[k : k + 1, :] = other


def fit_block(wide, maps, starts, n_model):
    halves = []
    for r in starts:
        x = jnp.concatenate(coherency(*split_parts(lambda n: maps[n, pl.ds(r, SUB), :])), axis=0)
        halves.append(x.astype(BF16))
    result = dot(wide[...], jnp.concatenate(halves, axis=1), NN)
    return result[0 : n_model * SUB] + result[n_model * SUB :]


def three_lanes(x, side):
    lane = iota(x.shape, 1)
    before = pltpu.roll(jnp.where(lane == LANES - 1, side, x), 1, 1)
    after = pltpu.roll(jnp.where(lane == 0, side, x), LANES - 1, 1)
    return x + before + after


def spread_kernel(z, maps, planes, wide, out, ends, fits):
    map_lines, n_model = z.map_lines, z.n_model
    for i in range(map_lines // (2 * SUB)):
        starts = (2 * i * SUB, (2 * i + 1) * SUB)
        result = fit_block(wide, maps, starts, n_model)
        for h, r in enumerate(starts):
            for k in range(n_model):
                fits[k, pl.ds(SUB + r, SUB), :] = result[
                    k * SUB : (k + 1) * SUB, h * LANES : (h + 1) * LANES
                ]
    blank = jnp.zeros((1, LANES), F32)
    inner = pl.ds(SUB, map_lines)
    for k in range(n_model):
        x = three_lanes(fits[k, inner, :], planes[:, k * LANES : (k + 1) * LANES])
        fits[k, inner, :] = x
        fits[k, SUB - 1 : SUB, :] = blank
        fits[k, SUB + map_lines : SUB + map_lines + 1, :] = blank
        x = fits[k, pl.ds(SUB - 1, map_lines), :] + x + fits[k, pl.ds(SUB + 1, map_lines), :]
        out[k] = x
        ends[0, k] = x[0:SUB]
        ends[1, k] = x[map_lines - SUB :]


def finish_kernel(z, given, ends, sec_a, sec_b, out, held, moving):
    del given
    below, above = by_parity("sec", sec_a[...], sec_b[...])
    line = iota((SUB, LANES), 0)
    copies = []
    for end, (at, row, start) in enumerate(((0, above, 0), (SUB - 1, below, z.map_lines - SUB))):
        for k in range(z.n_model):
            held[end, k] = ends[end, k] + jnp.where(line == at, row[k : k + 1, :], 0.0)
        copies.append(pltpu.make_async_copy(held.at[end], out.at[:, pl.ds(start, SUB), :], moving.at[end]))
        copies[-1].start()
    for copy in copies:
        copy.wait()


def body(radar_l, radar_s, weights_l, weights_s, owner_l, owner_s, slot_l, slot_s, models):
    z = Sizes(radar_l.shape[1], radar_s.shape[1], models.shape[0])
    lines_l, lines_s = z.lines
    shape = jax.ShapeDtypeStruct

    def call(kernel, args, shapes, mib, scratch=(), specs=None, flops=0, size=0):
        return pl.pallas_call(
            lambda *refs: kernel(z, *refs) if kernel is not matrix_kernel else kernel(*refs),
            in_specs=specs or [VMEM] * len(args),
            out_specs=[VMEM] * len(shapes),
            out_shape=shapes,
            scratch_shapes=scratch,
            compiler_params=params(mib),
            cost_estimate=pl.CostEstimate(flops=flops, bytes_accessed=size, transcendentals=0),
        )(*args)

    def call_one(kernel, args, specs, shapes, mib, scratch=(), aliases={}, flops=0, size=0):
        return pl.pallas_call(
            lambda *refs: kernel(z, *refs),
            grid=(1,),
            in_specs=specs,
            out_specs=[whole(x.shape) for x in shapes],
            out_shape=shapes,
            scratch_shapes=scratch,
            input_output_aliases=aliases,
            compiler_params=params(mib),
            cost_estimate=pl.CostEstimate(flops=flops, bytes_accessed=size, transcendentals=0),
        )(*args)

    row = lambda x: x.reshape(1, -1)
    radar = (radar_l, radar_s)
    column = shape((SUB, lines_l + lines_s), BF16)
    args = radar + (row(owner_l), slot_l, row(owner_s), slot_s)
    even, odd, base_l, base_s, marks = call_one(
        first_kernel,
        args,
        [ANY, ANY] + [whole(x.shape) for x in args[2:]],
        [column, column, shape((1, lines_l), jnp.int32), shape((1, lines_s), jnp.int32), shape((z.devices, LANES), F32)],
        58,
        scratch=[pltpu.VMEM(x.shape, BF16) for x in radar] + [pltpu.SemaphoreType.DMA((2,))],
        flops=10_000_000_000,
        size=1_000_000,
    )
    swap_a, swap_b = swap(even, odd, "swath")
    strip = shape((5 * SUB, LANES), BF16)
    tall = 2 * SUB
    edge = lambda lines, end: pl.BlockSpec(
        (COMPS, tall, LANES), lambda i: (0, end * (lines // tall - 1), 0)
    )
    edges = [edge(lines, end) for end in range(2) for lines in z.lines]
    side = whole(column.shape)
    even, odd = call_one(
        second_kernel, radar * 2 + (swap_a, swap_b), edges + [side, side], [strip, strip], 16, flops=1_000_000_000_000, size=1_000_000,
    )
    sec_a, sec_b = swap(even, odd, "sec")
    buffer = shape((z.devices * z.stride + up_to(COMPS * max(z.caps), SUB), LANES), F32)
    packed, edge_lines, edge_tiles = call(
        send_kernel,
        (base_l, base_s, radar_l, radar_s, swap_a, swap_b, weights_l, weights_s),
        [
            buffer,
            shape((2, 2, COMPS, tall, LANES), BF16),
            shape((2, 2, LANES, LANES), BF16),
        ],
        34,
        specs=[SMEM, SMEM] + [VMEM] * 4 + [ANY, VMEM],
        scratch=[
            *[pltpu.VMEM((3 + COMPS, n + 2 * SUB, LANES), F32) for n in z.lines],
            *[pltpu.VMEM((n * SUB, LANES), F32) for n in z.lines],
            pltpu.VMEM(weights_l.shape, BF16),
            pltpu.SemaphoreType.DMA((lines_l // z.part,)),
        ],
        flops=10_000_000_000,
        size=2 * (weights_l.size + weights_s.size),
    )
    args = (base_l, base_s, packed, sec_a, sec_b, swap_a, swap_b, marks, edge_lines, edge_tiles)
    sent, _ = pl.pallas_call(
        lambda *refs: tail_kernel(z, *refs),
        in_specs=[SMEM, SMEM] + [VMEM] * 8,
        out_specs=[ANY, VMEM],
        out_shape=[shape((z.devices, z.rows + SUB, LANES), BF16), buffer],
        scratch_shapes=[pltpu.VMEM((z.devices, z.rows + SUB, LANES), BF16), pltpu.SemaphoreType.DMA((4,))],
        input_output_aliases={2: 1},
        compiler_params=params(24),
    )(*args)
    got = lax.all_to_all(sent, AXES, split_axis=0, concat_axis=0, tiled=True)

    small, wide = call(
        matrix_kernel,
        (models,),
        [shape((z.n_model, CHANNELS), F32), shape((2 * z.n_model * SUB, CHANNELS * SUB), BF16)],
        16, flops=50_000_000, size=1_000_000,
    )
    rim = shape((z.n_model, LANES), F32)
    maps, planes, even, odd = call(
        merge_kernel,
        (got, small, wide),
        [
            shape((2 * COMPS, z.map_lines, LANES), F32),
            shape((z.map_lines, z.n_model * LANES), F32),
            rim,
            rim,
        ],
        24,
        scratch=[
            pltpu.VMEM((z.devices * max(z.caps), COMPS * LANES), F32),
            pltpu.VMEM((z.devices * SUB, LANES), F32),
            pltpu.VMEM((z.n_model * SUB, 2 * LANES), F32),
        ],
        flops=1_000_000_000,
        size=4_000_000,
    )
    sec_a, sec_b = swap(even, odd, "sec")
    edge = shape((2, z.n_model, SUB, LANES), F32)
    fit, ends = call(
        spread_kernel,
        (maps, planes, wide),
        [shape((z.n_model, z.map_lines, LANES), F32), edge],
        24,
        scratch=[pltpu.VMEM((z.n_model, z.map_lines + 2 * SUB, LANES), F32)],
        flops=10_000_000_000,
        size=4_000_000,
    )
    return pl.pallas_call(
        lambda *refs: finish_kernel(z, *refs),
        in_specs=[ANY, VMEM, VMEM, VMEM],
        out_specs=ANY,
        out_shape=shape(fit.shape, F32),
        scratch_shapes=[pltpu.VMEM(edge.shape, F32), pltpu.SemaphoreType.DMA((2,))],
        input_output_aliases={0: 0},
        compiler_params=params(16),
    )(fit, ends, sec_a, sec_b)


def solution(mesh):
    in_specs = (
        P(None, "sec", "swath"),
        P(None, "sec", "swath"),
        P(("sec", "swath"), None, None),
        P(("sec", "swath"), None, None),
        P(("sec", "swath"), None),
        P(("sec", "swath"), None),
        P(("sec", "swath")),
        P(("sec", "swath")),
        P(),
    )
    out_specs = P(None, "sec", "swath")
    return jax.shard_map(body, mesh=mesh, in_specs=in_specs, out_specs=out_specs, check_vma=False)
```

```python
import jax
import jax.numpy as jnp
from jax import lax
from jax.experimental import pallas as pl
from jax.experimental.pallas import tpu as pltpu
from jax.sharding import PartitionSpec as P

FIT_ITERS = 4
AXES = ("sec", "swath")

cu_square = 0.25
fit_rate = 0.25
upper_pairs = [(first, second) for first in range(6) for second in range(first, 6)]
strict_pairs = [(first, second) for first in range(6) for second in range(first + 1, 6)]
CHANNELS = len(upper_pairs) + len(strict_pairs)
COMPS = 6
NT = (((1,), (1,)), ((), ()))
NN = (((1,), (0,)), ((), ()))
TN = (((0,), (0,)), ((), ()))
HI = lax.Precision.HIGHEST
F32 = jnp.float32
BF16 = jnp.bfloat16
SUB = 8
LANES = 128
EXTRA = 5


def params(mib):
    return pltpu.CompilerParams(vmem_limit_bytes=mib << 20)


def iota(shape, dim):
    return lax.broadcasted_iota(jnp.int32, shape, dim)


def dot(a, b, dims, precision=None):
    return lax.dot_general(a, b, dims, precision=precision, preferred_element_type=F32)


def ones_where(mask, dtype=BF16):
    return jnp.where(mask, 1.0, 0.0).astype(dtype)


def swap(even_pairs, odd_pairs, axis):
    peers = lax.axis_size(axis)
    pairs = lambda start: [p for i in range(start, peers - 1, 2) for p in ((i, i + 1), (i + 1, i))]
    return lax.ppermute(even_pairs, axis, pairs(0)), lax.ppermute(odd_pairs, axis, pairs(1))


def by_parity(axis, one, other):
    even = lax.axis_index(axis) % 2 == 0
    return jnp.where(even, one, other), jnp.where(even, other, one)


VMEM = pl.BlockSpec(memory_space=pltpu.VMEM)
SMEM = pl.BlockSpec(memory_space=pltpu.SMEM)
ANY = pl.BlockSpec(memory_space=pl.ANY)


def whole(shape):
    return pl.BlockSpec(shape, lambda i: (0,) * len(shape))


def up_to(n, multiple):
    return -(-n // multiple) * multiple


class Sizes:
    def __init__(self, lines_l, map_lines, n_model):
        self.devices = lax.axis_size(AXES)
        self.swath = lax.axis_size("swath")
        self.lines = (lines_l, map_lines)
        self.map_lines = map_lines
        self.n_model = n_model
        self.caps = tuple(max(2, 2 * lines // self.devices) for lines in self.lines)
        self.starts = (0, COMPS * self.caps[0])
        self.rows = up_to(COMPS * sum(self.caps), SUB)
        self.stride = up_to(self.rows + SUB, LANES)
        self.lanes = up_to(self.rows, LANES)
        self.part = 64 if lines_l % 64 == 0 and map_lines % 64 == 0 else 2


def first_kernel(
    z, radar_l, radar_s, owner_l, slot_l, owner_s, slot_s, even_pairs, odd_pairs, base_l, base_s, marks,
    held_l, held_s, arrived,
):
    copies = [
        pltpu.make_async_copy(source, held, arrived.at[k])
        for k, (source, held) in enumerate(((radar_l, held_l), (radar_s, held_s)))
    ]
    for copy in copies:
        copy.start()
    plan(z, owner_l, slot_l, owner_s, slot_s, base_l, base_s, marks)
    shape = (2 * SUB, COMPS * LANES)
    row, at = iota(shape, 0), iota(shape, 1)
    pick = ones_where(at == jnp.where(row < SUB, row * LANES, (row - SUB) * LANES + LANES - 1))
    start = 0
    for radar, lines, copy in zip((held_l, held_s), z.lines, copies):
        copy.wait()
        rows = jnp.concatenate([radar[c] for c in range(COMPS)], axis=1)
        both = dot(pick, rows, NT)
        one, other = by_parity("swath", both[SUB:], both[0:SUB])
        even_pairs[:, start : start + lines] = one.astype(BF16)
        odd_pairs[:, start : start + lines] = other.astype(BF16)
        start += lines


def plan(z, owner_l, slot_l, owner_s, slot_s, base_l, base_s, marks):
    total = jnp.zeros((z.devices, LANES), F32)
    shift = 0
    for band, (owner, slot, base) in enumerate(((owner_l, slot_l, base_l), (owner_s, slot_s, base_s))):
        tiles = z.lines[band]
        hit = iota((z.devices, tiles), 0) == owner[...]
        earlier = ones_where(iota((tiles, tiles), 0) < iota((tiles, tiles), 1))
        before = dot(ones_where(hit), earlier, NN)
        rank = jnp.sum(jnp.where(hit, before, 0.0), axis=0, keepdims=True).astype(jnp.int32)
        base[...] = owner[...] * z.stride + z.starts[band] + rank
        line = jnp.where(hit, slot[...].reshape(1, tiles) + 1, 0).astype(F32).astype(BF16)
        place = ones_where(iota((LANES, tiles), 0) == rank + shift)
        total = total + dot(line, place, NT)
        shift += z.caps[band]
    me, other = iota((z.devices, z.devices), 0), iota((z.devices, z.devices), 1)
    inner = me % z.swath
    own = total.astype(BF16)
    before = dot(ones_where((other == me - 1) & (inner > 0)), own, NN)
    after = dot(ones_where((other == me + 1) & (inner < z.swath - 1)), own, NN)
    marks[...] = total + pltpu.roll(before, shift, 1) + pltpu.roll(after, 2 * shift, 1)


def second_kernel(z, top_l, top_s, bottom_l, bottom_s, swap_a, swap_b, even_pairs, odd_pairs):
    after, before = by_parity("swath", swap_a[...].astype(F32), swap_b[...].astype(F32))
    strips = []
    lines_l, lines_s = z.lines
    ends = (
        (top_l, top_s, 0, 0, lines_l),
        (bottom_l, bottom_s, top_l.shape[1] - 1, lines_l - 1, lines_l + lines_s - 1),
    )
    for rows_l, rows_s, row, at_l, at_s in ends:
        parts = [rows_l[...].astype(F32)[:, row, :], rows_s[...].astype(F32)[:, row, :]]
        for side in (before, after):
            for at in (at_l, at_s):
                column = side[0:COMPS, at : at + 1]
                parts.append(jnp.broadcast_to(column, (COMPS, LANES)))
        parts.append(jnp.zeros((even_pairs.shape[0] - 6 * COMPS, LANES), F32))
        strips.append(jnp.concatenate(parts, axis=0))
    one, other = by_parity("sec", strips[1], strips[0])
    even_pairs[...] = one.astype(BF16)
    odd_pairs[...] = other.astype(BF16)


def with_sides(x, left, right):
    lane = iota(x.shape, 1)
    width = x.shape[1]
    before = jnp.where(lane == 0, left, pltpu.roll(x, 1, 1))
    after = jnp.where(lane == width - 1, right, pltpu.roll(x, width - 1, 1))
    return before, after


def filter_planes(tiles, radar, halo, planes):
    inner = pl.ds(SUB, tiles)
    blank = jnp.zeros((1, LANES), F32)
    for plane in range(3 + COMPS):
        planes[plane, SUB - 1 : SUB, :] = blank
        planes[plane, SUB + tiles : SUB + tiles + 1, :] = blank
    total = jnp.zeros((tiles, LANES), F32)
    beside = jnp.zeros((tiles, LANES), F32)
    for c in range(COMPS):
        x = radar[c].astype(F32)
        side = halo[:, c * LANES : (c + 1) * LANES]
        total = total + x * x
        beside = beside + side * side
        before, after = neighbours(x, side)
        planes[3 + c, inner, :] = x + before + after
    for plane, value in enumerate((total,) + neighbours(total, beside)):
        planes[plane, inner, :] = value


def filter_lines(start, lines, radar, planes, filtered):
    at = lambda plane, shift: planes[plane, pl.ds(SUB + start + shift, lines), :]
    gain = gain_of([at(plane, d) for plane in range(3) for d in (-1, 0, 1)])
    for c in range(COMPS):
        mean = (at(3 + c, -1) + at(3 + c, 0) + at(3 + c, 1)) / 9.0
        x = radar[c, pl.ds(start, lines), :].astype(F32)
        filtered[pl.ds(start * SUB + c, lines, stride=SUB), :] = mean + gain * (x - mean)


def gain_of(near):
    mean_power = sum(near[1:], near[0]) / 9.0
    spread = jnp.zeros_like(mean_power)
    for q in near:
        spread = spread + (q - mean_power) ** 2
    spread = spread / 9.0
    return spread / (spread + cu_square * mean_power * mean_power + 1.0)


def send_kernel(
    z, base_l, base_s, radar_l, radar_s, swap_a, swap_b, weights_l, weights_s,
    packed, edge_lines, edge_tiles, planes_l, planes_s, filtered_l, filtered_s, held_l, arrived,
):
    copies = []
    for at in range(0, z.lines[0], z.part):
        part = pl.ds(at, z.part)
        copies.append(pltpu.make_async_copy(weights_l.at[part], held_l.at[part], arrived.at[len(copies)]))
        copies[-1].start()
    packed[...] = jnp.zeros_like(packed)
    tall = edge_lines.shape[3]
    for band, radar in enumerate((radar_l, radar_s)):
        edge_lines[band, 0] = radar[:, 0:tall, :]
        edge_lines[band, 1] = radar[:, z.lines[band] - tall :, :]
    after, before = by_parity("swath", swap_a[...].astype(F32), swap_b[...].astype(F32))
    sides = jnp.concatenate([before, after], axis=0).astype(BF16)
    column, to = iota((2 * SUB, COMPS * LANES), 0), iota((2 * SUB, COMPS * LANES), 1)
    target = jnp.where(column < SUB, column * LANES + LANES - 1, (column - SUB) * LANES)
    target = ones_where((to == target) & (column % SUB < COMPS))
    bands = (
        (radar_l, base_l, held_l, planes_l, filtered_l),
        (radar_s, base_s, weights_s, planes_s, filtered_s),
    )
    at = (0, z.lines[0])
    for band in (1, 0):
        radar, _, _, planes, _ = bands[band]
        part = slice(at[band], at[band] + z.lines[band])
        filter_planes(z.lines[band], radar, dot(sides[:, part], target, TN), planes)
    todo = [(band, start) for band in (1, 0) for start in range(0, z.lines[band], z.part)]

    def lines_of(band, start):
        radar, _, _, planes, filtered = bands[band]
        filter_lines(start, z.part, radar, planes, filtered)

    lines_of(*todo[0])
    for i, (band, start) in enumerate(todo):
        _, base, held, _, filtered = bands[band]
        if band == 0:
            copies[start // z.part].wait()
        if i + 1 < len(todo):
            lines_of(*todo[i + 1])
        for tile in range(start, start + z.part, 2):
            lines = filtered[pl.ds(tile * SUB, 2 * SUB), :].astype(BF16)
            matrix = held[pl.ds(tile, 2)].reshape(2 * LANES, LANES)
            result = dot(lines, matrix, NT)
            first, second = base[0, tile], base[0, tile + 1]
            packed[pl.ds(first, COMPS, stride=z.caps[band]), :] = result[0:COMPS, 0:LANES]
            packed[pl.ds(second, COMPS, stride=z.caps[band]), :] = result[SUB : SUB + COMPS, LANES:]
    for band, (_, _, held, _, _) in enumerate(bands):
        edge_tiles[band, 0] = held[0]
        edge_tiles[band, 1] = held[z.lines[band] - 1]


def tail_kernel(
    z, base_l, base_s, given, sec_a, sec_b, swap_a, swap_b, marks,
    lines_held, tiles_held, sent, packed, out, leaving,
):
    del given
    tall = lines_held.shape[3]
    after, before = by_parity("swath", swap_a[...].astype(F32), swap_b[...].astype(F32))
    down, up = by_parity("sec", sec_a[...].astype(F32), sec_b[...].astype(F32))
    shift = 0
    for band, base in enumerate((base_l, base_s)):
        lines = z.lines[band]
        for end in range(2):
            rows = lines_held[band, end].astype(F32)
            strip = (up, down)[end]
            first = 0 if end == 0 else lines - 2
            near_row = 0 if end == 0 else tall - 2
            columns = (before, after)
            values, sides = [], [[], []]
            for c in range(COMPS):
                row = band * COMPS + c
                far = strip[row : row + 1]
                near = rows[c, near_row : near_row + 2]
                values.append(jnp.concatenate([far, near] if end == 0 else [near, far], axis=0))
                for side in range(2):
                    corner = 2 * COMPS * (1 + side) + row
                    far = strip[corner : corner + 1, 0:1]
                    near = [
                        columns[side][c : c + 1, shift + first + k : shift + first + k + 1]
                        for k in range(2)
                    ]
                    sides[side].append(jnp.concatenate([far] + near if end == 0 else near + [far], axis=0))
            squares = lambda parts: sum(v * v for v in parts)
            power = squares(values)
            planes = (power,) + with_sides(power, squares(sides[0]), squares(sides[1]))
            gain = gain_of([plane[k : k + 1] for plane in planes for k in range(3)])
            lines_out = []
            for c in range(COMPS):
                left, right = with_sides(values[c], sides[0][c], sides[1][c])
                total = values[c] + left + right
                mean = (total[0:1] + total[1:2] + total[2:3]) / 9.0
                lines_out.append(mean + gain * (values[c][1:2] - mean))
            lines_out.append(jnp.zeros((SUB - COMPS, LANES), F32))
            result = dot(jnp.concatenate(lines_out, axis=0).astype(BF16), tiles_held[band, end], NT)
            target = base[0, 0 if end == 0 else lines - 1]
            packed[pl.ds(target, COMPS, stride=z.caps[band]), :] = result[0:COMPS]
        shift += lines

    steps = z.lanes // LANES
    row, lane = iota((SUB, LANES), 0), iota((SUB, LANES), 1)
    pick = ones_where(
        ((row >= 1) & (row <= steps) & (lane == LANES - 1)) | ((row > steps) & (row <= 2 * steps) & (lane == 0))
    )
    columns = [
        dot(pick, packed[o * z.stride : o * z.stride + z.lanes, :].astype(BF16), NT) for o in range(z.devices)
    ]
    group, copies = z.devices // 4, []
    for o in range(z.devices):
        extra = jnp.broadcast_to(marks[o : o + 1, :], (SUB, LANES))
        one_less, one_more = max(o - 1, 0), min(o + 1, z.devices - 1)
        for k in range(steps):
            part = slice(k * LANES, (k + 1) * LANES)
            extra = jnp.where(row == 1 + k, columns[one_less][:, part], extra)
            extra = jnp.where(row == 1 + steps + k, columns[one_more][:, part], extra)
        out[o, 0 : z.rows, :] = packed[o * z.stride : o * z.stride + z.rows, :].astype(BF16)
        out[o, z.rows :, :] = extra.astype(BF16)
        if (o + 1) % group == 0:
            part = pl.ds(o + 1 - group, group)
            copies.append(pltpu.make_async_copy(out.at[part], sent.at[part], leaving.at[o // group]))
            copies[-1].start()
    for copy in copies:
        copy.wait()


def matrix_kernel(models, small, wide):
    m = models[...]
    n_model = m.shape[0]
    eye = ones_where(iota((CHANNELS, CHANNELS), 0) == iota((CHANNELS, CHANNELS), 1), F32)
    powers = jnp.zeros(m.shape, F32)
    for _ in range(FIT_ITERS):
        predicted = dot(m, powers, TN, HI)
        powers = powers + fit_rate * dot(m, eye - predicted, NN, HI)
    powers = powers / 9.0
    small[...] = powers
    rows, columns = wide.shape[0] // 2, wide.shape[1]
    left = ones_where(iota((rows, n_model), 0) // SUB == iota((rows, n_model), 1), F32)
    right = ones_where(iota((CHANNELS, columns), 1) // SUB == iota((CHANNELS, columns), 0), F32)
    spread = dot(dot(left, powers, NN, HI), right, NN, HI)
    same = iota((rows, columns), 0) % SUB == iota((rows, columns), 1) % SUB
    spread = jnp.where(same, spread, 0.0)
    high = spread.astype(BF16)
    low = (spread - high.astype(F32)).astype(BF16)
    wide[...] = jnp.concatenate([high, low], axis=0)


def coherency(real, imag):
    joint = [real[f] * real[g] + imag[f] * imag[g] for f, g in upper_pairs]
    return joint + [imag[f] * real[g] - real[f] * imag[g] for f, g in strict_pairs]


def split_parts(maps):
    pick = lambda at: [maps(band * COMPS + at + c) for band in range(2) for c in range(3)]
    return pick(0), pick(3)


def merge_kernel(z, got, small, wide, maps, planes, even_pairs, odd_pairs, stage, extras, two):
    map_lines, n_model, devices = z.map_lines, z.n_model, z.devices
    steps = z.lanes // LANES
    for s in range(devices):
        extras[s * SUB : (s + 1) * SUB, :] = got[s, z.rows : z.rows + SUB, :].astype(F32)
    piece = lambda r: extras[pl.ds(r, devices, stride=SUB), :]
    marks = piece(0)
    sides = [
        jnp.concatenate([piece(1 + side * steps + k) for k in range(steps)], axis=1) for side in range(2)
    ]
    shift = sum(z.caps)
    edges = [[None] * (2 * COMPS) for _ in range(2)]
    at_mark = 0
    for band in range(2):
        capacity = z.caps[band]
        places = devices * capacity
        for s in range(devices):
            block = got[s, 0 : z.rows, :].astype(F32)
            for c in range(COMPS):
                low = z.starts[band] + c * capacity
                stage[s * capacity : (s + 1) * capacity, c * LANES : (c + 1) * LANES] = block[
                    low : low + capacity, :
                ]
        turned = lambda x, by: pltpu.roll(x, (x.shape[1] - by) % x.shape[1], 1)[:, 0:LANES]
        rows = [turned(marks, at_mark + k * shift) for k in range(3)]
        for side in range(2):
            rows += [turned(sides[side], z.starts[band] + c * capacity) for c in range(COMPS)]
        at_mark += capacity
        place = iota((devices, places), 1)
        low = iota((devices, places), 0) * capacity
        mine = (place >= low) & (place < low + capacity)
        offset = jnp.sum(jnp.where(mine, place - low, 0), axis=0, keepdims=True)
        pick = ones_where(iota((LANES, places), 0) == offset)
        spread = dot(jnp.concatenate(rows, axis=0).astype(BF16), pick, NN)
        flat = [
            jnp.sum(jnp.where(mine, spread[k * devices : (k + 1) * devices], 0.0), axis=0, keepdims=True)
            for k in range(len(rows))
        ]
        lines = iota((map_lines, places), 0) + 1
        tables = [ones_where(lines == flat[k].astype(jnp.int32)) for k in range(3)]
        summed = dot(tables[0], stage[0:places, :].astype(BF16), NN)
        for c in range(COMPS):
            maps[band * COMPS + c] = summed[:, c * LANES : (c + 1) * LANES]
        for side in range(2):
            values = flat[3 + side * COMPS : 3 + (side + 1) * COMPS]
            values = jnp.concatenate(values + [jnp.zeros((SUB - COMPS, places), F32)], axis=0).astype(BF16)
            column = dot(values, tables[1 + side], NT)
            for c in range(COMPS):
                edges[side][band * COMPS + c] = column[c : c + 1, :]
    turned = []
    for side in range(2):
        joint = jnp.concatenate(coherency(*split_parts(lambda i: edges[side][i])), axis=0)
        turned.append(dot(small[...], joint, NN, HI))
    x = jnp.concatenate(turned, axis=0)
    high = x.astype(BF16)
    x = jnp.concatenate([high, (x - high.astype(F32)).astype(BF16)], axis=0)
    at = iota((4 * n_model, n_model * LANES), 0) % (2 * n_model)
    to = iota((4 * n_model, n_model * LANES), 1)
    target = jnp.where(at < n_model, at * LANES + LANES - 1, (at - n_model) * LANES)
    planes[...] = dot(x, ones_where(to == target), TN)

    ends = (0, map_lines - SUB)
    two[...] = fit_block(wide, maps, ends, n_model)
    for k in range(n_model):
        part = slice(k * LANES, (k + 1) * LANES)
        top = two[k * SUB : k * SUB + 1, 0:LANES]
        bottom = two[k * SUB + SUB - 1 : (k + 1) * SUB, LANES:]
        top = three_lanes(top, planes[0:1, part])
        bottom = three_lanes(bottom, planes[map_lines - 1 : map_lines, part])
        one, other = by_parity("sec", bottom, top)
        even_pairs[k : k + 1, :] = one
        odd_pairs[k : k + 1, :] = other


def fit_block(wide, maps, starts, n_model):
    halves = []
    for r in starts:
        x = jnp.concatenate(coherency(*split_parts(lambda n: maps[n, pl.ds(r, SUB), :])), axis=0)
        halves.append(x.astype(BF16))
    result = dot(wide[...], jnp.concatenate(halves, axis=1), NN)
    return result[0 : n_model * SUB] + result[n_model * SUB :]


def neighbours(x, side):
    lane = iota(x.shape, 1)
    before = pltpu.roll(jnp.where(lane == LANES - 1, side, x), 1, 1)
    return before, pltpu.roll(jnp.where(lane == 0, side, x), LANES - 1, 1)


def three_lanes(x, side):
    before, after = neighbours(x, side)
    return x + before + after


def spread_kernel(z, maps, planes, wide, out, ends, fits, done, leaving):
    map_lines, n_model = z.map_lines, z.n_model
    for i in range(map_lines // (2 * SUB)):
        starts = (2 * i * SUB, (2 * i + 1) * SUB)
        result = fit_block(wide, maps, starts, n_model)
        for h, r in enumerate(starts):
            for k in range(n_model):
                fits[k, pl.ds(SUB + r, SUB), :] = result[
                    k * SUB : (k + 1) * SUB, h * LANES : (h + 1) * LANES
                ]
    blank = jnp.zeros((1, LANES), F32)
    inner = pl.ds(SUB, map_lines)
    copies = []
    for k in range(n_model):
        x = three_lanes(fits[k, inner, :], planes[:, k * LANES : (k + 1) * LANES])
        fits[k, inner, :] = x
        fits[k, SUB - 1 : SUB, :] = blank
        fits[k, SUB + map_lines : SUB + map_lines + 1, :] = blank
        x = fits[k, pl.ds(SUB - 1, map_lines), :] + x + fits[k, pl.ds(SUB + 1, map_lines), :]
        done[k] = x
        copies.append(pltpu.make_async_copy(done.at[k], out.at[k], leaving.at[k]))
        copies[-1].start()
        ends[0, k] = x[0:SUB]
        ends[1, k] = x[map_lines - SUB :]
    for copy in copies:
        copy.wait()


def finish_kernel(z, given, ends, sec_a, sec_b, out, held, moving):
    del given
    below, above = by_parity("sec", sec_a[...], sec_b[...])
    line = iota((SUB, LANES), 0)
    copies = []
    for end, (at, row, start) in enumerate(((0, above, 0), (SUB - 1, below, z.map_lines - SUB))):
        for k in range(z.n_model):
            held[end, k] = ends[end, k] + jnp.where(line == at, row[k : k + 1, :], 0.0)
        copies.append(pltpu.make_async_copy(held.at[end], out.at[:, pl.ds(start, SUB), :], moving.at[end]))
        copies[-1].start()
    for copy in copies:
        copy.wait()


def body(radar_l, radar_s, weights_l, weights_s, owner_l, owner_s, slot_l, slot_s, models):
    z = Sizes(radar_l.shape[1], radar_s.shape[1], models.shape[0])
    lines_l, lines_s = z.lines
    shape = jax.ShapeDtypeStruct

    def call(kernel, args, shapes, mib, scratch=(), specs=None, outs=None, flops=0, size=0):
        return pl.pallas_call(
            lambda *refs: kernel(z, *refs) if kernel is not matrix_kernel else kernel(*refs),
            in_specs=specs or [VMEM] * len(args),
            out_specs=outs or [VMEM] * len(shapes),
            out_shape=shapes,
            scratch_shapes=scratch,
            compiler_params=params(mib),
            cost_estimate=pl.CostEstimate(flops=flops, bytes_accessed=size, transcendentals=0),
        )(*args)

    def call_one(kernel, args, specs, shapes, mib, scratch=(), aliases={}, flops=0, size=0):
        return pl.pallas_call(
            lambda *refs: kernel(z, *refs),
            grid=(1,),
            in_specs=specs,
            out_specs=[whole(x.shape) for x in shapes],
            out_shape=shapes,
            scratch_shapes=scratch,
            input_output_aliases=aliases,
            compiler_params=params(mib),
            cost_estimate=pl.CostEstimate(flops=flops, bytes_accessed=size, transcendentals=0),
        )(*args)

    row = lambda x: x.reshape(1, -1)
    radar = (radar_l, radar_s)
    column = shape((SUB, lines_l + lines_s), BF16)
    args = radar + (row(owner_l), slot_l, row(owner_s), slot_s)
    even, odd, base_l, base_s, marks = call_one(
        first_kernel,
        args,
        [ANY, ANY] + [whole(x.shape) for x in args[2:]],
        [column, column, shape((1, lines_l), jnp.int32), shape((1, lines_s), jnp.int32), shape((z.devices, LANES), F32)],
        58,
        scratch=[pltpu.VMEM(x.shape, BF16) for x in radar] + [pltpu.SemaphoreType.DMA((2,))],
        flops=10_000_000_000,
        size=1_000_000,
    )
    swap_a, swap_b = swap(even, odd, "swath")
    strip = shape((5 * SUB, LANES), BF16)
    tall = 2 * SUB
    edge = lambda lines, end: pl.BlockSpec(
        (COMPS, tall, LANES), lambda i: (0, end * (lines // tall - 1), 0)
    )
    edges = [edge(lines, end) for end in range(2) for lines in z.lines]
    side = whole(column.shape)
    even, odd = call_one(
        second_kernel, radar * 2 + (swap_a, swap_b), edges + [side, side], [strip, strip], 16, flops=1_000_000_000_000, size=1_000_000,
    )
    sec_a, sec_b = swap(even, odd, "sec")
    buffer = shape((z.devices * z.stride + up_to(COMPS * max(z.caps), SUB), LANES), F32)
    packed, edge_lines, edge_tiles = call(
        send_kernel,
        (base_l, base_s, radar_l, radar_s, swap_a, swap_b, weights_l, weights_s),
        [
            buffer,
            shape((2, 2, COMPS, tall, LANES), BF16),
            shape((2, 2, LANES, LANES), BF16),
        ],
        34,
        specs=[SMEM, SMEM] + [VMEM] * 4 + [ANY, VMEM],
        scratch=[
            *[pltpu.VMEM((3 + COMPS, n + 2 * SUB, LANES), F32) for n in z.lines],
            *[pltpu.VMEM((n * SUB, LANES), F32) for n in z.lines],
            pltpu.VMEM(weights_l.shape, BF16),
            pltpu.SemaphoreType.DMA((lines_l // z.part,)),
        ],
        flops=10_000_000_000,
        size=2 * (weights_l.size + weights_s.size),
    )
    args = (base_l, base_s, packed, sec_a, sec_b, swap_a, swap_b, marks, edge_lines, edge_tiles)
    sent, _ = pl.pallas_call(
        lambda *refs: tail_kernel(z, *refs),
        in_specs=[SMEM, SMEM] + [VMEM] * 8,
        out_specs=[ANY, VMEM],
        out_shape=[shape((z.devices, z.rows + SUB, LANES), BF16), buffer],
        scratch_shapes=[pltpu.VMEM((z.devices, z.rows + SUB, LANES), BF16), pltpu.SemaphoreType.DMA((4,))],
        input_output_aliases={2: 1},
        compiler_params=params(24),
    )(*args)
    got = lax.all_to_all(sent, AXES, split_axis=0, concat_axis=0, tiled=True)

    small, wide = call(
        matrix_kernel,
        (models,),
        [shape((z.n_model, CHANNELS), F32), shape((2 * z.n_model * SUB, CHANNELS * SUB), BF16)],
        16, flops=50_000_000, size=1_000_000,
    )
    rim = shape((z.n_model, LANES), F32)
    maps, planes, even, odd = call(
        merge_kernel,
        (got, small, wide),
        [
            shape((2 * COMPS, z.map_lines, LANES), F32),
            shape((z.map_lines, z.n_model * LANES), F32),
            rim,
            rim,
        ],
        24,
        scratch=[
            pltpu.VMEM((z.devices * max(z.caps), COMPS * LANES), F32),
            pltpu.VMEM((z.devices * SUB, LANES), F32),
            pltpu.VMEM((z.n_model * SUB, 2 * LANES), F32),
        ],
        flops=1_000_000_000,
        size=4_000_000,
    )
    sec_a, sec_b = swap(even, odd, "sec")
    edge = shape((2, z.n_model, SUB, LANES), F32)
    fit, ends = call(
        spread_kernel,
        (maps, planes, wide),
        [shape((z.n_model, z.map_lines, LANES), F32), edge],
        24,
        scratch=[
            pltpu.VMEM((z.n_model, z.map_lines + 2 * SUB, LANES), F32),
            pltpu.VMEM((z.n_model, z.map_lines, LANES), F32),
            pltpu.SemaphoreType.DMA((z.n_model,)),
        ],
        outs=[ANY, VMEM],
        flops=10_000_000_000,
        size=4_000_000,
    )
    return pl.pallas_call(
        lambda *refs: finish_kernel(z, *refs),
        in_specs=[ANY, VMEM, VMEM, VMEM],
        out_specs=ANY,
        out_shape=shape(fit.shape, F32),
        scratch_shapes=[pltpu.VMEM(edge.shape, F32), pltpu.SemaphoreType.DMA((2,))],
        input_output_aliases={0: 0},
        compiler_params=params(16),
    )(fit, ends, sec_a, sec_b)


def solution(mesh):
    in_specs = (
        P(None, "sec", "swath"),
        P(None, "sec", "swath"),
        P(("sec", "swath"), None, None),
        P(("sec", "swath"), None, None),
        P(("sec", "swath"), None),
        P(("sec", "swath"), None),
        P(("sec", "swath")),
        P(("sec", "swath")),
        P(),
    )
    out_specs = P(None, "sec", "swath")
    return jax.shard_map(body, mesh=mesh, in_specs=in_specs, out_specs=out_specs, check_vma=False)
```

```python
import jax
import jax.numpy as jnp
from jax import lax
from jax.experimental import pallas as pl
from jax.experimental.pallas import tpu as pltpu
from jax.sharding import PartitionSpec as P


FIT_ITERS = 4
AXES = ("sec", "swath")

cu_square = 0.25
fit_rate = 0.25
upper_pairs = [(first, second) for first in range(6) for second in range(first, 6)]
strict_pairs = [(first, second) for first in range(6) for second in range(first + 1, 6)]
CHANNELS = len(upper_pairs) + len(strict_pairs)
COMPS = 6
NT = (((1,), (1,)), ((), ()))
NN = (((1,), (0,)), ((), ()))
TN = (((0,), (0,)), ((), ()))
HI = lax.Precision.HIGHEST
F32 = jnp.float32
BF16 = jnp.bfloat16
SUB = 8
LANES = 128


def params(mib):
    return pltpu.CompilerParams(vmem_limit_bytes=mib << 20)


def iota(shape, dim):
    return lax.broadcasted_iota(jnp.int32, shape, dim)


def dot(a, b, dims, precision=None):
    return lax.dot_general(a, b, dims, precision=precision, preferred_element_type=F32)


def ones_where(mask, dtype=BF16):
    return jnp.where(mask, 1.0, 0.0).astype(dtype)


def swap(even_pairs, odd_pairs, axis):
    peers = lax.axis_size(axis)
    pairs = lambda start: [p for i in range(start, peers - 1, 2) for p in ((i, i + 1), (i + 1, i))]
    odd = lax.ppermute(odd_pairs, axis, pairs(1))
    even = lax.ppermute(even_pairs, axis, pairs(0))
    return even, odd


def by_parity(axis, one, other):
    even = lax.axis_index(axis) % 2 == 0
    return jnp.where(even, one, other), jnp.where(even, other, one)


VMEM = pl.BlockSpec(memory_space=pltpu.VMEM)
SMEM = pl.BlockSpec(memory_space=pltpu.SMEM)
ANY = pl.BlockSpec(memory_space=pl.ANY)


def whole(shape):
    return pl.BlockSpec(shape, lambda i: (0,) * len(shape))


def up_to(n, multiple):
    return -(-n // multiple) * multiple


class Sizes:
    def __init__(self, lines_l, map_lines, n_model):
        self.devices = lax.axis_size(AXES)
        self.swath = lax.axis_size("swath")
        self.lines = (lines_l, map_lines)
        self.map_lines = map_lines
        self.n_model = n_model
        self.caps = tuple(max(2, 2 * lines // self.devices) for lines in self.lines)
        self.starts = (0, COMPS * self.caps[0])
        self.rows = up_to(COMPS * sum(self.caps), SUB)
        self.stride = up_to(self.rows + SUB, LANES)
        self.lanes = up_to(self.rows, LANES)
        self.part = 64 if lines_l % 64 == 0 and map_lines % 64 == 0 else 2


def first_kernel(z, radar_l, radar_s, even_pairs, odd_pairs):
    shape = (2 * SUB, COMPS * LANES)
    row, at = iota(shape, 0), iota(shape, 1)
    pick = ones_where(at == jnp.where(row < SUB, row * LANES, (row - SUB) * LANES + LANES - 1))
    start = 0
    for radar, lines in zip((radar_l, radar_s), z.lines):
        rows = jnp.concatenate([radar[c] for c in range(COMPS)], axis=1)
        both = dot(pick, rows, NT)
        one, other = by_parity("swath", both[SUB:], both[0:SUB])
        even_pairs[:, start : start + lines] = one.astype(BF16)
        odd_pairs[:, start : start + lines] = other.astype(BF16)
        start += lines


def plan_kernel(z, owner_l, slot_l, owner_s, slot_s, base_l, base_s, marks):
    total = jnp.zeros((z.devices, LANES), F32)
    shift = 0
    for band, (owner, slot, base) in enumerate(((owner_l, slot_l, base_l), (owner_s, slot_s, base_s))):
        tiles = z.lines[band]
        hit = iota((z.devices, tiles), 0) == owner[...]
        earlier = ones_where(iota((tiles, tiles), 0) < iota((tiles, tiles), 1))
        before = dot(ones_where(hit), earlier, NN)
        rank = jnp.sum(jnp.where(hit, before, 0.0), axis=0, keepdims=True).astype(jnp.int32)
        base[...] = owner[...] * z.stride + z.starts[band] + rank
        line = jnp.where(hit, slot[...].reshape(1, tiles) + 1, 0).astype(F32).astype(BF16)
        place = ones_where(iota((LANES, tiles), 0) == rank + shift)
        total = total + dot(line, place, NT)
        shift += z.caps[band]
    me, other = iota((z.devices, z.devices), 0), iota((z.devices, z.devices), 1)
    inner = me % z.swath
    own = total.astype(BF16)
    before = dot(ones_where((other == me - 1) & (inner > 0)), own, NN)
    after = dot(ones_where((other == me + 1) & (inner < z.swath - 1)), own, NN)
    marks[...] = total + pltpu.roll(before, shift, 1) + pltpu.roll(after, 2 * shift, 1)


def second_kernel(z, top_l, top_s, bottom_l, bottom_s, swap_a, swap_b, even_pairs, odd_pairs):
    after, before = by_parity("swath", swap_a[...].astype(F32), swap_b[...].astype(F32))
    strips = []
    lines_l, lines_s = z.lines
    ends = (
        (top_l, top_s, 0, 0, lines_l),
        (bottom_l, bottom_s, top_l.shape[1] - 1, lines_l - 1, lines_l + lines_s - 1),
    )
    for rows_l, rows_s, row, at_l, at_s in ends:
        parts = [rows_l[...].astype(F32)[:, row, :], rows_s[...].astype(F32)[:, row, :]]
        for side in (before, after):
            for at in (at_l, at_s):
                column = side[0:COMPS, at : at + 1]
                parts.append(jnp.broadcast_to(column, (COMPS, LANES)))
        parts.append(jnp.zeros((even_pairs.shape[0] - 6 * COMPS, LANES), F32))
        strips.append(jnp.concatenate(parts, axis=0))
    one, other = by_parity("sec", strips[1], strips[0])
    even_pairs[...] = one.astype(BF16)
    odd_pairs[...] = other.astype(BF16)


def with_sides(x, left, right):
    lane = iota(x.shape, 1)
    width = x.shape[1]
    before = jnp.where(lane == 0, left, pltpu.roll(x, 1, 1))
    after = jnp.where(lane == width - 1, right, pltpu.roll(x, width - 1, 1))
    return before, after


def filter_planes(tiles, radar, halo, planes):
    inner = pl.ds(SUB, tiles)
    blank = jnp.zeros((1, LANES), F32)
    for plane in range(3 + COMPS):
        planes[plane, SUB - 1 : SUB, :] = blank
        planes[plane, SUB + tiles : SUB + tiles + 1, :] = blank
    total = jnp.zeros((tiles, LANES), F32)
    beside = jnp.zeros((tiles, LANES), F32)
    for c in range(COMPS):
        x = radar[c].astype(F32)
        side = halo[:, c * LANES : (c + 1) * LANES]
        total = total + x * x
        beside = beside + side * side
        before, after = neighbours(x, side)
        planes[3 + c, inner, :] = x + before + after
    for plane, value in enumerate((total,) + neighbours(total, beside)):
        planes[plane, inner, :] = value


def filter_lines(start, lines, radar, planes, filtered):
    at = lambda plane, shift: planes[plane, pl.ds(SUB + start + shift, lines), :]
    gain = gain_of([at(plane, d) for plane in range(3) for d in (-1, 0, 1)])
    for c in range(COMPS):
        mean = (at(3 + c, -1) + at(3 + c, 0) + at(3 + c, 1)) / 9.0
        x = radar[c, pl.ds(start, lines), :].astype(F32)
        filtered[pl.ds(start * SUB + c, lines, stride=SUB), :] = mean + gain * (x - mean)


def gain_of(near):
    mean_power = sum(near[1:], near[0]) / 9.0
    spread = jnp.zeros_like(mean_power)
    for q in near:
        spread = spread + (q - mean_power) ** 2
    spread = spread / 9.0
    return spread / (spread + cu_square * mean_power * mean_power + 1.0)


def send_kernel(
    z, base_l, base_s, radar_l, radar_s, swap_a, swap_b, weights_l, weights_s,
    packed, edge_lines, edge_tiles, planes_l, planes_s, filtered_l, filtered_s, held_l, arrived,
):
    copies = []
    for at in range(0, z.lines[0], z.part):
        part = pl.ds(at, z.part)
        copies.append(pltpu.make_async_copy(weights_l.at[part], held_l.at[part], arrived.at[len(copies)]))
        copies[-1].start()
    packed[...] = jnp.zeros_like(packed)
    tall = edge_lines.shape[3]
    for band, radar in enumerate((radar_l, radar_s)):
        edge_lines[band, 0] = radar[:, 0:tall, :]
        edge_lines[band, 1] = radar[:, z.lines[band] - tall :, :]
    after, before = by_parity("swath", swap_a[...].astype(F32), swap_b[...].astype(F32))
    sides = jnp.concatenate([before, after], axis=0).astype(BF16)
    column, to = iota((2 * SUB, COMPS * LANES), 0), iota((2 * SUB, COMPS * LANES), 1)
    target = jnp.where(column < SUB, column * LANES + LANES - 1, (column - SUB) * LANES)
    target = ones_where((to == target) & (column % SUB < COMPS))
    bands = (
        (radar_l, base_l, held_l, planes_l, filtered_l),
        (radar_s, base_s, weights_s, planes_s, filtered_s),
    )
    at = (0, z.lines[0])
    for band in (1, 0):
        radar, _, _, planes, _ = bands[band]
        part = slice(at[band], at[band] + z.lines[band])
        filter_planes(z.lines[band], radar, dot(sides[:, part], target, TN), planes)
    todo = [(band, start) for band in (1, 0) for start in range(0, z.lines[band], z.part)]

    def lines_of(band, start):
        radar, _, _, planes, filtered = bands[band]
        filter_lines(start, z.part, radar, planes, filtered)

    lines_of(*todo[0])
    for i, (band, start) in enumerate(todo):
        _, base, held, _, filtered = bands[band]
        if band == 0:
            copies[start // z.part].wait()
        if i + 1 < len(todo):
            lines_of(*todo[i + 1])
        for tile in range(start, start + z.part, 2):
            lines = filtered[pl.ds(tile * SUB, 2 * SUB), :].astype(BF16)
            matrix = held[pl.ds(tile, 2)].reshape(2 * LANES, LANES)
            result = dot(lines, matrix, NT)
            first, second = base[0, tile], base[0, tile + 1]
            packed[pl.ds(first, COMPS, stride=z.caps[band]), :] = result[0:COMPS, 0:LANES]
            packed[pl.ds(second, COMPS, stride=z.caps[band]), :] = result[SUB : SUB + COMPS, LANES:]
    for band, (_, _, held, _, _) in enumerate(bands):
        edge_tiles[band, 0] = held[0]
        edge_tiles[band, 1] = held[z.lines[band] - 1]


def tail_kernel(
    z, base_l, base_s, given, sec_a, sec_b, swap_a, swap_b, marks,
    lines_held, tiles_held, sent, packed, out, leaving,
):
    del given
    tall = lines_held.shape[3]
    after, before = by_parity("swath", swap_a[...].astype(F32), swap_b[...].astype(F32))
    down, up = by_parity("sec", sec_a[...].astype(F32), sec_b[...].astype(F32))
    shift = 0
    for band, base in enumerate((base_l, base_s)):
        lines = z.lines[band]
        for end in range(2):
            rows = lines_held[band, end].astype(F32)
            strip = (up, down)[end]
            first = 0 if end == 0 else lines - 2
            near_row = 0 if end == 0 else tall - 2
            columns = (before, after)
            values, sides = [], [[], []]
            for c in range(COMPS):
                row = band * COMPS + c
                far = strip[row : row + 1]
                near = rows[c, near_row : near_row + 2]
                values.append(jnp.concatenate([far, near] if end == 0 else [near, far], axis=0))
                for side in range(2):
                    corner = 2 * COMPS * (1 + side) + row
                    far = strip[corner : corner + 1, 0:1]
                    near = [
                        columns[side][c : c + 1, shift + first + k : shift + first + k + 1]
                        for k in range(2)
                    ]
                    sides[side].append(jnp.concatenate([far] + near if end == 0 else near + [far], axis=0))
            squares = lambda parts: sum(v * v for v in parts)
            power = squares(values)
            planes = (power,) + with_sides(power, squares(sides[0]), squares(sides[1]))
            gain = gain_of([plane[k : k + 1] for plane in planes for k in range(3)])
            lines_out = []
            for c in range(COMPS):
                left, right = with_sides(values[c], sides[0][c], sides[1][c])
                total = values[c] + left + right
                mean = (total[0:1] + total[1:2] + total[2:3]) / 9.0
                lines_out.append(mean + gain * (values[c][1:2] - mean))
            lines_out.append(jnp.zeros((SUB - COMPS, LANES), F32))
            result = dot(jnp.concatenate(lines_out, axis=0).astype(BF16), tiles_held[band, end], NT)
            target = base[0, 0 if end == 0 else lines - 1]
            packed[pl.ds(target, COMPS, stride=z.caps[band]), :] = result[0:COMPS]
        shift += lines

    steps = z.lanes // LANES
    row, lane = iota((SUB, LANES), 0), iota((SUB, LANES), 1)
    pick = ones_where(
        ((row >= 1) & (row <= steps) & (lane == LANES - 1)) | ((row > steps) & (row <= 2 * steps) & (lane == 0))
    )
    columns = [
        dot(pick, packed[o * z.stride : o * z.stride + z.lanes, :].astype(BF16), NT) for o in range(z.devices)
    ]
    group, copies = z.devices // 8, []
    for o in range(z.devices):
        extra = jnp.broadcast_to(marks[o : o + 1, :], (SUB, LANES))
        one_less, one_more = max(o - 1, 0), min(o + 1, z.devices - 1)
        for k in range(steps):
            part = slice(k * LANES, (k + 1) * LANES)
            extra = jnp.where(row == 1 + k, columns[one_less][:, part], extra)
            extra = jnp.where(row == 1 + steps + k, columns[one_more][:, part], extra)
        out[o, 0 : z.rows, :] = packed[o * z.stride : o * z.stride + z.rows, :].astype(BF16)
        out[o, z.rows :, :] = extra.astype(BF16)
        if (o + 1) % group == 0:
            part = pl.ds(o + 1 - group, group)
            copies.append(pltpu.make_async_copy(out.at[part], sent.at[part], leaving.at[o // group]))
            copies[-1].start()
    for copy in copies:
        copy.wait()


def matrix_kernel(models, small, wide):
    m = models[...]
    n_model = m.shape[0]
    eye = ones_where(iota((CHANNELS, CHANNELS), 0) == iota((CHANNELS, CHANNELS), 1), F32)
    powers = jnp.zeros(m.shape, F32)
    for _ in range(FIT_ITERS):
        predicted = dot(m, powers, TN, HI)
        powers = powers + fit_rate * dot(m, eye - predicted, NN, HI)
    powers = powers / 9.0
    small[...] = powers
    rows, columns = wide.shape[0] // 2, wide.shape[1]
    left = ones_where(iota((rows, n_model), 0) // SUB == iota((rows, n_model), 1), F32)
    right = ones_where(iota((CHANNELS, columns), 1) // SUB == iota((CHANNELS, columns), 0), F32)
    spread = dot(dot(left, powers, NN, HI), right, NN, HI)
    same = iota((rows, columns), 0) % SUB == iota((rows, columns), 1) % SUB
    spread = jnp.where(same, spread, 0.0)
    high = spread.astype(BF16)
    low = (spread - high.astype(F32)).astype(BF16)
    wide[...] = jnp.concatenate([high, low], axis=0)


def coherency(real, imag):
    joint = [real[f] * real[g] + imag[f] * imag[g] for f, g in upper_pairs]
    return joint + [imag[f] * real[g] - real[f] * imag[g] for f, g in strict_pairs]


def split_parts(maps):
    pick = lambda at: [maps(band * COMPS + at + c) for band in range(2) for c in range(3)]
    return pick(0), pick(3)


def merge_kernel(z, got, small, wide, maps, planes, even_pairs, odd_pairs, stage, extras, two):
    map_lines, n_model, devices = z.map_lines, z.n_model, z.devices
    steps = z.lanes // LANES
    for s in range(devices):
        extras[s * SUB : (s + 1) * SUB, :] = got[s, z.rows : z.rows + SUB, :].astype(F32)
    piece = lambda r: extras[pl.ds(r, devices, stride=SUB), :]
    marks = piece(0)
    sides = [
        jnp.concatenate([piece(1 + side * steps + k) for k in range(steps)], axis=1) for side in range(2)
    ]
    shift = sum(z.caps)
    edges = [[None] * (2 * COMPS) for _ in range(2)]
    at_mark = 0
    for band in range(2):
        capacity = z.caps[band]
        places = devices * capacity
        for s in range(devices):
            block = got[s, 0 : z.rows, :].astype(F32)
            for c in range(COMPS):
                low = z.starts[band] + c * capacity
                stage[s * capacity : (s + 1) * capacity, c * LANES : (c + 1) * LANES] = block[
                    low : low + capacity, :
                ]
        turned = lambda x, by: pltpu.roll(x, (x.shape[1] - by) % x.shape[1], 1)[:, 0:LANES]
        rows = [turned(marks, at_mark + k * shift) for k in range(3)]
        for side in range(2):
            rows += [turned(sides[side], z.starts[band] + c * capacity) for c in range(COMPS)]
        at_mark += capacity
        place = iota((devices, places), 1)
        low = iota((devices, places), 0) * capacity
        mine = (place >= low) & (place < low + capacity)
        offset = jnp.sum(jnp.where(mine, place - low, 0), axis=0, keepdims=True)
        pick = ones_where(iota((LANES, places), 0) == offset)
        spread = dot(jnp.concatenate(rows, axis=0).astype(BF16), pick, NN)
        flat = [
            jnp.sum(jnp.where(mine, spread[k * devices : (k + 1) * devices], 0.0), axis=0, keepdims=True)
            for k in range(len(rows))
        ]
        lines = iota((map_lines, places), 0) + 1
        tables = [ones_where(lines == flat[k].astype(jnp.int32)) for k in range(3)]
        summed = dot(tables[0], stage[0:places, :].astype(BF16), NN)
        for c in range(COMPS):
            maps[band * COMPS + c] = summed[:, c * LANES : (c + 1) * LANES]
        for side in range(2):
            values = flat[3 + side * COMPS : 3 + (side + 1) * COMPS]
            values = jnp.concatenate(values + [jnp.zeros((SUB - COMPS, places), F32)], axis=0).astype(BF16)
            column = dot(values, tables[1 + side], NT)
            for c in range(COMPS):
                edges[side][band * COMPS + c] = column[c : c + 1, :]
    turned = []
    for side in range(2):
        joint = jnp.concatenate(coherency(*split_parts(lambda i: edges[side][i])), axis=0)
        turned.append(dot(small[...], joint, NN, HI))
    x = jnp.concatenate(turned, axis=0)
    high = x.astype(BF16)
    x = jnp.concatenate([high, (x - high.astype(F32)).astype(BF16)], axis=0)
    at = iota((4 * n_model, n_model * LANES), 0) % (2 * n_model)
    to = iota((4 * n_model, n_model * LANES), 1)
    target = jnp.where(at < n_model, at * LANES + LANES - 1, (at - n_model) * LANES)
    planes[...] = dot(x, ones_where(to == target), TN)

    ends = (0, map_lines - SUB)
    two[...] = fit_block(wide, maps, ends, n_model)
    for k in range(n_model):
        part = slice(k * LANES, (k + 1) * LANES)
        top = two[k * SUB : k * SUB + 1, 0:LANES]
        bottom = two[k * SUB + SUB - 1 : (k + 1) * SUB, LANES:]
        top = three_lanes(top, planes[0:1, part])
        bottom = three_lanes(bottom, planes[map_lines - 1 : map_lines, part])
        one, other = by_parity("sec", bottom, top)
        even_pairs[k : k + 1, :] = one
        odd_pairs[k : k + 1, :] = other


def fit_block(wide, maps, starts, n_model):
    halves = []
    for r in starts:
        x = jnp.concatenate(coherency(*split_parts(lambda n: maps[n, pl.ds(r, SUB), :])), axis=0)
        halves.append(x.astype(BF16))
    result = dot(wide[...], jnp.concatenate(halves, axis=1), NN)
    return result[0 : n_model * SUB] + result[n_model * SUB :]


def neighbours(x, side):
    lane = iota(x.shape, 1)
    before = pltpu.roll(jnp.where(lane == LANES - 1, side, x), 1, 1)
    return before, pltpu.roll(jnp.where(lane == 0, side, x), LANES - 1, 1)


def three_lanes(x, side):
    before, after = neighbours(x, side)
    return x + before + after


def spread_kernel(z, maps, planes, wide, out, ends, fits, done, leaving):
    map_lines, n_model = z.map_lines, z.n_model
    for i in range(map_lines // (2 * SUB)):
        starts = (2 * i * SUB, (2 * i + 1) * SUB)
        result = fit_block(wide, maps, starts, n_model)
        for h, r in enumerate(starts):
            for k in range(n_model):
                fits[k, pl.ds(SUB + r, SUB), :] = result[
                    k * SUB : (k + 1) * SUB, h * LANES : (h + 1) * LANES
                ]
    blank = jnp.zeros((1, LANES), F32)
    inner = pl.ds(SUB, map_lines)
    copies = []
    for k in range(n_model):
        x = three_lanes(fits[k, inner, :], planes[:, k * LANES : (k + 1) * LANES])
        fits[k, inner, :] = x
        fits[k, SUB - 1 : SUB, :] = blank
        fits[k, SUB + map_lines : SUB + map_lines + 1, :] = blank
        x = fits[k, pl.ds(SUB - 1, map_lines), :] + x + fits[k, pl.ds(SUB + 1, map_lines), :]
        done[k] = x
        copies.append(pltpu.make_async_copy(done.at[k], out.at[k], leaving.at[k]))
        copies[-1].start()
        ends[0, k] = x[0:SUB]
        ends[1, k] = x[map_lines - SUB :]
    for copy in copies:
        copy.wait()


def finish_kernel(z, given, ends, sec_a, sec_b, out, held, moving):
    del given
    below, above = by_parity("sec", sec_a[...], sec_b[...])
    line = iota((SUB, LANES), 0)
    copies = []
    for end, (at, row, start) in enumerate(((0, above, 0), (SUB - 1, below, z.map_lines - SUB))):
        for k in range(z.n_model):
            held[end, k] = ends[end, k] + jnp.where(line == at, row[k : k + 1, :], 0.0)
        copies.append(pltpu.make_async_copy(held.at[end], out.at[:, pl.ds(start, SUB), :], moving.at[end]))
        copies[-1].start()
    for copy in copies:
        copy.wait()


def body(radar_l, radar_s, weights_l, weights_s, owner_l, owner_s, slot_l, slot_s, models):
    z = Sizes(radar_l.shape[1], radar_s.shape[1], models.shape[0])
    lines_l, lines_s = z.lines
    shape = jax.ShapeDtypeStruct

    def call(kernel, args, shapes, mib, scratch=(), specs=None, outs=None, flops=0, size=0):
        return pl.pallas_call(
            lambda *refs: kernel(z, *refs) if kernel is not matrix_kernel else kernel(*refs),
            in_specs=specs or [VMEM] * len(args),
            out_specs=outs or [VMEM] * len(shapes),
            out_shape=shapes,
            scratch_shapes=scratch,
            compiler_params=params(mib),
            cost_estimate=pl.CostEstimate(flops=flops, bytes_accessed=size, transcendentals=0),
        )(*args)

    def call_one(kernel, args, specs, shapes, mib, scratch=(), aliases={}, flops=0, size=0):
        return pl.pallas_call(
            lambda *refs: kernel(z, *refs),
            grid=(1,),
            in_specs=specs,
            out_specs=[whole(x.shape) for x in shapes],
            out_shape=shapes,
            scratch_shapes=scratch,
            input_output_aliases=aliases,
            compiler_params=params(mib),
            cost_estimate=pl.CostEstimate(flops=flops, bytes_accessed=size, transcendentals=0),
        )(*args)

    row = lambda x: x.reshape(1, -1)
    radar = (radar_l, radar_s)
    column = shape((SUB, lines_l + lines_s), BF16)
    even, odd = call_one(
        first_kernel, radar, [whole(x.shape) for x in radar], [column, column], 58,
        flops=10_000_000_000, size=1_000_000,
    )
    swap_a, swap_b = swap(even, odd, "swath")
    args = (row(owner_l), slot_l, row(owner_s), slot_s)
    base_l, base_s, marks = call_one(
        plan_kernel,
        args,
        [whole(x.shape) for x in args],
        [shape((1, lines_l), jnp.int32), shape((1, lines_s), jnp.int32), shape((z.devices, LANES), F32)],
        58,
        flops=1_000_000_000,
        size=1_000_000,
    )
    strip = shape((5 * SUB, LANES), BF16)
    tall = 2 * SUB
    edge = lambda lines, end: pl.BlockSpec(
        (COMPS, tall, LANES), lambda i: (0, end * (lines // tall - 1), 0)
    )
    edges = [edge(lines, end) for end in range(2) for lines in z.lines]
    side = whole(column.shape)
    even, odd = call_one(
        second_kernel, radar * 2 + (swap_a, swap_b), edges + [side, side], [strip, strip], 16, flops=1_000_000_000_000, size=1_000_000,
    )
    sec_a, sec_b = swap(even, odd, "sec")
    buffer = shape((z.devices * z.stride + up_to(COMPS * max(z.caps), SUB), LANES), F32)
    packed, edge_lines, edge_tiles = call(
        send_kernel,
        (base_l, base_s, radar_l, radar_s, swap_a, swap_b, weights_l, weights_s),
        [
            buffer,
            shape((2, 2, COMPS, tall, LANES), BF16),
            shape((2, 2, LANES, LANES), BF16),
        ],
        34,
        specs=[SMEM, SMEM] + [VMEM] * 4 + [ANY, VMEM],
        scratch=[
            *[pltpu.VMEM((3 + COMPS, n + 2 * SUB, LANES), F32) for n in z.lines],
            *[pltpu.VMEM((n * SUB, LANES), F32) for n in z.lines],
            pltpu.VMEM(weights_l.shape, BF16),
            pltpu.SemaphoreType.DMA((lines_l // z.part,)),
        ],
        flops=10_000_000_000,
        size=2 * (weights_l.size + weights_s.size),
    )
    args = (base_l, base_s, packed, sec_a, sec_b, swap_a, swap_b, marks, edge_lines, edge_tiles)
    sent, _ = pl.pallas_call(
        lambda *refs: tail_kernel(z, *refs),
        in_specs=[SMEM, SMEM] + [VMEM] * 8,
        out_specs=[ANY, VMEM],
        out_shape=[shape((z.devices, z.rows + SUB, LANES), BF16), buffer],
        scratch_shapes=[pltpu.VMEM((z.devices, z.rows + SUB, LANES), BF16), pltpu.SemaphoreType.DMA((8,))],
        input_output_aliases={2: 1},
        compiler_params=params(24),
    )(*args)
    got = lax.all_to_all(sent, AXES, split_axis=0, concat_axis=0, tiled=True)

    small, wide = call(
        matrix_kernel,
        (models,),
        [shape((z.n_model, CHANNELS), F32), shape((2 * z.n_model * SUB, CHANNELS * SUB), BF16)],
        16, flops=50_000_000, size=1_000_000,
    )
    rim = shape((z.n_model, LANES), F32)
    maps, planes, even, odd = call(
        merge_kernel,
        (got, small, wide),
        [
            shape((2 * COMPS, z.map_lines, LANES), F32),
            shape((z.map_lines, z.n_model * LANES), F32),
            rim,
            rim,
        ],
        24,
        scratch=[
            pltpu.VMEM((z.devices * max(z.caps), COMPS * LANES), F32),
            pltpu.VMEM((z.devices * SUB, LANES), F32),
            pltpu.VMEM((z.n_model * SUB, 2 * LANES), F32),
        ],
        flops=1_000_000_000,
        size=4_000_000,
    )
    sec_a, sec_b = swap(even, odd, "sec")
    edge = shape((2, z.n_model, SUB, LANES), F32)
    fit, ends = call(
        spread_kernel,
        (maps, planes, wide),
        [shape((z.n_model, z.map_lines, LANES), F32), edge],
        24,
        scratch=[
            pltpu.VMEM((z.n_model, z.map_lines + 2 * SUB, LANES), F32),
            pltpu.VMEM((z.n_model, z.map_lines, LANES), F32),
            pltpu.SemaphoreType.DMA((z.n_model,)),
        ],
        outs=[ANY, VMEM],
        flops=10_000_000_000,
        size=4_000_000,
    )
    return pl.pallas_call(
        lambda *refs: finish_kernel(z, *refs),
        in_specs=[ANY, VMEM, VMEM, VMEM],
        out_specs=ANY,
        out_shape=shape(fit.shape, F32),
        scratch_shapes=[pltpu.VMEM(edge.shape, F32), pltpu.SemaphoreType.DMA((2,))],
        input_output_aliases={0: 0},
        compiler_params=params(16),
    )(fit, ends, sec_a, sec_b)


def solution(mesh):
    in_specs = (
        P(None, "sec", "swath"),
        P(None, "sec", "swath"),
        P(("sec", "swath"), None, None),
        P(("sec", "swath"), None, None),
        P(("sec", "swath"), None),
        P(("sec", "swath"), None),
        P(("sec", "swath")),
        P(("sec", "swath")),
        P(),
    )
    out_specs = P(None, "sec", "swath")
    return jax.shard_map(body, mesh=mesh, in_specs=in_specs, out_specs=out_specs, check_vma=False)
```
